32 devices in a mesh: shard: 4 (over z), ctx: 4 (over x, core), tp: 2 (over y).
Axes of the slice: x: 2, y: 2, z: 4, core: 2. Of those that a mesh axis runs over, the one named last changes fastest.
Arguments:
- tokens: bfloat16 [16, 1024, 768], P('shard', 'ctx'), may hold values from -6 to 6
- starts: int32 [16, 2], P('shard'), may hold values from 0 to 768, as said below
- w_query: float32 [768, 768], P('shard', 'tp'), may hold values from -0.3125 to 0.3125
- w_key: float32 [768, 768], P('shard', 'tp'), may hold values from -0.3125 to 0.3125
- w_value: float32 [768, 768], P('shard', 'tp'), may hold values from -0.21875 to 0.21875
- w_out: float32 [768, 768], P('shard', 'tp'), may hold values from -1.25 to 1.25
- w_up: float32 [768, 3072], P('shard', 'tp'), may hold values from -0.21875 to 0.21875
- w_down: float32 [768, 3072], P('shard', 'tp'), may hold values from -0.109375 to 0.109375
- head_bias: float32 [2, 768], P(None, 'tp'), may hold values from -4 to 4
- up_bias: float32 [3072], P('tp'), may hold values from -4 to 4
- out_biases: float32 [2, 768], replicated, may hold values from -4 to 4
- norm_gains: float32 [2, 768], replicated, may hold values from 0.25 to 1.75
- norm_shifts: float32 [2, 768], replicated, may hold values from -4 to 4
- cotangent: bfloat16 [16, 1024, 768], P('shard', 'ctx'), may hold values from -6 to 6
Outputs:
- activations: bfloat16 [16, 1024, 768], P('shard', 'ctx')
- input_grad: float32 [16, 1024, 768], P('shard', 'ctx')
- grad_query: float32 [768, 768], P('shard', 'tp')
- grad_key: float32 [768, 768], P('shard', 'tp')
- grad_value: float32 [768, 768], P('shard', 'tp')
- grad_out: float32 [768, 768], P('shard', 'tp')
- grad_up: float32 [768, 3072], P('shard', 'tp')
- grad_down: float32 [768, 3072], P('shard', 'tp')
- grad_head_bias: float32 [2, 768], P(None, 'tp')
- grad_up_bias: float32 [3072], P('tp')
- grad_out_biases: float32 [2, 768], replicated
- grad_norm_gains: float32 [2, 768], replicated
- grad_norm_shifts: float32 [2, 768], replicated
The draws below stay inside these ranges and needn't reach their ends.
Inputs may be any that keep to these rules, and one draw needn't show every extreme that they name: `starts`: each row holds the first positions of the 2 picture pieces of one sequence in increasing order; the pieces of 256 tokens are disjoint and lie inside the sequence of 1024 tokens.
All inputs are finite; a program needn't handle non-finite values.
Results may differ from the reference program's by a relative error of at most 0.019.
Values may be sent and summed in bfloat16 or wider, within the bound.
A program may use at most 128 MiB of HBM per device.

```python
import math
import jax
import jax.numpy as jnp
from jax import lax

D = 768
HEADS = 12
HEAD = 64
FF = 3072
SEQ_DEV = 4
PIECE = 256
PIECES = 2
LEN = 1024
SEQS = 16


def draw_starts(key, part):
    spare_room = LEN - PIECES * PIECE
    offsets = jax.random.randint(key, (SEQS, PIECES), 0, spare_room + 1).astype(jnp.int32)
    offsets = offsets.at[0, 0].set(0).at[SEQS - 1, PIECES - 1].set(spare_room)
    offsets = jnp.sort(offsets, axis=1)
    return (offsets + jnp.arange(PIECES, dtype=jnp.int32)[None, :] * PIECE).astype(jnp.int32)


def strengthened(result, stream_key, source, target, shards_of, factor):
    owner, partner = [(jnp.arange(result.shape[position]) // (result.shape[position] // shards_of)).reshape([-1 if axis == position else 1 for axis in range(result.ndim)]) for position in (source, target)]
    chosen = jax.random.permutation(stream_key, shards_of)[partner]
    strong = (owner == chosen) | (owner == (partner + shards_of // 2) % shards_of)
    return jnp.where(strong, factor * result, result)


def block_scale(own_key, extent, split, smallest, high):
    level, own = 1.0, jax.random.fold_in(own_key, 6)
    for dim, shards_of in split:
        draws = jnp.exp(jax.random.uniform(jax.random.fold_in(own, dim), (shards_of,), jnp.float32, smallest / len(split), high / len(split)))
        level = level * jnp.repeat(draws, extent[dim] // shards_of).reshape([-1 if axis == dim else 1 for axis in range(len(extent))])
    return level


def gaussian(own_key, dims, deviation, most, split=(), kind=jnp.bfloat16):
    gain = block_scale(own_key, dims, split, -0.22, 0.18) if split else 1.0
    drawn = jax.random.normal(own_key, dims, jnp.float32) * deviation * gain
    return jnp.minimum(jnp.maximum(drawn, -most), most).astype(kind)


def bell_draw_with(own_key, dims, scale, limit, split, heavy, kind=jnp.bfloat16):
    entries = scale * jax.random.normal(own_key, dims, jnp.float32)
    if split:
        entries = entries * block_scale(own_key, dims, split, -0.22, 0.18)
    return jnp.clip(strengthened(entries, jax.random.fold_in(own_key, 3), *heavy), -limit, limit).astype(kind)


def setup_inputs(seed: int = 0) -> dict:
    key_of = jax.random.split(jax.random.key(seed), 15)
    return {
        "tokens": gaussian(key_of[0], (SEQS, LEN, D), 1.0, 6.0, ((0, 4), (1, 4))),
        "starts": draw_starts(jax.random.fold_in(key_of[14], 71), 0),
        "w_query": gaussian(key_of[2], (D, D), (D // 2) ** -0.5, 0.3125, ((0, 4), (1, 2)), jnp.float32),
        "w_key": gaussian(key_of[3], (D, D), (D // 2) ** -0.5, 0.3125, ((0, 4), (1, 2)), jnp.float32),
        "w_value": gaussian(key_of[4], (D, D), D ** -0.5, 0.21875, ((0, 4), (1, 2)), jnp.float32),
        "w_out": gaussian(key_of[5], (D, D), (D // 32) ** -0.5, 1.25, ((0, 4), (1, 2)), jnp.float32),
        "w_up": gaussian(key_of[6], (D, FF), D ** -0.5, 0.21875, ((0, 4), (1, 2)), jnp.float32),
        "w_down": gaussian(key_of[7], (D, FF), FF ** -0.5, 0.109375, ((0, 4), (1, 2)), jnp.float32),
        "head_bias": gaussian(key_of[8], (2, D), 0.3, 4.0, ((1, 2),), jnp.float32),
        "up_bias": gaussian(key_of[9], (FF,), 0.3, 4.0, ((0, 2),), jnp.float32),
        "out_biases": gaussian(key_of[10], (2, D), 0.3, 4.0, (), jnp.float32),
        "norm_gains": jnp.clip(1.0 + 0.15 * jax.random.normal(key_of[11], (2, D), jnp.float32), 0.25, 1.75),
        "norm_shifts": gaussian(key_of[12], (2, D), 0.3, 4.0, (), jnp.float32),
        "cotangent": bell_draw_with(key_of[13], (SEQS, LEN, D), 1.0, 6.0, ((0, 4), (1, 4)), (0, 2, 4, 2.0)),
    }


@jax.custom_vjp
def low(v):
    return lax.optimization_barrier(v.astype(jnp.bfloat16)).astype(jnp.float32)

@jax.custom_vjp
def low_back(v):
    return v

def low_keep(v):
    return (low(v), None)

def low_pass(kept, grad):
    return (grad,)

def back_keep(v):
    return (v, None)

def back_low(kept, grad):
    return (low(grad),)
low.defvjp(low_keep, low_pass)
low_back.defvjp(back_keep, back_low)
norm_eps = 1e-05
masked_score = -1e+30
highest = lax.Precision.HIGHEST

def product(former, latter):
    return jnp.dot(former, latter, precision=highest)

def layer_norm(values, gain_row, shift_row):
    centre = lax.optimization_barrier(jnp.mean(values, axis=-1, keepdims=True))
    centred = values - centre
    spread = lax.optimization_barrier(jnp.mean(centred * centred, axis=-1, keepdims=True))
    return centred * lax.rsqrt(spread + norm_eps) * gain_row + shift_row

def piece_labels(seq_starts):
    places = jnp.arange(LEN, dtype=jnp.int32)
    inside = (places[None, :] >= seq_starts[:, None]) & (places[None, :] < seq_starts[:, None] + PIECE)
    numbers = jnp.arange(1, PIECES + 1, dtype=jnp.int32)
    return lax.optimization_barrier(jnp.sum(jnp.where(inside, numbers[:, None], 0), axis=0)).astype(jnp.int32)

def attend(blocks):
    query_rows, key_rows, value_rows, seq_starts = blocks
    labels = piece_labels(seq_starts)
    places = jnp.arange(LEN, dtype=jnp.int32)
    allowed = (places[None, :] <= places[:, None]) | (labels[None, :] == labels[:, None]) & (labels[:, None] > 0)
    query_heads = query_rows.reshape(LEN, HEADS, HEAD)
    key_heads = key_rows.reshape(LEN, HEADS, HEAD)
    value_heads = value_rows.reshape(LEN, HEADS, HEAD)
    scores = low_back(jnp.einsum('qhd,khd->hqk', query_heads, key_heads, precision=highest) * (1.0 / math.sqrt(HEAD)))
    scores = jnp.where(allowed[None], scores, masked_score)
    row_top = lax.optimization_barrier(jnp.max(scores, axis=-1, keepdims=True))
    raised = jnp.exp(scores - row_top)
    attn_probs = raised / lax.optimization_barrier(jnp.sum(raised, axis=-1, keepdims=True))
    mixed_heads = jnp.einsum('hqk,khd->qhd', low(attn_probs), value_heads, precision=highest)
    return mixed_heads.reshape(LEN, D)

def layer(inputs, group_starts, params):
    w_query, w_key, w_value, w_out, w_up, w_down, head_bias, up_bias, out_biases, norm_gains, norm_shifts = params
    flat_rows = inputs.reshape(-1, D)
    queries = low(low_back(product(flat_rows, low(w_query))) + head_bias[0])
    key_rows = low(low_back(product(flat_rows, low(w_key))))
    value_rows = low(low_back(product(flat_rows, low(w_value))) + head_bias[1])
    per_seq = (-1, LEN, D)
    mixed = lax.map(jax.checkpoint(attend), (queries.reshape(per_seq), key_rows.reshape(per_seq), value_rows.reshape(per_seq), group_starts))
    mixed = low(low_back(mixed.reshape(-1, D)))
    attn_out = low_back(product(mixed, low(w_out).T)) + out_biases[0]
    first_norm = layer_norm(flat_rows + attn_out, norm_gains[0], norm_shifts[0])
    hidden = low_back(product(low(first_norm), low(w_up))) + up_bias
    active = low(jax.nn.gelu(hidden, approximate=False))
    ffn_out = low_back(product(active, low(w_down).T)) + out_biases[1]
    final_norm = layer_norm(first_norm + ffn_out, norm_gains[1], norm_shifts[1])
    return final_norm.reshape(inputs.shape)

def reference(tokens, starts, w_query, w_key, w_value, w_out, w_up, w_down, head_bias, up_bias, out_biases, norm_gains, norm_shifts, cotangent):
    params = (w_query, w_key, w_value, w_out, w_up, w_down, head_bias, up_bias, out_biases, norm_gains, norm_shifts)
    group_tokens = tokens.astype(jnp.float32).reshape(-1, SEQ_DEV, LEN, D)
    group_cots = cotangent.astype(jnp.float32).reshape(-1, SEQ_DEV, LEN, D)
    group_starts = starts.reshape(-1, SEQ_DEV, PIECES)

    def one_group(totals, blocks):
        inputs, seq_starts, cot_rows = blocks

        def run_layer(inputs_here, params_here):
            return layer(inputs_here, seq_starts, params_here)
        outputs, pullback = jax.vjp(run_layer, inputs, params)
        grad_inputs, grad_params = pullback(cot_rows)
        totals = jax.tree.map(jnp.add, totals, grad_params)
        return (totals, (outputs.astype(jnp.bfloat16), grad_inputs))
    totals, (outputs, grad_inputs) = lax.scan(one_group, jax.tree.map(jnp.zeros_like, params), (group_tokens, group_starts, group_cots))
    return (outputs.reshape(SEQS, LEN, D), grad_inputs.reshape(SEQS, LEN, D), totals[0], totals[1], totals[2], totals[3], totals[4], totals[5], totals[6], totals[7], totals[8], totals[9], totals[10])
```

```python
import math

import jax
import jax.numpy as jnp
from jax import lax
from jax.experimental import pallas as pl
from jax.experimental.pallas import tpu as pltpu
from jax.sharding import PartitionSpec as P

HEAD = 64
PIECE = 256
BLOCK = 256
PAIR = 128

norm_eps = 1e-05
masked_score = -1e30
AXES = ("shard", "ctx", "tp")


def matmul(former, latter):
    return jnp.dot(former, latter, preferred_element_type=jnp.float32)


def over_rows(former, latter):
    return lax.dot_general(
        former, latter, (((0,), (0,)), ((), ())), preferred_element_type=jnp.float32
    )


def over_cols(former, latter):
    return lax.dot_general(
        former, latter, (((1,), (1,)), ((), ())), preferred_element_type=jnp.float32
    )


def low(values):
    return values.astype(jnp.bfloat16)


def normalize(values):
    centre = jnp.mean(values, axis=-1, keepdims=True)
    centred = values - centre
    spread = jnp.mean(centred * centred, axis=-1, keepdims=True)
    scaling = lax.rsqrt(spread + norm_eps)
    return (centred * scaling, scaling)


def norm_back(grad_out, scaled, scaling, gain_row):
    grad_scaled = grad_out * gain_row
    mean_grad = jnp.mean(grad_scaled, axis=-1, keepdims=True)
    mean_along = jnp.mean(grad_scaled * scaled, axis=-1, keepdims=True)
    return scaling * (grad_scaled - mean_grad - scaled * mean_along)


def edge_mask(starts_ref, key_first, query_first, keys_first):
    key_shape = (BLOCK, 1) if keys_first else (1, BLOCK)
    query_shape = (1, BLOCK) if keys_first else (BLOCK, 1)
    key_at = key_first + lax.broadcasted_iota(jnp.int32, key_shape, 0 if keys_first else 1)
    query_at = query_first + lax.broadcasted_iota(jnp.int32, query_shape, 1 if keys_first else 0)
    seen = key_at <= query_at
    for piece in range(2):
        start = starts_ref[piece]
        key_in = (key_at >= start) & (key_at < start + PIECE)
        query_in = (query_at >= start) & (query_at < start + PIECE)
        seen = seen | (key_in & query_in)
    return seen


def two_heads(rows):
    lane = lax.broadcasted_iota(jnp.int32, rows.shape, 1)
    zero = jnp.zeros_like(rows)
    return jnp.concatenate(
        [jnp.where(lane < HEAD, rows, zero), jnp.where(lane >= HEAD, rows, zero)], axis=0
    )


def join_heads(rows):
    half = rows.shape[0] // 2
    lane = lax.broadcasted_iota(jnp.int32, (half, rows.shape[1]), 1)
    return jnp.where(lane < HEAD, rows[:half], rows[half:])


def attend_kernel(starts_ref, q_ref, k_ref, v_ref, mixed_ref, total_ref):
    length = q_ref.shape[0]
    blocks = length // BLOCK
    for at in range(blocks):
        rows = slice(at * BLOCK, (at + 1) * BLOCK)
        reach = min(blocks, at + 2)
        queries = two_heads(q_ref[rows, :])
        scores = []
        for key_at in range(reach):
            part = over_cols(queries, k_ref[key_at * BLOCK : (key_at + 1) * BLOCK, :])
            if key_at >= at:
                seen = edge_mask(starts_ref, key_at * BLOCK, at * BLOCK, False)
                seen = jnp.concatenate([seen, seen], axis=0)
                part = jnp.where(seen, part, masked_score)
            scores.append(part)
        scores = jnp.concatenate(scores, axis=1)
        top = jnp.max(scores, axis=1, keepdims=True)
        raised = jnp.exp(scores - top)
        total = jnp.sum(raised, axis=1, keepdims=True)
        mixed = matmul(low(raised), v_ref[: reach * BLOCK, :]) / total
        mixed_ref[rows, :] = low(join_heads(mixed))
        wide = jnp.broadcast_to(top + jnp.log(total), (2 * BLOCK, PAIR))
        row = jnp.transpose(wide)[0:1, :]
        total_ref[0, 0:1, rows] = row[:, :BLOCK]
        total_ref[0, 1:2, rows] = row[:, BLOCK:]


def attend_forward(starts, qkv, heads_width):
    length = qkv.shape[0]
    pairs = heads_width // PAIR
    return pl.pallas_call(
        attend_kernel,
        grid_spec=pltpu.PrefetchScalarGridSpec(
            num_scalar_prefetch=1,
            grid=(pairs,),
            in_specs=[
                pl.BlockSpec((length, PAIR), lambda p, s: (0, p)),
                pl.BlockSpec((length, PAIR), lambda p, s: (0, p + pairs)),
                pl.BlockSpec((length, PAIR), lambda p, s: (0, p + 2 * pairs)),
            ],
            out_specs=[
                pl.BlockSpec((length, PAIR), lambda p, s: (0, p)),
                pl.BlockSpec((1, 2, length), lambda p, s: (p, 0, 0)),
            ],
        ),
        out_shape=[
            jax.ShapeDtypeStruct((length, heads_width), jnp.bfloat16),
            jax.ShapeDtypeStruct((pairs, 2, length), jnp.float32),
        ],
        cost_estimate=pl.CostEstimate(
            flops=8 * length * length * heads_width,
            bytes_accessed=8 * length * heads_width,
            transcendentals=length * length * heads_width // HEAD,
        ),
    )(starts, qkv, qkv, qkv)


def attend_back_kernel(
    starts_ref,
    q_ref,
    k_ref,
    v_ref,
    mixed_ref,
    grad_ref,
    total_ref,
    dq_ref,
    dk_ref,
    dv_ref,
    sums_ref,
    dk_acc,
    dv_acc,
):
    length = q_ref.shape[0]
    blocks = length // BLOCK
    query_sum = jnp.zeros((1, PAIR), jnp.float32)
    for at in range(blocks):
        rows = slice(at * BLOCK, (at + 1) * BLOCK)
        reach = min(blocks, at + 2)
        span = slice(0, reach * BLOCK)
        queries = two_heads(q_ref[rows, :])
        grads = two_heads(grad_ref[rows, :])
        along = grad_ref[rows, :].astype(jnp.float32) * mixed_ref[rows, :].astype(jnp.float32)
        along = jnp.transpose(along)
        inner = jnp.concatenate(
            [
                jnp.sum(along[:HEAD], axis=0, keepdims=True),
                jnp.sum(along[HEAD:], axis=0, keepdims=True),
            ],
            axis=1,
        )
        total = jnp.concatenate([total_ref[0, 0:1, rows], total_ref[0, 1:2, rows]], axis=1)
        scores = []
        for key_at in range(reach):
            part = over_cols(k_ref[key_at * BLOCK : (key_at + 1) * BLOCK, :], queries)
            if key_at >= at:
                seen = edge_mask(starts_ref, key_at * BLOCK, at * BLOCK, True)
                seen = jnp.concatenate([seen, seen], axis=1)
                part = jnp.where(seen, part, masked_score)
            scores.append(part)
        probs = jnp.exp(jnp.concatenate(scores, axis=0) - total)
        grad_probs = over_cols(v_ref[span, :], grads)
        grad_scores = low(probs * (grad_probs - inner))
        dv = matmul(low(probs), grads)
        dk = matmul(grad_scores, queries)
        fresh = slice(max(0, (reach - 1)) * BLOCK, reach * BLOCK) if at + 1 < blocks else None
        if at == 0:
            dv_acc[span, :] = dv
            dk_acc[span, :] = dk
        elif fresh is None:
            dv_acc[span, :] += dv
            dk_acc[span, :] += dk
        else:
            old = slice(0, (reach - 1) * BLOCK)
            dv_acc[old, :] += dv[old, :]
            dk_acc[old, :] += dk[old, :]
            dv_acc[fresh, :] = dv[fresh, :]
            dk_acc[fresh, :] = dk[fresh, :]
        dq = join_heads(over_rows(grad_scores, k_ref[span, :])) * (1.0 / math.sqrt(HEAD))
        query_sum += jnp.sum(dq, axis=0, keepdims=True)
        dq_ref[rows, :] = low(dq)
    dk_ref[...] = low(dk_acc[...])
    dv_ref[...] = low(dv_acc[...])
    sums_ref[0, 0:1, :] = query_sum
    sums_ref[0, 1:2, :] = jnp.sum(dv_acc[...], axis=0, keepdims=True)


def attend_backward(starts, qkv, mixed, grad_mixed, totals):
    length, heads_width = mixed.shape
    pairs = heads_width // PAIR
    column = pl.BlockSpec((length, PAIR), lambda p, s: (0, p))
    out = jax.ShapeDtypeStruct((length, heads_width), jnp.bfloat16)
    return pl.pallas_call(
        attend_back_kernel,
        grid_spec=pltpu.PrefetchScalarGridSpec(
            num_scalar_prefetch=1,
            grid=(pairs,),
            in_specs=[
                column,
                pl.BlockSpec((length, PAIR), lambda p, s: (0, p + pairs)),
                pl.BlockSpec((length, PAIR), lambda p, s: (0, p + 2 * pairs)),
                column,
                column,
                pl.BlockSpec((1, 2, length), lambda p, s: (p, 0, 0)),
            ],
            out_specs=[column, column, column, pl.BlockSpec((1, 2, PAIR), lambda p, s: (p, 0, 0))],
            scratch_shapes=[pltpu.VMEM((length, PAIR), jnp.float32)] * 2,
        ),
        out_shape=[out, out, out, jax.ShapeDtypeStruct((pairs, 2, PAIR), jnp.float32)],
        cost_estimate=pl.CostEstimate(
            flops=20 * length * length * heads_width,
            bytes_accessed=16 * length * heads_width,
            transcendentals=length * length * heads_width // HEAD,
        ),
    )(starts, qkv, qkv, qkv, mixed, grad_mixed, totals)


def make_local(shards, ctxs, tps):
    def ranks(move):
        pairs = []
        for s in range(shards):
            for c in range(ctxs):
                for t in range(tps):
                    s2, c2, t2 = move(s, c, t)
                    pairs.append(((s * ctxs + c) * tps + t, (s2 * ctxs + c2) * tps + t2))
        return pairs

    core_pairs = ranks(lambda s, c, t: (s, c ^ 1, t))
    x_pairs = ranks(lambda s, c, t: (s, c ^ 2, t))
    y_pairs = ranks(lambda s, c, t: (s, c, t ^ 1))
    z_pairs = [ranks(lambda s, c, t: ((s + r) % shards, c, t)) for r in range(shards)]
    direct = shards <= 8

    def to_core(values):
        return lax.ppermute(values, AXES, core_pairs)

    def to_x(values):
        return lax.ppermute(values, AXES, x_pairs)

    def to_y(values):
        return lax.ppermute(values, AXES, y_pairs)

    def put(base, values, at):
        return lax.dynamic_update_index_in_dim(base, values, at, 0)

    def z_gather(part):
        if not direct:
            return lax.all_gather(part, "shard", axis=0)
        here = lax.axis_index("shard")
        whole = jnp.zeros((shards,) + part.shape, part.dtype)
        whole = put(whole, part, here)
        for r in range(1, shards):
            got = lax.ppermute(part, AXES, z_pairs[r])
            whole = put(whole, got, lax.rem(here + shards - r, shards))
        return whole

    def z_reduce(blocks):
        if not direct:
            return lax.psum_scatter(blocks, "shard", scatter_dimension=0).astype(jnp.float32)
        here = lax.axis_index("shard")
        total = lax.dynamic_index_in_dim(blocks, here, 0, False).astype(jnp.float32)
        for r in range(1, shards):
            sent = lax.dynamic_index_in_dim(blocks, lax.rem(here + r, shards), 0, False)
            total = total + lax.ppermute(sent, AXES, z_pairs[r]).astype(jnp.float32)
        return total

    def sum_all(vector):
        vector = vector + to_core(vector)
        vector = vector + to_x(vector)
        vector = vector + to_y(vector)
        if not direct:
            return lax.psum(vector, "shard")
        return jnp.sum(z_gather(vector), axis=0)

    def pick(flag, former, latter):
        return jnp.where(flag, former, latter)

    def pair_order(index, mine, other):
        return jnp.stack([pick(index == 0, mine, other), pick(index == 0, other, mine)])

    def local(
        tokens,
        starts,
        w_query,
        w_key,
        w_value,
        w_out,
        w_up,
        w_down,
        head_bias,
        up_bias,
        out_biases,
        norm_gains,
        norm_shifts,
        cotangent,
    ):
        seq_dev, block, width = tokens.shape
        assert ctxs == 4 and tps == 2 and seq_dev == 4 and block == BLOCK
        rows_own = w_query.shape[0]
        half_width = w_query.shape[1]
        ctx = lax.axis_index("ctx")
        t = lax.axis_index("tp")
        core = lax.rem(ctx, 2)
        cx = lax.div(ctx, 2)
        seq_of = lambda cx_, t_: 2 * cx_ + t_
        seq = seq_of(cx, t)
        other_x = 1 - cx

        def take(array, index):
            return lax.dynamic_index_in_dim(array, index, 0, False)

        attn_local = low(jnp.concatenate([w_query, w_key, w_value], axis=1))
        attn_part = take(attn_local.reshape(2, rows_own // 2, 3 * half_width), core)
        attn_z = z_gather(attn_part)
        attn_y = to_y(attn_z)
        mine = pick(core == t, attn_z, attn_y)
        sent = pick(core == t, attn_y, attn_z)
        got = to_core(sent)
        qkv_full = jnp.stack(
            [pick(core == 0, mine, got), pick(core == 0, got, mine)], axis=1
        ).reshape(width, 3 * half_width)
        bias_other = to_y(head_bias)
        bias_here = pick(core == t, head_bias, bias_other)

        token_own = take(tokens, seq)
        token_far = to_x(take(tokens, seq_of(other_x, t)))
        rows_two = pair_order(cx, token_own, token_far)
        rows_peer = to_core(rows_two)
        rows_all = jnp.stack(
            [
                pick(core == 0, rows_two[0], rows_peer[0]),
                pick(core == 0, rows_peer[0], rows_two[0]),
                pick(core == 0, rows_two[1], rows_peer[1]),
                pick(core == 0, rows_peer[1], rows_two[1]),
            ]
        ).reshape(4 * block, width)
        rows_here = rows_two.reshape(2 * block, width)
        cot_own = take(cotangent, seq)
        cot_far = to_x(take(cotangent, seq_of(other_x, t)))
        cot_here = pair_order(cx, cot_own, cot_far).reshape(2 * block, width)

        def gather_a(local_block, after):
            shape = local_block.shape
            part = take(local_block.reshape(2, shape[0] // 2, shape[1]), core)
            part, _ = lax.optimization_barrier((part, after))
            z = z_gather(part)
            y = to_y(z)
            halves = pair_order(t, z, y)
            peer = to_core(halves)
            both = pair_order(core, halves, peer)
            return both.transpose(2, 0, 3, 1, 4).reshape(width, 2 * shape[1])

        def gather_b(local_block, after):
            shape = local_block.shape
            part = take(local_block.reshape(4, shape[0] // 4, shape[1]), ctx)
            part, _ = lax.optimization_barrier((part, after))
            z = z_gather(part)
            y = to_y(z)
            halves = pair_order(t, z, y)
            far = to_x(halves)
            quad = pair_order(cx, halves, far)
            peer = to_core(quad)
            both = pair_order(core, quad, peer)
            return both.transpose(3, 1, 0, 4, 2, 5).reshape(width, 2 * shape[1])

        first_hop = attn_z[0, 0, 0]
        out_full = gather_a(low(w_out), first_hop)
        up_full = gather_a(low(w_up), first_hop)
        down_full = gather_b(low(w_down), first_hop)
        up_bias_far = to_y(up_bias)
        up_bias_full = pair_order(t, up_bias, up_bias_far).reshape(-1)

        seq_starts = take(starts, seq)
        zero_row = jnp.zeros((half_width,), jnp.float32)
        qkv_bias = jnp.concatenate([bias_here[0], zero_row, bias_here[1]])
        columns = jnp.arange(3 * half_width)
        qkv_scale = jnp.where(columns < half_width, 1.0 / math.sqrt(HEAD), 1.0)
        qkv = low(low(matmul(rows_all, qkv_full) + qkv_bias).astype(jnp.float32) * qkv_scale)
        mixed_heads, totals = attend_forward(seq_starts, qkv, half_width)

        def split_rows(array):
            parts = array.reshape(2, 2, block, array.shape[1])
            one = parts[:, 0].reshape(2 * block, -1)
            two = parts[:, 1].reshape(2 * block, -1)
            return pick(core == 0, one, two), pick(core == 0, two, one)

        def join_columns(mine_, other_):
            return jnp.concatenate(
                [pick(core == 0, mine_, other_), pick(core == 0, other_, mine_)], axis=1
            )

        mixed_own, mixed_sent = split_rows(mixed_heads)
        mixed = join_columns(mixed_own, to_core(mixed_sent))

        attn_out = over_cols(mixed, out_full) + out_biases[0]
        first_scaled, first_rstd = normalize(rows_here.astype(jnp.float32) + attn_out)
        first_norm = first_scaled * norm_gains[0] + norm_shifts[0]
        first_low = low(first_norm)
        hidden = matmul(first_low, up_full) + up_bias_full
        gauss = 0.5 * (1.0 + lax.erf(hidden * (1.0 / math.sqrt(2.0))))
        active = low(hidden * gauss)
        slope = low(
            gauss + hidden * jnp.exp(-0.5 * hidden * hidden) * (1.0 / math.sqrt(2.0 * math.pi))
        )
        ffn_out = over_cols(active, down_full) + out_biases[1]
        second_scaled, second_rstd = normalize(first_norm + ffn_out)
        final_low = low(second_scaled * norm_gains[1] + norm_shifts[1])

        def deliver(rows):
            parts = rows.reshape(2, block, width)
            near = take(parts, cx)
            far = to_x(take(parts, other_x))
            near_y, far_y = to_y(near), to_y(far)
            result = jnp.zeros((seq_dev, block, width), rows.dtype)
            result = put(result, near, seq)
            result = put(result, far, seq_of(other_x, t))
            result = put(result, near_y, seq_of(cx, 1 - t))
            return put(result, far_y, seq_of(other_x, 1 - t))

        activations = deliver(final_low)

        grad_final = cot_here.astype(jnp.float32)
        gain_two = jnp.sum(grad_final * second_scaled, axis=0)
        shift_two = jnp.sum(grad_final, axis=0)
        grad_second = norm_back(grad_final, second_scaled, second_rstd, norm_gains[1])
        bias_two = jnp.sum(grad_second, axis=0)
        grad_ffn = low(grad_second)
        grad_active = matmul(grad_ffn, down_full)
        grad_hidden = grad_active * slope.astype(jnp.float32)
        up_bias_grad = jnp.sum(grad_hidden, axis=0)
        grad_hidden_low = low(grad_hidden)
        grad_first = grad_second + over_cols(grad_hidden_low, up_full)
        gain_one = jnp.sum(grad_first * first_scaled, axis=0)
        shift_one = jnp.sum(grad_first, axis=0)
        grad_sum_one = norm_back(grad_first, first_scaled, first_rstd, norm_gains[0])
        bias_one = jnp.sum(grad_sum_one, axis=0)
        grad_attn = low(grad_sum_one)
        grad_mixed = low(matmul(grad_attn, out_full))
        gm_halves = grad_mixed.reshape(2 * block, 2, half_width)
        gm_own = pick(core == 0, gm_halves[:, 0], gm_halves[:, 1])
        gm_sent = pick(core == 0, gm_halves[:, 1], gm_halves[:, 0])
        gm_peer = to_core(gm_sent)

        def join_rows(mine_, other_):
            mine_ = mine_.reshape(2, block, -1)
            other_ = other_.reshape(2, block, -1)
            return jnp.stack(
                [pick(core == 0, mine_, other_), pick(core == 0, other_, mine_)], axis=1
            ).reshape(4 * block, -1)

        grad_heads = join_rows(gm_own, gm_peer)
        grad_down_local = low(over_rows(grad_ffn, active))
        grad_up_local = low(over_rows(first_low, grad_hidden_low))
        grad_out_local = low(over_rows(grad_attn, mixed))

        def reduce_a(terms):
            cols = terms.shape[1] // 2
            parts = terms.reshape(shards, 2, rows_own // 2, 2, cols).transpose(1, 3, 0, 2, 4)
            parts = take(parts, core) + to_core(take(parts, 1 - core))
            parts = take(parts, t) + to_y(take(parts, 1 - t))
            block_ = low(z_reduce(parts))
            block_ = low(block_ + to_x(block_))
            return pair_order(core, block_, to_core(block_)).reshape(rows_own, cols).astype(
                jnp.float32
            )

        def reduce_b(terms):
            cols = terms.shape[1] // 2
            parts = terms.reshape(shards, 2, 2, rows_own // 4, 2, cols)
            parts = parts.transpose(2, 1, 4, 0, 3, 5)
            parts = take(parts, core) + to_core(take(parts, 1 - core))
            parts = take(parts, cx) + to_x(take(parts, other_x))
            parts = take(parts, t) + to_y(take(parts, 1 - t))
            block_ = low(z_reduce(parts))
            quad = pair_order(cx, block_, to_x(block_))
            both = pair_order(core, quad, to_core(quad))
            return both.transpose(1, 0, 2, 3).reshape(rows_own, cols).astype(jnp.float32)

        grad_down = reduce_b(grad_down_local)
        grad_up = reduce_a(grad_up_local)
        grad_out = reduce_a(grad_out_local)
        early = jnp.concatenate(
            [up_bias_grad, bias_one, bias_two, gain_one, gain_two, shift_one, shift_two]
        )
        early = sum_all(early)

        dq, dk, dv, head_sums = attend_backward(seq_starts, qkv, mixed_heads, grad_heads, totals)
        part_low = low(
            over_cols(dq, qkv_full[:, :half_width])
            + over_cols(dk, qkv_full[:, half_width : 2 * half_width])
            + over_cols(dv, qkv_full[:, 2 * half_width :])
        )
        part_own, part_sent = split_rows(part_low)
        part_peer = to_core(part_sent)
        input_rows = low(
            grad_sum_one + part_own.astype(jnp.float32) + part_peer.astype(jnp.float32)
        )
        input_grad = deliver(input_rows).astype(jnp.float32)

        head_grads = low(
            jnp.stack([over_rows(rows_all, dq), over_rows(rows_all, dk), over_rows(rows_all, dv)])
        )
        parts = head_grads.reshape(3, shards, 2, rows_own // 2, half_width)
        parts = parts.transpose(2, 1, 0, 3, 4)
        swapped = to_core(take(parts, 1 - core))
        kept = take(parts, core)
        for_here = pick(core == t, kept, swapped)
        for_there = pick(core == t, swapped, kept)
        parts = for_here + to_y(for_there)
        block_ = low(z_reduce(parts))
        block_ = low(block_ + to_x(block_))
        head_blocks = pair_order(core, block_, to_core(block_))
        head_blocks = head_blocks.transpose(1, 0, 2, 3).reshape(3, rows_own, half_width)
        head_blocks = head_blocks.astype(jnp.float32)

        sums = head_sums.transpose(1, 0, 2).reshape(2, half_width)
        both = jnp.zeros((2, 2, half_width), jnp.float32)
        both = sum_all(put(both, sums, core))
        grad_head_bias = take(both, t)

        units = up_bias_grad.shape[0]
        up_sum = take(early[:units].reshape(2, units // 2), t)
        pairs = early[units:].reshape(3, 2, width)
        return (
            activations,
            input_grad,
            head_blocks[0],
            head_blocks[1],
            head_blocks[2],
            grad_out,
            grad_up,
            grad_down,
            grad_head_bias,
            up_sum,
            pairs[0],
            pairs[1],
            pairs[2],
        )

    return local


def solution(mesh):
    sizes = [mesh.shape[name] for name in AXES]
    return jax.shard_map(
        make_local(*sizes),
        mesh=mesh,
        in_specs=(
            P("shard", "ctx", None),
            P("shard", None),
            P("shard", "tp"),
            P("shard", "tp"),
            P("shard", "tp"),
            P("shard", "tp"),
            P("shard", "tp"),
            P("shard", "tp"),
            P(None, "tp"),
            P("tp"),
            P(),
            P(),
            P(),
            P("shard", "ctx", None),
        ),
        out_specs=(
            P("shard", "ctx", None),
            P("shard", "ctx", None),
            P("shard", "tp"),
            P("shard", "tp"),
            P("shard", "tp"),
            P("shard", "tp"),
            P("shard", "tp"),
            P("shard", "tp"),
            P(None, "tp"),
            P("tp"),
            P(),
            P(),
            P(),
        ),
        check_vma=False,
    )
```

```python
import math

import jax
import jax.numpy as jnp
from jax import lax
from jax.experimental import pallas as pl
from jax.experimental.pallas import tpu as pltpu
from jax.sharding import PartitionSpec as P

HEAD = 64
PIECE = 256
BLOCK = 256
PAIR = 128

norm_eps = 1e-05
masked_score = -1e30
AXES = ("shard", "ctx", "tp")


def matmul(former, latter):
    return jnp.dot(former, latter, preferred_element_type=jnp.float32)


def over_rows(former, latter):
    return lax.dot_general(
        former, latter, (((0,), (0,)), ((), ())), preferred_element_type=jnp.float32
    )


def over_cols(former, latter):
    return lax.dot_general(
        former, latter, (((1,), (1,)), ((), ())), preferred_element_type=jnp.float32
    )


def low(values):
    return values.astype(jnp.bfloat16)


def normalize(values):
    centre = jnp.mean(values, axis=-1, keepdims=True)
    centred = values - centre
    spread = jnp.mean(centred * centred, axis=-1, keepdims=True)
    scaling = lax.rsqrt(spread + norm_eps)
    return (centred * scaling, scaling)


def norm_back(grad_out, scaled, scaling, gain_row):
    grad_scaled = grad_out * gain_row
    mean_grad = jnp.mean(grad_scaled, axis=-1, keepdims=True)
    mean_along = jnp.mean(grad_scaled * scaled, axis=-1, keepdims=True)
    return scaling * (grad_scaled - mean_grad - scaled * mean_along)


def edge_mask(starts_ref, seq, key_first, query_first, keys_first):
    key_shape = (BLOCK, 1) if keys_first else (1, BLOCK)
    query_shape = (1, BLOCK) if keys_first else (BLOCK, 1)
    key_at = key_first + lax.broadcasted_iota(jnp.int32, key_shape, 0 if keys_first else 1)
    query_at = query_first + lax.broadcasted_iota(jnp.int32, query_shape, 1 if keys_first else 0)
    seen = key_at <= query_at
    for piece in range(2):
        start = starts_ref[seq, piece]
        key_in = (key_at >= start) & (key_at < start + PIECE)
        query_in = (query_at >= start) & (query_at < start + PIECE)
        seen = seen | (key_in & query_in)
    return seen


def two_heads(rows):
    lane = lax.broadcasted_iota(jnp.int32, rows.shape, 1)
    zero = jnp.zeros_like(rows)
    return jnp.concatenate(
        [jnp.where(lane < HEAD, rows, zero), jnp.where(lane >= HEAD, rows, zero)], axis=0
    )


def join_heads(rows):
    half = rows.shape[0] // 2
    lane = lax.broadcasted_iota(jnp.int32, (half, rows.shape[1]), 1)
    return jnp.where(lane < HEAD, rows[:half], rows[half:])


def attend_pair(starts_ref, seq, q_ref, k_ref, v_ref, mixed_ref, total_ref):
    length = q_ref.shape[0]
    blocks = length // BLOCK
    for at in range(blocks):
        rows = slice(at * BLOCK, (at + 1) * BLOCK)
        reach = min(blocks, at + 2)
        queries = two_heads(q_ref[rows, :])
        scores = []
        for key_at in range(reach):
            part = over_cols(queries, k_ref[key_at * BLOCK : (key_at + 1) * BLOCK, :])
            if key_at >= at:
                seen = edge_mask(starts_ref, seq, key_at * BLOCK, at * BLOCK, False)
                seen = jnp.concatenate([seen, seen], axis=0)
                part = jnp.where(seen, part, masked_score)
            scores.append(part)
        scores = jnp.concatenate(scores, axis=1)
        top = jnp.max(scores, axis=1, keepdims=True)
        raised = jnp.exp(scores - top)
        total = jnp.sum(raised, axis=1, keepdims=True)
        mixed = matmul(low(raised), v_ref[: reach * BLOCK, :]) / total
        mixed_ref[rows, :] = low(join_heads(mixed))
        wide = jnp.broadcast_to(top + jnp.log(total), (2 * BLOCK, PAIR))
        row = jnp.transpose(wide)[0:1, :]
        total_ref[0:1, rows] = row[:, :BLOCK]
        total_ref[1:2, rows] = row[:, BLOCK:]


class Copies:
    def __init__(self):
        self.sent = []

    def start(self, when, make):
        self.sent.append((when, make))
        if when is None:
            make().start()
        else:
            pl.when(when)(lambda: make().start())

    def finish(self):
        for when, make in self.sent:
            if when is None:
                make().wait_send()
            else:
                pl.when(when)(lambda make=make: make().wait_send())


def both(former, latter):
    if former is None:
        return latter
    return former if latter is None else former & latter


def arrive(when, region, sem, device):
    def wait():
        pltpu.make_async_remote_copy(
            src_ref=region,
            dst_ref=region,
            send_sem=sem,
            recv_sem=sem,
            device_id=device,
            device_id_type=pl.DeviceIdType.MESH,
        ).wait_recv()

    if when is None:
        wait()
    else:
        pl.when(when)(wait)


class Place:
    def __init__(self, shards):
        self.shards = shards
        self.s = lax.axis_index("shard")
        self.c = lax.axis_index("ctx")
        self.t = lax.axis_index("tp")
        self.h = lax.rem(self.c, 2)
        self.cx = lax.div(self.c, 2)
        self.core = (self.s, self.c + 1 - 2 * self.h, self.t)
        self.x = (self.s, self.c + 2 - 4 * self.cx, self.t)
        self.y = (self.s, self.c, 1 - self.t)
        self.up = (self.s + 1, self.c, self.t)
        self.down = (self.s - 1, self.c, self.t)
        self.has_up = self.s < shards - 1
        self.has_down = self.s > 0

    def enter(self):
        barrier = pltpu.get_barrier_semaphore()

        def greet(device):
            pl.semaphore_signal(
                barrier, inc=1, device_id=device, device_id_type=pl.DeviceIdType.MESH
            )

        for device in (self.core, self.x, self.y):
            greet(device)
        pl.when(self.has_up)(lambda: greet(self.up))
        pl.when(self.has_down)(lambda: greet(self.down))
        vertical = jnp.where(self.has_up, 1, 0) + jnp.where(self.has_down, 1, 0)
        pl.semaphore_wait(barrier, 3 + vertical)

    def ring(self, k):
        if k == 0:
            return [(None, self.s)]
        return [(self.s - k >= 0, self.s - k), (self.s + k < self.shards, self.s + k)]


class Gather:
    def __init__(self, place, copies, sems, row, here, first):
        self.place, self.copies, self.row = place, copies, row
        self.sems, self.here, self.first = sems, here, first

    def copy(self, kind, index, source, target, device):
        send, recv = self.sems
        return pltpu.make_async_remote_copy(
            src_ref=source,
            dst_ref=target,
            send_sem=send.at[self.row, kind, index],
            recv_sem=recv.at[self.row, 0 if kind < 2 else kind - 1, index],
            device_id=device,
            device_id_type=pl.DeviceIdType.MESH,
        )

    def recv_sem(self, stage, block):
        return self.sems[1].at[self.row, stage, block]

    def source(self, k, block):
        return self.first if k == 0 else self.here(block, self.place.t)

    def z_send(self, k):
        p = self.place
        (under, below), *rest = p.ring(k - 1)
        over, above = rest[0] if rest else (under, below)
        self.copies.start(
            both(under, p.has_up),
            lambda: self.copy(0, below, self.source(k - 1, below), self.here(below, p.t), p.up),
        )
        self.copies.start(
            both(over, p.has_down),
            lambda: self.copy(1, above, self.source(k - 1, above), self.here(above, p.t), p.down),
        )

    def z_wait(self, k):
        p = self.place
        for when, block in p.ring(k):
            arrive(when, self.here(block, p.t), self.recv_sem(0, block), p.y)

    def y_send(self, k, part=lambda ref: ref):
        p = self.place
        for when, block in p.ring(k):
            self.copies.start(
                when,
                lambda block=block: self.copy(
                    2,
                    block,
                    part(self.source(k, block)),
                    part(self.here(block, p.t)),
                    p.y,
                ),
            )

    def y_wait(self, k, part=lambda ref: ref):
        p = self.place
        for when, block in p.ring(k):
            arrive(when, part(self.here(block, 1 - p.t)), self.recv_sem(1, block), p.y)

    def relay(self, kind, k, sent, device):
        for when, block in self.place.ring(k):
            self.copies.start(
                when,
                lambda block=block: self.copy(kind, block, sent(block), sent(block), device),
            )

    def relay_wait(self, kind, k, got, device):
        for when, block in self.place.ring(k):
            arrive(when, got(block), self.recv_sem(kind - 1, block), device)


def forward_kernel(
    shards,
    starts_ref,
    wq_ref,
    wk_ref,
    wv_ref,
    wo_ref,
    wu_ref,
    wd_ref,
    head_bias_ref,
    up_bias_ref,
    tokens_ref,
    cot_ref,
    x_ref,
    cot_rows_ref,
    wqkv_ref,
    qkv_ref,
    heads_ref,
    rows_ref,
    total_ref,
    out_ref,
    up_ref,
    down_ref,
    up_bias_out,
    x_all,
    wg,
    qkv,
    mixed,
    wo_low,
    wu_low,
    wd_low,
    bias_all,
    send,
    recv,
    token_send,
    token_recv,
    local_sem,
):
    p = Place(shards)
    copies = Copies()
    half = wq_ref.shape[1]
    quarter = wg.shape[4]
    units = wu_ref.shape[1]
    seq_of = lambda cx, t: 2 * cx + t
    seq = seq_of(p.cx, p.t)
    seq_far = seq_of(1 - p.cx, p.t)
    far = 2 * (1 - p.cx) + p.h
    peer = p.c + 1 - 2 * p.h
    locals_ = []

    def local(source, target):
        copy = pltpu.make_async_copy(source, target, local_sem.at[len(locals_)])
        copy.start()
        locals_.append(copy)
        return copy

    def remote(index, source, target, device):
        return pltpu.make_async_remote_copy(
            src_ref=source,
            dst_ref=target,
            send_sem=token_send.at[index],
            recv_sem=token_recv.at[index],
            device_id=device,
            device_id_type=pl.DeviceIdType.MESH,
        )

    own_tokens = local(tokens_ref.at[seq], x_all.at[p.c])
    cot_own = local(cot_ref.at[seq], cot_rows_ref.at[p.cx])
    for third, ref in enumerate((wq_ref, wk_ref, wv_ref)):
        for hh in range(2):
            for xx in range(2):
                first = (2 * hh + xx) * quarter
                wg[p.t, p.s, hh, xx, :, third * half : (third + 1) * half] = low(
                    ref[first : first + quarter, :]
                )
    p.enter()
    copies.start(None, lambda: remote(0, tokens_ref.at[seq_far], x_all.at[p.c], p.x))
    copies.start(None, lambda: remote(1, tokens_ref.at[seq], x_all.at[p.c], p.core))
    sems = (send, recv)
    attn = Gather(p, copies, sems, 0, lambda b, t: wg.at[t, b, p.h], wg.at[p.t, p.s, p.h])
    attn.z_send(1)
    sub = lambda ref: ref.at[p.cx]
    attn.y_send(0, sub)
    copies.start(None, lambda: remote(2, head_bias_ref, bias_all.at[p.t], p.y))
    copies.start(None, lambda: remote(3, up_bias_ref, up_bias_out.at[p.t], p.y))
    bias_all[p.t] = head_bias_ref[...]
    up_bias_out[p.t] = up_bias_ref[...]

    for hh in range(2):
        rows = slice(hh * 2 * quarter, (hh + 1) * 2 * quarter)
        wo_low[hh] = low(wo_ref[rows, :])
        wu_low[hh] = low(wu_ref[rows, :])
        for xx in range(2):
            first = (2 * hh + xx) * quarter
            wd_low[hh, xx] = low(wd_ref[first : first + quarter, :])
    cols = lambda t, n: pl.ds(pl.multiple_of(t * n, 128), n)
    local(wo_low.at[p.h], out_ref.at[p.s, p.h, :, cols(p.t, half)])
    local(wu_low.at[p.h], up_ref.at[p.s, p.h, :, cols(p.t, units)])
    local(wd_low.at[p.h, p.cx], down_ref.at[p.s, p.h, p.cx, :, cols(p.t, units)])
    own_weights = locals_[-3:]
    out = Gather(
        p, copies, sems, 1, lambda b, t: out_ref.at[b, p.h, :, cols(t, half)], wo_low.at[p.h]
    )
    up = Gather(
        p, copies, sems, 2, lambda b, t: up_ref.at[b, p.h, :, cols(t, units)], wu_low.at[p.h]
    )
    down = Gather(
        p,
        copies,
        sems,
        3,
        lambda b, t: down_ref.at[b, p.h, p.cx, :, cols(t, units)],
        wd_low.at[p.h, p.cx],
    )

    far_block = x_all.at[far]
    arrive(None, far_block, token_recv.at[0], p.x)
    copies.start(None, lambda: remote(4, far_block, far_block, p.core))
    copies.start(None, lambda: remote(5, cot_ref.at[seq_far], cot_rows_ref.at[p.cx], p.x))

    last = shards - 1
    for k in range(1, shards):
        attn.z_wait(k)
        if k < last:
            attn.z_send(k + 1)
        attn.y_send(k, sub)
        if k == max(1, last - 1):
            out.z_send(1)
            up.z_send(1)
    out.y_send(0)
    up.y_send(0)
    for k in range(shards):
        attn.y_wait(k, sub)
        attn.relay(3, k, lambda b: wg.at[1 - p.t, b, p.h, p.cx], p.x)
    for k in range(shards):
        attn.relay_wait(3, k, lambda b: wg.at[1 - p.t, b, p.h, 1 - p.cx], p.x)
        attn.relay(4, k, lambda b: wg.at[1 - p.h, b, p.h], p.core)
    down.z_send(1)
    for k in range(1, shards):
        out.z_wait(k)
        if k < last:
            out.z_send(k + 1)
        out.y_send(k)
    up.z_wait(1)
    if last > 1:
        up.z_send(2)
    up.y_send(1)
    for k in range(shards):
        attn.relay_wait(4, k, lambda b: wg.at[p.h, b, 1 - p.h], p.core)
    own_tokens.wait()
    peer_far = 2 * (1 - p.cx) + 1 - p.h
    arrive(None, x_all.at[peer], token_recv.at[1], p.core)
    arrive(None, x_all.at[peer_far], token_recv.at[4], p.core)
    arrive(None, bias_all.at[1 - p.t], token_recv.at[2], p.y)
    local(x_all, x_ref)
    local(wg.at[p.h], wqkv_ref)

    weights = wg[p.h].reshape(shards * 4 * quarter, 3 * half)
    bias = bias_all[p.h]
    scale = 1.0 / math.sqrt(HEAD)
    pairs = half // PAIR

    def project(at, carry):
        result = matmul(x_all[at], weights)
        rows = pl.ds(pl.multiple_of(at * BLOCK, BLOCK), BLOCK)
        for j in range(3 * pairs):
            part = result[:, j * PAIR : (j + 1) * PAIR]
            if j < pairs:
                part = low(part + bias[0:1, j * PAIR : (j + 1) * PAIR])
                part = low(part.astype(jnp.float32) * scale)
            elif j < 2 * pairs:
                part = low(part)
            else:
                column = (j - 2 * pairs) * PAIR
                part = low(part + bias[1:2, column : column + PAIR])
            qkv[j, rows, :] = part
        return carry

    lax.fori_loop(0, x_all.shape[0], project, 0)
    local(qkv, qkv_ref)

    def on_the_way(stage):
        if stage == 0:
            up.z_wait(2)
            if last > 2:
                up.z_send(3)
            up.y_send(2)
            down.z_wait(1)
            if last > 1:
                down.z_send(2)
            down.y_send(0)
            down.y_send(1)
        if stage == 1:
            for k in range(3, shards):
                up.z_wait(k)
                if k < last:
                    up.z_send(k + 1)
                up.y_send(k)
            down.z_wait(2)
            if last > 2:
                down.z_send(3)
            down.y_send(2)
            for k in range(shards):
                out.y_wait(k)
                if k == 0:
                    for copy in own_weights:
                        copy.wait()
                out.relay(4, k, lambda b: out_ref.at[b, p.h], p.core)

    def attend(pair, carry):
        attend_pair(
            starts_ref,
            seq,
            qkv.at[pair],
            qkv.at[pairs + pair],
            qkv.at[2 * pairs + pair],
            mixed.at[pair],
            total_ref.at[pair],
        )
        return carry

    lax.fori_loop(0, 1, attend, 0)
    on_the_way(0)
    lax.fori_loop(1, 2, attend, 0)
    on_the_way(1)
    lax.fori_loop(2, pairs, attend, 0)

    def heads_of(late, hh, pair):
        column = pl.multiple_of(hh * half + pair * PAIR, PAIR)
        return rows_ref.at[late, :, pl.ds(column, PAIR)]

    for pair in range(pairs):
        for late in range(2):
            block = 2 * late + 1 - p.h
            index = 6 + 2 * pair + late
            rows = pl.ds(pl.multiple_of(block * BLOCK, BLOCK), BLOCK)
            copies.start(
                None,
                lambda index=index, pair=pair, rows=rows, late=late: remote(
                    index, mixed.at[pair, rows, :], heads_of(late, p.h, pair), p.core
                ),
            )
    for pair in range(pairs):
        local(mixed.at[pair], heads_ref.at[pair])
        for late in range(2):
            rows = pl.ds(pl.multiple_of((2 * late + p.h) * BLOCK, BLOCK), BLOCK)
            local(mixed.at[pair, rows, :], heads_of(late, p.h, pair))

    for k in range(3, shards):
        down.z_wait(k)
        if k < last:
            down.z_send(k + 1)
        down.y_send(k)
    for k in range(shards):
        up.y_wait(k)
        up.relay(4, k, lambda b: up_ref.at[b, p.h], p.core)
    for k in range(shards):
        down.y_wait(k)
        down.relay(3, k, lambda b: down_ref.at[b, p.h, p.cx], p.x)
    for k in range(shards):
        down.relay_wait(3, k, lambda b: down_ref.at[b, p.h, 1 - p.cx], p.x)
        down.relay(4, k, lambda b: down_ref.at[b, p.h], p.core)
    for k in range(shards):
        out.relay_wait(4, k, lambda b: out_ref.at[b, 1 - p.h], p.core)
        up.relay_wait(4, k, lambda b: up_ref.at[b, 1 - p.h], p.core)
        down.relay_wait(4, k, lambda b: down_ref.at[b, 1 - p.h], p.core)
    for pair in range(pairs):
        for late in range(2):
            index = 6 + 2 * pair + late
            arrive(None, heads_of(late, 1 - p.h, pair), token_recv.at[index], p.core)
    arrive(None, up_bias_out.at[1 - p.t], token_recv.at[3], p.y)
    arrive(None, cot_rows_ref.at[1 - p.cx], token_recv.at[5], p.x)
    copies.finish()
    for copy in locals_:
        if all(copy is not done for done in [own_tokens] + own_weights):
            copy.wait()


def forward(shards, starts, weights, head_bias, up_bias, tokens, cotangent):
    w_query, w_out, w_up = weights[0], weights[3], weights[4]
    seq_dev, block, width = tokens.shape
    rows_own, half = w_query.shape
    units = w_up.shape[1]
    quarter = rows_own // 4
    pairs = half // PAIR
    length = seq_dev * block
    low_type, full_type = jnp.bfloat16, jnp.float32
    shape = jax.ShapeDtypeStruct
    vmem = pl.BlockSpec(memory_space=pltpu.VMEM)
    anywhere = pl.BlockSpec(memory_space=pl.ANY)
    return pl.pallas_call(
        lambda *refs: forward_kernel(shards, *refs),
        in_specs=[pl.BlockSpec(memory_space=pltpu.SMEM)] + [vmem] * 8 + [anywhere] * 2,
        out_specs=[anywhere] * 6 + [vmem] + [anywhere] * 3 + [vmem],
        out_shape=[
            shape((seq_dev, block, width), low_type),
            shape((2, block, width), low_type),
            shape((shards, 2, 2, quarter, 3 * half), low_type),
            shape((3 * pairs, length, PAIR), low_type),
            shape((pairs, length, PAIR), low_type),
            shape((2, block, 2 * half), low_type),
            shape((pairs, 2, length), full_type),
            shape((shards, 2, 2 * quarter, 2 * half), low_type),
            shape((shards, 2, 2 * quarter, 2 * units), low_type),
            shape((shards, 2, 2, quarter, 2 * units), low_type),
            shape((2, 1, units), full_type),
        ],
        scratch_shapes=[
            pltpu.VMEM((seq_dev, block, width), low_type),
            pltpu.VMEM((2, shards, 2, 2, quarter, 3 * half), low_type),
            pltpu.VMEM((3 * pairs, length, PAIR), low_type),
            pltpu.VMEM((pairs, length, PAIR), low_type),
            pltpu.VMEM((2, 2 * quarter, half), low_type),
            pltpu.VMEM((2, 2 * quarter, units), low_type),
            pltpu.VMEM((2, 2, quarter, units), low_type),
            pltpu.VMEM((2, 2, half), full_type),
            pltpu.SemaphoreType.DMA((4, 5, shards)),
            pltpu.SemaphoreType.DMA((4, 4, shards)),
            pltpu.SemaphoreType.DMA((6 + 2 * pairs,)),
            pltpu.SemaphoreType.DMA((6 + 2 * pairs,)),
            pltpu.SemaphoreType.DMA((8 + 3 * pairs,)),
        ],
        compiler_params=pltpu.CompilerParams(
            collective_id=1, has_side_effects=True, vmem_limit_bytes=60 * 1024 * 1024
        ),
    )(starts, *weights, head_bias, up_bias, tokens, cotangent)


def attend_back_kernel(
    starts_ref,
    q_ref,
    k_ref,
    v_ref,
    mixed_ref,
    grad_ref,
    total_ref,
    dq_ref,
    dk_ref,
    dv_ref,
    sums_ref,
    dk_acc,
    dv_acc,
):
    length = q_ref.shape[0]
    blocks = length // BLOCK
    query_sum = jnp.zeros((1, PAIR), jnp.float32)
    for at in range(blocks):
        rows = slice(at * BLOCK, (at + 1) * BLOCK)
        reach = min(blocks, at + 2)
        span = slice(0, reach * BLOCK)
        queries = two_heads(q_ref[rows, :])
        grads = two_heads(grad_ref[rows, :])
        along = grad_ref[rows, :].astype(jnp.float32) * mixed_ref[rows, :].astype(jnp.float32)
        along = jnp.transpose(along)
        inner = jnp.concatenate(
            [
                jnp.sum(along[:HEAD], axis=0, keepdims=True),
                jnp.sum(along[HEAD:], axis=0, keepdims=True),
            ],
            axis=1,
        )
        total = jnp.concatenate([total_ref[0, 0:1, rows], total_ref[0, 1:2, rows]], axis=1)
        scores = []
        for key_at in range(reach):
            part = over_cols(k_ref[key_at * BLOCK : (key_at + 1) * BLOCK, :], queries)
            if key_at >= at:
                seen = edge_mask(starts_ref, 0, key_at * BLOCK, at * BLOCK, True)
                seen = jnp.concatenate([seen, seen], axis=1)
                part = jnp.where(seen, part, masked_score)
            scores.append(part)
        probs = jnp.exp(jnp.concatenate(scores, axis=0) - total)
        grad_probs = over_cols(v_ref[span, :], grads)
        grad_scores = low(probs * (grad_probs - inner))
        dv = matmul(low(probs), grads)
        dk = matmul(grad_scores, queries)
        fresh = slice(max(0, (reach - 1)) * BLOCK, reach * BLOCK) if at + 1 < blocks else None
        if at == 0:
            dv_acc[span, :] = dv
            dk_acc[span, :] = dk
        elif fresh is None:
            dv_acc[span, :] += dv
            dk_acc[span, :] += dk
        else:
            old = slice(0, (reach - 1) * BLOCK)
            dv_acc[old, :] += dv[old, :]
            dk_acc[old, :] += dk[old, :]
            dv_acc[fresh, :] = dv[fresh, :]
            dk_acc[fresh, :] = dk[fresh, :]
        dq = join_heads(over_rows(grad_scores, k_ref[span, :])) * (1.0 / math.sqrt(HEAD))
        query_sum += jnp.sum(dq, axis=0, keepdims=True)
        dq_ref[rows, :] = low(dq)
    dk_ref[...] = low(dk_acc[...])
    dv_ref[...] = low(dv_acc[...])
    sums_ref[0, 0:1, :] = query_sum
    sums_ref[0, 1:2, :] = jnp.sum(dv_acc[...], axis=0, keepdims=True)


def attend_backward(starts, qkv, mixed, grad_mixed, totals):
    length, heads_width = grad_mixed.shape
    pairs = heads_width // PAIR
    column = pl.BlockSpec((length, PAIR), lambda p, s: (0, p))
    out = jax.ShapeDtypeStruct((length, heads_width), jnp.bfloat16)
    return pl.pallas_call(
        attend_back_kernel,
        grid_spec=pltpu.PrefetchScalarGridSpec(
            num_scalar_prefetch=1,
            grid=(pairs,),
            in_specs=[
                pl.BlockSpec((None, length, PAIR), lambda p, s: (p, 0, 0)),
                pl.BlockSpec((None, length, PAIR), lambda p, s: (p + pairs, 0, 0)),
                pl.BlockSpec((None, length, PAIR), lambda p, s: (p + 2 * pairs, 0, 0)),
                pl.BlockSpec((None, length, PAIR), lambda p, s: (p, 0, 0)),
                column,
                pl.BlockSpec((1, 2, length), lambda p, s: (p, 0, 0)),
            ],
            out_specs=[column, column, column, pl.BlockSpec((1, 2, PAIR), lambda p, s: (p, 0, 0))],
            scratch_shapes=[pltpu.VMEM((length, PAIR), jnp.float32)] * 2,
        ),
        out_shape=[out, out, out, jax.ShapeDtypeStruct((pairs, 2, PAIR), jnp.float32)],
        cost_estimate=pl.CostEstimate(
            flops=20 * length * length * heads_width,
            bytes_accessed=16 * length * heads_width,
            transcendentals=length * length * heads_width // HEAD,
        ),
    )(starts, qkv, qkv, qkv, mixed, grad_mixed, totals)


def make_local(shards, ctxs, tps):
    def ranks(move):
        pairs = []
        for s in range(shards):
            for c in range(ctxs):
                for t in range(tps):
                    s2, c2, t2 = move(s, c, t)
                    pairs.append(((s * ctxs + c) * tps + t, (s2 * ctxs + c2) * tps + t2))
        return pairs

    core_pairs = ranks(lambda s, c, t: (s, c ^ 1, t))
    x_pairs = ranks(lambda s, c, t: (s, c ^ 2, t))
    y_pairs = ranks(lambda s, c, t: (s, c, t ^ 1))
    z_pairs = [ranks(lambda s, c, t: ((s + r) % shards, c, t)) for r in range(shards)]
    direct = shards <= 8

    def to_core(values):
        return lax.ppermute(values, AXES, core_pairs)

    def to_x(values):
        return lax.ppermute(values, AXES, x_pairs)

    def to_y(values):
        return lax.ppermute(values, AXES, y_pairs)

    def put(base, values, at):
        return lax.dynamic_update_index_in_dim(base, values, at, 0)

    def z_gather(part):
        if not direct:
            return lax.all_gather(part, "shard", axis=0)
        here = lax.axis_index("shard")
        whole = jnp.zeros((shards,) + part.shape, part.dtype)
        whole = put(whole, part, here)
        for r in range(1, shards):
            got = lax.ppermute(part, AXES, z_pairs[r])
            whole = put(whole, got, lax.rem(here + shards - r, shards))
        return whole

    def z_reduce(blocks):
        if not direct:
            return lax.psum_scatter(blocks, "shard", scatter_dimension=0).astype(jnp.float32)
        here = lax.axis_index("shard")
        total = lax.dynamic_index_in_dim(blocks, here, 0, False).astype(jnp.float32)
        for r in range(1, shards):
            sent = lax.dynamic_index_in_dim(blocks, lax.rem(here + r, shards), 0, False)
            total = total + lax.ppermute(sent, AXES, z_pairs[r]).astype(jnp.float32)
        return total

    def sum_all(vector):
        vector = vector + to_core(vector)
        vector = vector + to_x(vector)
        vector = vector + to_y(vector)
        if not direct:
            return lax.psum(vector, "shard")
        return jnp.sum(z_gather(vector), axis=0)

    def pick(flag, former, latter):
        return jnp.where(flag, former, latter)

    def pair_order(index, mine, other):
        return jnp.stack([pick(index == 0, mine, other), pick(index == 0, other, mine)])

    def local(
        tokens,
        starts,
        w_query,
        w_key,
        w_value,
        w_out,
        w_up,
        w_down,
        head_bias,
        up_bias,
        out_biases,
        norm_gains,
        norm_shifts,
        cotangent,
    ):
        seq_dev, block, width = tokens.shape
        assert ctxs == 4 and tps == 2 and seq_dev == 4 and block == BLOCK
        rows_own = w_query.shape[0]
        half_width = w_query.shape[1]
        ctx = lax.axis_index("ctx")
        t = lax.axis_index("tp")
        core = lax.rem(ctx, 2)
        cx = lax.div(ctx, 2)
        seq_of = lambda cx_, t_: 2 * cx_ + t_
        seq = seq_of(cx, t)
        other_x = 1 - cx

        def take(array, index):
            return lax.dynamic_index_in_dim(array, index, 0, False)

        (
            x_blocks,
            cot_rows,
            wqkv,
            qkv,
            mixed_heads,
            mixed_rows,
            totals,
            out_full,
            up_full,
            down_full,
            up_bias_full,
        ) = forward(
            shards,
            starts,
            (w_query, w_key, w_value, w_out, w_up, w_down),
            head_bias,
            up_bias.reshape(1, -1),
            tokens,
            cotangent,
        )
        rows_all = x_blocks.reshape(4 * block, width)
        x_pairs_ = x_blocks.reshape(2, 2, block, width)
        rows_here = pick(core == 0, x_pairs_[:, 0], x_pairs_[:, 1]).reshape(2 * block, width)
        cot_here = cot_rows.reshape(2 * block, width)
        qkv_full = wqkv.reshape(width, 3 * half_width)
        out_full = out_full.reshape(width, -1)
        up_full = up_full.reshape(width, -1)
        down_full = down_full.reshape(width, -1)
        up_bias_full = up_bias_full.reshape(-1)
        mixed = mixed_rows.reshape(2 * block, width)
        seq_starts = lax.dynamic_slice_in_dim(starts, seq, 1, 0)

        def split_rows(array):
            parts = array.reshape(2, 2, block, array.shape[1])
            one = parts[:, 0].reshape(2 * block, -1)
            two = parts[:, 1].reshape(2 * block, -1)
            return pick(core == 0, one, two), pick(core == 0, two, one)

        attn_out = over_cols(mixed, out_full) + out_biases[0]
        first_scaled, first_rstd = normalize(rows_here.astype(jnp.float32) + attn_out)
        first_norm = first_scaled * norm_gains[0] + norm_shifts[0]
        first_low = low(first_norm)
        hidden = matmul(first_low, up_full) + up_bias_full
        gauss = 0.5 * (1.0 + lax.erf(hidden * (1.0 / math.sqrt(2.0))))
        active = low(hidden * gauss)
        slope = low(
            gauss + hidden * jnp.exp(-0.5 * hidden * hidden) * (1.0 / math.sqrt(2.0 * math.pi))
        )
        ffn_out = over_cols(active, down_full) + out_biases[1]
        second_scaled, second_rstd = normalize(first_norm + ffn_out)
        final_low = low(second_scaled * norm_gains[1] + norm_shifts[1])

        def deliver(rows):
            parts = rows.reshape(2, block, width)
            near = take(parts, cx)
            far = to_x(take(parts, other_x))
            near_y, far_y = to_y(near), to_y(far)
            result = jnp.zeros((seq_dev, block, width), rows.dtype)
            result = put(result, near, seq)
            result = put(result, far, seq_of(other_x, t))
            result = put(result, near_y, seq_of(cx, 1 - t))
            return put(result, far_y, seq_of(other_x, 1 - t))

        activations = deliver(final_low)

        grad_final = cot_here.astype(jnp.float32)
        gain_two = jnp.sum(grad_final * second_scaled, axis=0)
        shift_two = jnp.sum(grad_final, axis=0)
        grad_second = norm_back(grad_final, second_scaled, second_rstd, norm_gains[1])
        bias_two = jnp.sum(grad_second, axis=0)
        grad_ffn = low(grad_second)
        grad_active = matmul(grad_ffn, down_full)
        grad_hidden = grad_active * slope.astype(jnp.float32)
        up_bias_grad = jnp.sum(grad_hidden, axis=0)
        grad_hidden_low = low(grad_hidden)
        grad_first = grad_second + over_cols(grad_hidden_low, up_full)
        gain_one = jnp.sum(grad_first * first_scaled, axis=0)
        shift_one = jnp.sum(grad_first, axis=0)
        grad_sum_one = norm_back(grad_first, first_scaled, first_rstd, norm_gains[0])
        bias_one = jnp.sum(grad_sum_one, axis=0)
        grad_attn = low(grad_sum_one)
        grad_mixed = low(matmul(grad_attn, out_full))
        gm_halves = grad_mixed.reshape(2 * block, 2, half_width)
        gm_own = pick(core == 0, gm_halves[:, 0], gm_halves[:, 1])
        gm_sent = pick(core == 0, gm_halves[:, 1], gm_halves[:, 0])
        gm_peer = to_core(gm_sent)

        def join_rows(mine_, other_):
            mine_ = mine_.reshape(2, block, -1)
            other_ = other_.reshape(2, block, -1)
            return jnp.stack(
                [pick(core == 0, mine_, other_), pick(core == 0, other_, mine_)], axis=1
            ).reshape(4 * block, -1)

        grad_heads = join_rows(gm_own, gm_peer)
        grad_down_local = low(over_rows(grad_ffn, active))
        grad_up_local = low(over_rows(first_low, grad_hidden_low))
        grad_out_local = low(over_rows(grad_attn, mixed))

        def reduce_a(terms):
            cols = terms.shape[1] // 2
            parts = terms.reshape(shards, 2, rows_own // 2, 2, cols).transpose(1, 3, 0, 2, 4)
            parts = take(parts, core) + to_core(take(parts, 1 - core))
            parts = take(parts, t) + to_y(take(parts, 1 - t))
            block_ = low(z_reduce(parts))
            block_ = low(block_ + to_x(block_))
            return pair_order(core, block_, to_core(block_)).reshape(rows_own, cols).astype(
                jnp.float32
            )

        def reduce_b(terms):
            cols = terms.shape[1] // 2
            parts = terms.reshape(shards, 2, 2, rows_own // 4, 2, cols)
            parts = parts.transpose(2, 1, 4, 0, 3, 5)
            parts = take(parts, core) + to_core(take(parts, 1 - core))
            parts = take(parts, cx) + to_x(take(parts, other_x))
            parts = take(parts, t) + to_y(take(parts, 1 - t))
            block_ = low(z_reduce(parts))
            quad = pair_order(cx, block_, to_x(block_))
            both = pair_order(core, quad, to_core(quad))
            return both.transpose(1, 0, 2, 3).reshape(rows_own, cols).astype(jnp.float32)

        grad_down = reduce_b(grad_down_local)
        grad_up = reduce_a(grad_up_local)
        grad_out = reduce_a(grad_out_local)
        early = jnp.concatenate(
            [up_bias_grad, bias_one, bias_two, gain_one, gain_two, shift_one, shift_two]
        )
        early = sum_all(early)

        dq, dk, dv, head_sums = attend_backward(seq_starts, qkv, mixed_heads, grad_heads, totals)
        part_low = low(
            over_cols(dq, qkv_full[:, :half_width])
            + over_cols(dk, qkv_full[:, half_width : 2 * half_width])
            + over_cols(dv, qkv_full[:, 2 * half_width :])
        )
        part_own, part_sent = split_rows(part_low)
        part_peer = to_core(part_sent)
        input_rows = low(
            grad_sum_one + part_own.astype(jnp.float32) + part_peer.astype(jnp.float32)
        )
        input_grad = deliver(input_rows).astype(jnp.float32)

        head_grads = low(
            jnp.stack([over_rows(rows_all, dq), over_rows(rows_all, dk), over_rows(rows_all, dv)])
        )
        parts = head_grads.reshape(3, shards, 2, rows_own // 2, half_width)
        parts = parts.transpose(2, 1, 0, 3, 4)
        swapped = to_core(take(parts, 1 - core))
        kept = take(parts, core)
        for_here = pick(core == t, kept, swapped)
        for_there = pick(core == t, swapped, kept)
        parts = for_here + to_y(for_there)
        block_ = low(z_reduce(parts))
        block_ = low(block_ + to_x(block_))
        head_blocks = pair_order(core, block_, to_core(block_))
        head_blocks = head_blocks.transpose(1, 0, 2, 3).reshape(3, rows_own, half_width)
        head_blocks = head_blocks.astype(jnp.float32)

        sums = head_sums.transpose(1, 0, 2).reshape(2, half_width)
        both = jnp.zeros((2, 2, half_width), jnp.float32)
        both = sum_all(put(both, sums, core))
        grad_head_bias = take(both, t)

        units = up_bias_grad.shape[0]
        up_sum = take(early[:units].reshape(2, units // 2), t)
        pairs = early[units:].reshape(3, 2, width)
        return (
            activations,
            input_grad,
            head_blocks[0],
            head_blocks[1],
            head_blocks[2],
            grad_out,
            grad_up,
            grad_down,
            grad_head_bias,
            up_sum,
            pairs[0],
            pairs[1],
            pairs[2],
        )

    return local


def solution(mesh):
    sizes = [mesh.shape[name] for name in AXES]
    return jax.shard_map(
        make_local(*sizes),
        mesh=mesh,
        in_specs=(
            P("shard", "ctx", None),
            P("shard", None),
            P("shard", "tp"),
            P("shard", "tp"),
            P("shard", "tp"),
            P("shard", "tp"),
            P("shard", "tp"),
            P("shard", "tp"),
            P(None, "tp"),
            P("tp"),
            P(),
            P(),
            P(),
            P("shard", "ctx", None),
        ),
        out_specs=(
            P("shard", "ctx", None),
            P("shard", "ctx", None),
            P("shard", "tp"),
            P("shard", "tp"),
            P("shard", "tp"),
            P("shard", "tp"),
            P("shard", "tp"),
            P("shard", "tp"),
            P(None, "tp"),
            P("tp"),
            P(),
            P(),
            P(),
        ),
        check_vma=False,
    )
```

```python
import math

import jax
import jax.numpy as jnp
from jax import lax
from jax.experimental import pallas as pl
from jax.experimental.pallas import tpu as pltpu
from jax.sharding import PartitionSpec as P

HEAD = 64
PIECE = 256
BLOCK = 256
PAIR = 128

norm_eps = 1e-05
masked_score = -1e30
AXES = ("shard", "ctx", "tp")


def matmul(former, latter):
    return jnp.dot(former, latter, preferred_element_type=jnp.float32)


def over_rows(former, latter):
    return lax.dot_general(
        former, latter, (((0,), (0,)), ((), ())), preferred_element_type=jnp.float32
    )


def over_cols(former, latter):
    return lax.dot_general(
        former, latter, (((1,), (1,)), ((), ())), preferred_element_type=jnp.float32
    )


def low(values):
    return values.astype(jnp.bfloat16)


def normalize(values):
    centre = jnp.mean(values, axis=-1, keepdims=True)
    centred = values - centre
    spread = jnp.mean(centred * centred, axis=-1, keepdims=True)
    scaling = lax.rsqrt(spread + norm_eps)
    return (centred * scaling, scaling)


def norm_back(grad_out, scaled, scaling, gain_row):
    grad_scaled = grad_out * gain_row
    mean_grad = jnp.mean(grad_scaled, axis=-1, keepdims=True)
    mean_along = jnp.mean(grad_scaled * scaled, axis=-1, keepdims=True)
    return scaling * (grad_scaled - mean_grad - scaled * mean_along)


def edge_mask(starts_ref, seq, key_first, query_first, keys_first):
    key_shape = (BLOCK, 1) if keys_first else (1, BLOCK)
    query_shape = (1, BLOCK) if keys_first else (BLOCK, 1)
    key_at = key_first + lax.broadcasted_iota(jnp.int32, key_shape, 0 if keys_first else 1)
    query_at = query_first + lax.broadcasted_iota(jnp.int32, query_shape, 1 if keys_first else 0)
    seen = key_at <= query_at
    for piece in range(2):
        start = starts_ref[seq, piece]
        key_in = (key_at >= start) & (key_at < start + PIECE)
        query_in = (query_at >= start) & (query_at < start + PIECE)
        seen = seen | (key_in & query_in)
    return seen


def two_heads(rows):
    lane = lax.broadcasted_iota(jnp.int32, rows.shape, 1)
    zero = jnp.zeros_like(rows)
    return jnp.concatenate(
        [jnp.where(lane < HEAD, rows, zero), jnp.where(lane >= HEAD, rows, zero)], axis=0
    )


def join_heads(rows):
    half = rows.shape[0] // 2
    lane = lax.broadcasted_iota(jnp.int32, (half, rows.shape[1]), 1)
    return jnp.where(lane < HEAD, rows[:half], rows[half:])


def attend_pair(starts_ref, seq, q_ref, k_ref, v_ref, mixed_ref, total_ref):
    length = q_ref.shape[0]
    blocks = length // BLOCK
    for at in range(blocks):
        rows = slice(at * BLOCK, (at + 1) * BLOCK)
        reach = min(blocks, at + 2)
        queries = two_heads(q_ref[rows, :])
        scores = []
        for key_at in range(reach):
            part = over_cols(queries, k_ref[key_at * BLOCK : (key_at + 1) * BLOCK, :])
            if key_at >= at:
                seen = edge_mask(starts_ref, seq, key_at * BLOCK, at * BLOCK, False)
                seen = jnp.concatenate([seen, seen], axis=0)
                part = jnp.where(seen, part, masked_score)
            scores.append(part)
        scores = jnp.concatenate(scores, axis=1)
        top = jnp.max(scores, axis=1, keepdims=True)
        raised = jnp.exp(scores - top)
        total = jnp.sum(raised, axis=1, keepdims=True)
        mixed = matmul(low(raised), v_ref[: reach * BLOCK, :]) / total
        mixed_ref[rows, :] = low(join_heads(mixed))
        wide = jnp.broadcast_to(top + jnp.log(total), (2 * BLOCK, PAIR))
        row = jnp.transpose(wide)[0:1, :]
        total_ref[0:1, rows] = row[:, :BLOCK]
        total_ref[1:2, rows] = row[:, BLOCK:]


class Copies:
    def __init__(self):
        self.sent = []

    def start(self, when, make):
        self.sent.append((when, make))
        if when is None:
            make().start()
        else:
            pl.when(when)(lambda: make().start())

    def finish(self):
        for when, make in self.sent:
            if when is None:
                make().wait_send()
            else:
                pl.when(when)(lambda make=make: make().wait_send())


def both(former, latter):
    if former is None:
        return latter
    return former if latter is None else former & latter


def arrive(when, region, sem, device):
    def wait():
        pltpu.make_async_remote_copy(
            src_ref=region,
            dst_ref=region,
            send_sem=sem,
            recv_sem=sem,
            device_id=device,
            device_id_type=pl.DeviceIdType.MESH,
        ).wait_recv()

    if when is None:
        wait()
    else:
        pl.when(when)(wait)


class Place:
    def __init__(self, shards):
        self.shards = shards
        self.s = lax.axis_index("shard")
        self.c = lax.axis_index("ctx")
        self.t = lax.axis_index("tp")
        self.h = lax.rem(self.c, 2)
        self.cx = lax.div(self.c, 2)
        self.core = (self.s, self.c + 1 - 2 * self.h, self.t)
        self.x = (self.s, self.c + 2 - 4 * self.cx, self.t)
        self.y = (self.s, self.c, 1 - self.t)
        self.up = (self.s + 1, self.c, self.t)
        self.down = (self.s - 1, self.c, self.t)
        self.nh, self.nx, self.nt = 1 - self.h, 1 - self.cx, 1 - self.t
        self.steps = [
            (lax.rem(self.s + r, shards), lax.rem(self.s + shards - r, shards))
            for r in range(1, shards)
        ]
        self.has_up = self.s < shards - 1
        self.has_down = self.s > 0

    def enter(self, whole_line):
        barrier = pltpu.get_barrier_semaphore()

        def greet(device):
            pl.semaphore_signal(
                barrier, inc=1, device_id=device, device_id_type=pl.DeviceIdType.MESH
            )

        for device in (self.core, self.x, self.y):
            greet(device)
        if whole_line:
            for there, _ in self.steps:
                greet((there, self.c, self.t))
            pl.semaphore_wait(barrier, 3 + len(self.steps))
            return
        pl.when(self.has_up)(lambda: greet(self.up))
        pl.when(self.has_down)(lambda: greet(self.down))
        vertical = jnp.where(self.has_up, 1, 0) + jnp.where(self.has_down, 1, 0)
        pl.semaphore_wait(barrier, 3 + vertical)

    def ring(self, k):
        if k == 0:
            return [(None, self.s)]
        return [(self.s - k >= 0, self.s - k), (self.s + k < self.shards, self.s + k)]


class Gather:
    def __init__(self, place, copies, sems, row, here, first):
        self.place, self.copies, self.row = place, copies, row
        self.sems, self.here, self.first = sems, here, first

    def copy(self, kind, index, source, target, device):
        send, recv = self.sems
        return pltpu.make_async_remote_copy(
            src_ref=source,
            dst_ref=target,
            send_sem=send.at[self.row, kind, index],
            recv_sem=recv.at[self.row, 0 if kind < 2 else kind - 1, index],
            device_id=device,
            device_id_type=pl.DeviceIdType.MESH,
        )

    def recv_sem(self, stage, block):
        return self.sems[1].at[self.row, stage, block]

    def source(self, k, block):
        return self.first if k == 0 else self.here(block, self.place.t)

    def z_send(self, k):
        p = self.place
        (under, below), *rest = p.ring(k - 1)
        over, above = rest[0] if rest else (under, below)
        self.copies.start(
            both(under, p.has_up),
            lambda: self.copy(0, below, self.source(k - 1, below), self.here(below, p.t), p.up),
        )
        self.copies.start(
            both(over, p.has_down),
            lambda: self.copy(1, above, self.source(k - 1, above), self.here(above, p.t), p.down),
        )

    def z_wait(self, k):
        p = self.place
        for when, block in p.ring(k):
            arrive(when, self.here(block, p.t), self.recv_sem(0, block), p.y)

    def y_send(self, k, part=lambda ref: ref):
        p = self.place
        for when, block in p.ring(k):
            self.copies.start(
                when,
                lambda block=block: self.copy(
                    2,
                    block,
                    part(self.source(k, block)),
                    part(self.here(block, p.t)),
                    p.y,
                ),
            )

    def y_wait(self, k, part=lambda ref: ref):
        p = self.place
        for when, block in p.ring(k):
            arrive(when, part(self.here(block, 1 - p.t)), self.recv_sem(1, block), p.y)

    def relay(self, kind, k, sent, device):
        for when, block in self.place.ring(k):
            self.copies.start(
                when,
                lambda block=block: self.copy(kind, block, sent(block), sent(block), device),
            )

    def relay_wait(self, kind, k, got, device):
        for when, block in self.place.ring(k):
            arrive(when, got(block), self.recv_sem(kind - 1, block), device)


def forward_kernel(
    shards,
    starts_ref,
    wq_ref,
    wk_ref,
    wv_ref,
    wo_ref,
    wu_ref,
    wd_ref,
    head_bias_ref,
    up_bias_ref,
    tokens_ref,
    cot_ref,
    x_ref,
    cot_rows_ref,
    wqkv_ref,
    qkv_ref,
    heads_ref,
    rows_ref,
    total_ref,
    out_ref,
    up_ref,
    down_ref,
    up_bias_out,
    x_all,
    wg,
    qkv,
    mixed,
    wo_low,
    wu_low,
    wd_low,
    bias_all,
    send,
    recv,
    token_send,
    token_recv,
    local_sem,
):
    p = Place(shards)
    copies = Copies()
    half = wq_ref.shape[1]
    quarter = wg.shape[4]
    units = wu_ref.shape[1]
    seq_of = lambda cx, t: 2 * cx + t
    seq = seq_of(p.cx, p.t)
    seq_far = seq_of(1 - p.cx, p.t)
    far = 2 * (1 - p.cx) + p.h
    peer = p.c + 1 - 2 * p.h
    locals_ = []

    def local(source, target):
        copy = pltpu.make_async_copy(source, target, local_sem.at[len(locals_)])
        copy.start()
        locals_.append(copy)
        return copy

    def remote(index, source, target, device):
        return pltpu.make_async_remote_copy(
            src_ref=source,
            dst_ref=target,
            send_sem=token_send.at[index],
            recv_sem=token_recv.at[index],
            device_id=device,
            device_id_type=pl.DeviceIdType.MESH,
        )

    own_tokens = local(tokens_ref.at[seq], x_all.at[p.c])
    cot_own = local(cot_ref.at[seq], cot_rows_ref.at[p.cx])
    for third, ref in enumerate((wq_ref, wk_ref, wv_ref)):
        for hh in range(2):
            for xx in range(2):
                first = (2 * hh + xx) * quarter
                wg[p.t, p.s, hh, xx, :, third * half : (third + 1) * half] = low(
                    ref[first : first + quarter, :]
                )
    p.enter(False)
    copies.start(None, lambda: remote(0, tokens_ref.at[seq_far], x_all.at[p.c], p.x))
    copies.start(None, lambda: remote(1, tokens_ref.at[seq], x_all.at[p.c], p.core))
    sems = (send, recv)
    attn = Gather(p, copies, sems, 0, lambda b, t: wg.at[t, b, p.h], wg.at[p.t, p.s, p.h])
    attn.z_send(1)
    sub = lambda ref: ref.at[p.cx]
    attn.y_send(0, sub)
    copies.start(None, lambda: remote(2, head_bias_ref, bias_all.at[p.t], p.y))
    copies.start(None, lambda: remote(3, up_bias_ref, up_bias_out.at[p.t], p.y))
    bias_all[p.t] = head_bias_ref[...]
    up_bias_out[p.t] = up_bias_ref[...]

    for hh in range(2):
        rows = slice(hh * 2 * quarter, (hh + 1) * 2 * quarter)
        wo_low[hh] = low(wo_ref[rows, :])
        wu_low[hh] = low(wu_ref[rows, :])
        for xx in range(2):
            first = (2 * hh + xx) * quarter
            wd_low[hh, xx] = low(wd_ref[first : first + quarter, :])
    cols = lambda t, n: pl.ds(pl.multiple_of(t * n, 128), n)
    local(wo_low.at[p.h], out_ref.at[p.s, p.h, :, cols(p.t, half)])
    local(wu_low.at[p.h], up_ref.at[p.s, p.h, :, cols(p.t, units)])
    local(wd_low.at[p.h, p.cx], down_ref.at[p.s, p.h, p.cx, :, cols(p.t, units)])
    own_weights = locals_[-3:]
    out = Gather(
        p, copies, sems, 1, lambda b, t: out_ref.at[b, p.h, :, cols(t, half)], wo_low.at[p.h]
    )
    up = Gather(
        p, copies, sems, 2, lambda b, t: up_ref.at[b, p.h, :, cols(t, units)], wu_low.at[p.h]
    )
    down = Gather(
        p,
        copies,
        sems,
        3,
        lambda b, t: down_ref.at[b, p.h, p.cx, :, cols(t, units)],
        wd_low.at[p.h, p.cx],
    )

    far_block = x_all.at[far]
    arrive(None, far_block, token_recv.at[0], p.x)
    copies.start(None, lambda: remote(4, far_block, far_block, p.core))
    copies.start(None, lambda: remote(5, cot_ref.at[seq_far], cot_rows_ref.at[p.cx], p.x))

    last = shards - 1
    for k in range(1, shards):
        attn.z_wait(k)
        if k < last:
            attn.z_send(k + 1)
        attn.y_send(k, sub)
        if k == max(1, last - 1):
            out.z_send(1)
            up.z_send(1)
    out.y_send(0)
    up.y_send(0)
    for k in range(shards):
        attn.y_wait(k, sub)
        attn.relay(3, k, lambda b: wg.at[1 - p.t, b, p.h, p.cx], p.x)
    for k in range(shards):
        attn.relay_wait(3, k, lambda b: wg.at[1 - p.t, b, p.h, 1 - p.cx], p.x)
        attn.relay(4, k, lambda b: wg.at[1 - p.h, b, p.h], p.core)
    down.z_send(1)
    for k in range(1, shards):
        out.z_wait(k)
        if k < last:
            out.z_send(k + 1)
        out.y_send(k)
    up.z_wait(1)
    if last > 1:
        up.z_send(2)
    up.y_send(1)
    for k in range(shards):
        attn.relay_wait(4, k, lambda b: wg.at[p.h, b, 1 - p.h], p.core)
    own_tokens.wait()
    peer_far = 2 * (1 - p.cx) + 1 - p.h
    arrive(None, x_all.at[peer], token_recv.at[1], p.core)
    arrive(None, x_all.at[peer_far], token_recv.at[4], p.core)
    arrive(None, bias_all.at[1 - p.t], token_recv.at[2], p.y)
    local(x_all, x_ref)
    local(wg.at[p.h], wqkv_ref)

    weights = wg[p.h].reshape(shards * 4 * quarter, 3 * half)
    bias = bias_all[p.h]
    scale = 1.0 / math.sqrt(HEAD)
    pairs = half // PAIR

    def project(at, carry):
        result = matmul(x_all[at], weights)
        rows = pl.ds(pl.multiple_of(at * BLOCK, BLOCK), BLOCK)
        for j in range(3 * pairs):
            part = result[:, j * PAIR : (j + 1) * PAIR]
            if j < pairs:
                part = low(part + bias[0:1, j * PAIR : (j + 1) * PAIR])
                part = low(part.astype(jnp.float32) * scale)
            elif j < 2 * pairs:
                part = low(part)
            else:
                column = (j - 2 * pairs) * PAIR
                part = low(part + bias[1:2, column : column + PAIR])
            qkv[j, rows, :] = part
        return carry

    lax.fori_loop(0, x_all.shape[0], project, 0)
    local(qkv, qkv_ref)

    def on_the_way(stage):
        if stage == 0:
            up.z_wait(2)
            if last > 2:
                up.z_send(3)
            up.y_send(2)
            down.z_wait(1)
            if last > 1:
                down.z_send(2)
            down.y_send(0)
            down.y_send(1)
        if stage == 1:
            for k in range(3, shards):
                up.z_wait(k)
                if k < last:
                    up.z_send(k + 1)
                up.y_send(k)
            down.z_wait(2)
            if last > 2:
                down.z_send(3)
            down.y_send(2)
            for k in range(shards):
                out.y_wait(k)
                if k == 0:
                    for copy in own_weights:
                        copy.wait()
                out.relay(4, k, lambda b: out_ref.at[b, p.h], p.core)

    def attend(pair, carry):
        attend_pair(
            starts_ref,
            seq,
            qkv.at[pair],
            qkv.at[pairs + pair],
            qkv.at[2 * pairs + pair],
            mixed.at[pair],
            total_ref.at[pair],
        )
        return carry

    lax.fori_loop(0, 1, attend, 0)
    on_the_way(0)
    lax.fori_loop(1, 2, attend, 0)
    on_the_way(1)
    lax.fori_loop(2, pairs, attend, 0)

    def heads_of(late, hh, pair):
        column = pl.multiple_of(hh * half + pair * PAIR, PAIR)
        return rows_ref.at[late, :, pl.ds(column, PAIR)]

    for pair in range(pairs):
        for late in range(2):
            block = 2 * late + 1 - p.h
            index = 6 + 2 * pair + late
            rows = pl.ds(pl.multiple_of(block * BLOCK, BLOCK), BLOCK)
            copies.start(
                None,
                lambda index=index, pair=pair, rows=rows, late=late: remote(
                    index, mixed.at[pair, rows, :], heads_of(late, p.h, pair), p.core
                ),
            )
    for pair in range(pairs):
        local(mixed.at[pair], heads_ref.at[pair])
        for late in range(2):
            rows = pl.ds(pl.multiple_of((2 * late + p.h) * BLOCK, BLOCK), BLOCK)
            local(mixed.at[pair, rows, :], heads_of(late, p.h, pair))

    for k in range(3, shards):
        down.z_wait(k)
        if k < last:
            down.z_send(k + 1)
        down.y_send(k)
    for k in range(shards):
        up.y_wait(k)
        up.relay(4, k, lambda b: up_ref.at[b, p.h], p.core)
    for k in range(shards):
        down.y_wait(k)
        down.relay(3, k, lambda b: down_ref.at[b, p.h, p.cx], p.x)
    for k in range(shards):
        down.relay_wait(3, k, lambda b: down_ref.at[b, p.h, 1 - p.cx], p.x)
        down.relay(4, k, lambda b: down_ref.at[b, p.h], p.core)
    for k in range(shards):
        out.relay_wait(4, k, lambda b: out_ref.at[b, 1 - p.h], p.core)
        up.relay_wait(4, k, lambda b: up_ref.at[b, 1 - p.h], p.core)
        down.relay_wait(4, k, lambda b: down_ref.at[b, 1 - p.h], p.core)
    for pair in range(pairs):
        for late in range(2):
            index = 6 + 2 * pair + late
            arrive(None, heads_of(late, 1 - p.h, pair), token_recv.at[index], p.core)
    arrive(None, up_bias_out.at[1 - p.t], token_recv.at[3], p.y)
    arrive(None, cot_rows_ref.at[1 - p.cx], token_recv.at[5], p.x)
    copies.finish()
    for copy in locals_:
        if all(copy is not done for done in [own_tokens] + own_weights):
            copy.wait()


def forward(shards, starts, weights, head_bias, up_bias, tokens, cotangent):
    w_query, w_out, w_up = weights[0], weights[3], weights[4]
    seq_dev, block, width = tokens.shape
    rows_own, half = w_query.shape
    units = w_up.shape[1]
    quarter = rows_own // 4
    pairs = half // PAIR
    length = seq_dev * block
    low_type, full_type = jnp.bfloat16, jnp.float32
    shape = jax.ShapeDtypeStruct
    vmem = pl.BlockSpec(memory_space=pltpu.VMEM)
    anywhere = pl.BlockSpec(memory_space=pl.ANY)
    return pl.pallas_call(
        lambda *refs: forward_kernel(shards, *refs),
        in_specs=[pl.BlockSpec(memory_space=pltpu.SMEM)] + [vmem] * 8 + [anywhere] * 2,
        out_specs=[anywhere] * 6 + [vmem] + [anywhere] * 3 + [vmem],
        out_shape=[
            shape((seq_dev, block, width), low_type),
            shape((2, block, width), low_type),
            shape((shards, 2, 2, quarter, 3 * half), low_type),
            shape((3 * pairs, length, PAIR), low_type),
            shape((pairs, length, PAIR), low_type),
            shape((2, block, 2 * half), low_type),
            shape((pairs, 2, length), full_type),
            shape((shards, 2, 2 * quarter, 2 * half), low_type),
            shape((shards, 2, 2 * quarter, 2 * units), low_type),
            shape((shards, 2, 2, quarter, 2 * units), low_type),
            shape((2, 1, units), full_type),
        ],
        scratch_shapes=[
            pltpu.VMEM((seq_dev, block, width), low_type),
            pltpu.VMEM((2, shards, 2, 2, quarter, 3 * half), low_type),
            pltpu.VMEM((3 * pairs, length, PAIR), low_type),
            pltpu.VMEM((pairs, length, PAIR), low_type),
            pltpu.VMEM((2, 2 * quarter, half), low_type),
            pltpu.VMEM((2, 2 * quarter, units), low_type),
            pltpu.VMEM((2, 2, quarter, units), low_type),
            pltpu.VMEM((2, 2, half), full_type),
            pltpu.SemaphoreType.DMA((4, 5, shards)),
            pltpu.SemaphoreType.DMA((4, 4, shards)),
            pltpu.SemaphoreType.DMA((6 + 2 * pairs,)),
            pltpu.SemaphoreType.DMA((6 + 2 * pairs,)),
            pltpu.SemaphoreType.DMA((8 + 3 * pairs,)),
        ],
        compiler_params=pltpu.CompilerParams(
            collective_id=1, has_side_effects=True, vmem_limit_bytes=60 * 1024 * 1024
        ),
    )(starts, *weights, head_bias, up_bias, tokens, cotangent)


def attend_back_pair(
    starts_ref, seq, q_ref, k_ref, v_ref, mixed_ref, grad_ref, total_ref, dq_ref, dk_ref, dv_ref,
    sums_ref, dk_acc, dv_acc
):
    length = q_ref.shape[0]
    blocks = length // BLOCK
    query_sum = jnp.zeros((1, PAIR), jnp.float32)
    for at in range(blocks):
        rows = slice(at * BLOCK, (at + 1) * BLOCK)
        reach = min(blocks, at + 2)
        span = slice(0, reach * BLOCK)
        queries = two_heads(q_ref[rows, :])
        grads = two_heads(grad_ref[rows, :])
        along = grad_ref[rows, :].astype(jnp.float32) * mixed_ref[rows, :].astype(jnp.float32)
        along = jnp.transpose(along)
        inner = jnp.concatenate(
            [
                jnp.sum(along[:HEAD], axis=0, keepdims=True),
                jnp.sum(along[HEAD:], axis=0, keepdims=True),
            ],
            axis=1,
        )
        total = jnp.concatenate([total_ref[0:1, rows], total_ref[1:2, rows]], axis=1)
        scores = []
        for key_at in range(reach):
            part = over_cols(k_ref[key_at * BLOCK : (key_at + 1) * BLOCK, :], queries)
            if key_at >= at:
                seen = edge_mask(starts_ref, seq, key_at * BLOCK, at * BLOCK, True)
                seen = jnp.concatenate([seen, seen], axis=1)
                part = jnp.where(seen, part, masked_score)
            scores.append(part)
        probs = jnp.exp(jnp.concatenate(scores, axis=0) - total)
        grad_probs = over_cols(v_ref[span, :], grads)
        grad_scores = low(probs * (grad_probs - inner))
        dv = matmul(low(probs), grads)
        dk = matmul(grad_scores, queries)
        if at == 0:
            dv_acc[span, :] = dv
            dk_acc[span, :] = dk
        elif at + 1 == blocks:
            dv_acc[span, :] += dv
            dk_acc[span, :] += dk
        else:
            old = slice(0, (reach - 1) * BLOCK)
            fresh = slice((reach - 1) * BLOCK, reach * BLOCK)
            dv_acc[old, :] += dv[old, :]
            dk_acc[old, :] += dk[old, :]
            dv_acc[fresh, :] = dv[fresh, :]
            dk_acc[fresh, :] = dk[fresh, :]
        dq = join_heads(over_rows(grad_scores, k_ref[span, :])) * (1.0 / math.sqrt(HEAD))
        query_sum += jnp.sum(dq, axis=0, keepdims=True)
        dq_ref[rows, :] = low(dq)
    dk_ref[...] = low(dk_acc[...])
    dv_ref[...] = low(dv_acc[...])
    sums_ref[0:1, :] = query_sum
    sums_ref[1:2, :] = jnp.sum(dv_acc[...], axis=0, keepdims=True)


class Links:
    def __init__(self, place, send, recv, copies):
        self.place, self.send, self.recv, self.copies = place, send, recv, copies
        self.made = 0

    def __call__(self, source, target, device):
        index = self.made
        ref = lambda of: of() if callable(of) else of
        self.made += 1
        make = lambda: pltpu.make_async_remote_copy(
            src_ref=ref(source),
            dst_ref=ref(target),
            send_sem=self.send.at[index],
            recv_sem=self.recv.at[index],
            device_id=device,
            device_id_type=pl.DeviceIdType.MESH,
        )
        self.copies.start(None, make)
        return lambda region: arrive(None, region, self.recv.at[index], device)

    def around(self, source, target):
        p = self.place
        waits = []
        for r, (there, _) in enumerate(p.steps):
            wait = self(
                lambda there=there: source(there), lambda r=r: target(r), (there, p.c, p.t)
            )
            waits.append(lambda wait=wait, r=r: wait(target(r)))
        return waits


def wide(ref):
    return ref[...].astype(jnp.float32)


def add_blocks(target, other, count):
    def body(i, carry):
        target[i] = low(wide(target.at[i]) + wide(other.at[i]))
        return carry

    lax.fori_loop(0, count, body, 0)


def backward_kernel(
    shards,
    starts_ref,
    down_ref,
    up_ref,
    out_ref,
    qkv_ref,
    wqkv_ref,
    x_ref,
    heads_ref,
    total_ref,
    mixed_grad_ref,
    sum_one_ref,
    final_ref,
    early_ref,
    act_out,
    input_out,
    down_out,
    up_out,
    out_out,
    qkv_out,
    early_out,
    head_out,
    qkv,
    wqkv,
    x_t,
    x_all,
    heads,
    grad_heads,
    sum_one,
    dqkv,
    dk_acc,
    dv_acc,
    sums,
    input_acc,
    part_sent,
    part_got,
    input_rows,
    down_own,
    down_core,
    down_x,
    down_y,
    down_z,
    down_fin,
    up_own,
    up_core,
    up_z,
    up_y,
    up_x,
    up_fin,
    out_own,
    out_core,
    out_y,
    out_z,
    out_x,
    out_fin,
    pair_sent,
    pair_both,
    pair_x,
    pair_y,
    pair_z,
    pair_fin,
    early_sums,
    early_got,
    early_z,
    head_sums,
    head_got,
    head_z,
    send,
    recv,
    local_sem,
):
    p = Place(shards)
    copies = Copies()
    link = Links(p, send, recv, copies)
    h, cx, t, s = p.h, p.cx, p.t, p.s
    nh, nx, nt = p.nh, p.nx, p.nt
    pairs = heads.shape[0]
    half = pairs * PAIR
    block = input_rows.shape[1]
    quarter = down_own.shape[3]
    units = down_own.shape[4]
    length = x_all.shape[0]
    seq_of = lambda cx_, t_: 2 * cx_ + t_
    near, far = seq_of(cx, t), seq_of(1 - cx, t)
    locals_ = []

    def local(source, target):
        copy = pltpu.make_async_copy(source, target, local_sem.at[len(locals_)])
        copy.start()
        locals_.append(copy)
        return copy

    x_here = local(x_ref, x_all)
    others = [local(qkv_ref, qkv), local(wqkv_ref, wqkv), local(heads_ref, heads)]
    sum_here = local(sum_one_ref, sum_one)
    for tt in range(2):
        one = pl.ds(tt * units, units)
        local(down_ref.at[:, h, :, :, one], down_own.at[tt])
        local(up_ref.at[:, h, :, one], up_own.at[tt])
        local(out_ref.at[:, h, :, pl.ds(tt * half, half)], out_own.at[tt])
    mine = locals_[5:11]
    for pair in range(pairs):
        for late in range(2):
            rows = pl.ds(pl.multiple_of((2 * late + h) * block, block), block)
            column = pl.multiple_of(h * half + pair * PAIR, PAIR)
            others.append(
                local(
                    mixed_grad_ref.at[late, :, pl.ds(column, PAIR)], grad_heads.at[pair, rows, :]
                )
            )

    p.enter(True)

    grad_waits = []
    for pair in range(pairs):
        for late in range(2):
            there = pl.ds(pl.multiple_of((2 * late + h) * block, block), block)
            here = pl.ds(pl.multiple_of((2 * late + 1 - h) * block, block), block)
            column = pl.multiple_of((1 - h) * half + pair * PAIR, PAIR)
            wait = link(
                mixed_grad_ref.at[late, :, pl.ds(column, PAIR)],
                grad_heads.at[pair, there, :],
                p.core,
            )
            grad_waits.append(
                lambda wait=wait, pair=pair, here=here: wait(grad_heads.at[pair, here, :])
            )

    def deliver(source, target):
        local(source.at[cx], target.at[near])
        wait_y = link(source.at[cx], target.at[near], p.y)
        wait_x = link(source.at[nx], target.at[near], p.x)
        yield
        wait_x(target.at[far])
        wait_far = link(lambda: target.at[far], lambda: target.at[far], p.y)
        yield
        wait_y(target.at[seq_of(cx, nt)])
        wait_far(target.at[seq_of(nx, nt)])
        yield

    def reduce_down():
        waits = [
            link(
                down_ref.at[:, nh, :, :, pl.ds(tt * units, units)], down_core.at[tt], p.core
            )
            for tt in range(2)
        ]
        yield
        for tt in range(2):
            mine[3 * tt].wait()
            waits[tt](down_core.at[tt])
            add_blocks(down_own.at[tt], down_core.at[tt], shards)
        wait = link(down_own.at[:, :, nx], down_x, p.x)
        yield
        wait(down_x)

        def body(i, carry):
            for tt in range(2):
                down_own[tt, i, cx] = low(wide(down_own.at[tt, i, cx]) + wide(down_x.at[tt, i]))
            return carry

        lax.fori_loop(0, shards, body, 0)
        wait = link(lambda: down_own.at[nt, :, cx], down_y, p.y)
        yield
        wait(down_y)

        def body_y(i, carry):
            down_own[t, i, cx] = low(wide(down_own.at[t, i, cx]) + wide(down_y.at[i]))
            return carry

        lax.fori_loop(0, shards, body_y, 0)
        waits = link.around(lambda b: down_own.at[t, b, cx], lambda r: down_z.at[r])
        yield
        total = wide(down_own.at[t, s, cx])
        for r, wait in enumerate(waits):
            wait()
            total = total + wide(down_z.at[r])
        down_fin[h, cx] = low(total)
        wait = link(down_fin.at[h, cx], down_fin.at[h, cx], p.x)
        yield
        wait(down_fin.at[h, nx])
        wait = link(down_fin.at[h], down_fin.at[h], p.core)
        yield
        wait(down_fin.at[nh])
        local(down_fin, down_out)
        yield

    def reduce_up():
        waits = [
            link(up_ref.at[:, nh, :, pl.ds(tt * units, units)], up_core.at[tt], p.core)
            for tt in range(2)
        ]
        yield
        for tt in range(2):
            mine[3 * tt + 1].wait()
            waits[tt](up_core.at[tt])
            add_blocks(up_own.at[tt], up_core.at[tt], shards)
        waits = link.around(lambda b: up_own.at[:, b], lambda r: up_z.at[r])
        yield
        for wait in waits:
            wait()
        for tt in range(2):
            total = wide(up_own.at[tt, s])
            for r in range(shards - 1):
                total = total + wide(up_z.at[r, tt])
            up_own[tt, s] = low(total)
        wait = link(up_own.at[nt, s], up_y, p.y)
        yield
        wait(up_y)
        up_own[t, s] = low(wide(up_own.at[t, s]) + wide(up_y))
        wait = link(up_own.at[t, s], up_x, p.x)
        yield
        wait(up_x)
        up_fin[h] = low(wide(up_own.at[t, s]) + wide(up_x))
        wait = link(up_fin.at[h], up_fin.at[h], p.core)
        yield
        wait(up_fin.at[nh])
        local(up_fin, up_out)
        yield

    def reduce_out():
        waits = [
            link(out_ref.at[:, nh, :, pl.ds(tt * half, half)], out_core.at[tt], p.core)
            for tt in range(2)
        ]
        yield
        for tt in range(2):
            mine[3 * tt + 2].wait()
            waits[tt](out_core.at[tt])
            add_blocks(out_own.at[tt], out_core.at[tt], shards)
        wait = link(out_own.at[nt], out_y, p.y)
        yield
        wait(out_y)
        add_blocks(out_own.at[t], out_y, shards)
        waits = link.around(lambda b: out_own.at[t, b], lambda r: out_z.at[r])
        yield
        total = wide(out_own.at[t, s])
        for r, wait in enumerate(waits):
            wait()
            total = total + wide(out_z.at[r])
        out_own[t, s] = low(total)
        wait = link(out_own.at[t, s], out_x, p.x)
        yield
        wait(out_x)
        out_fin[h] = low(wide(out_own.at[t, s]) + wide(out_x))
        wait = link(out_fin.at[h], out_fin.at[h], p.core)
        yield
        wait(out_fin.at[nh])
        local(out_fin, out_out)
        yield

    def reduce_pair(pair):
        sent, whole = lambda: pair_sent.at[pair], lambda: pair_both.at[pair]
        wait = link(lambda: sent().at[nh], lambda: whole().at[h], p.core)
        pair_both[pair, h] = pair_sent[pair, h]
        yield
        wait(whole().at[nh])
        wait = link(lambda: whole().at[:, :, nx], lambda: pair_x.at[pair], p.x)
        yield
        wait(pair_x.at[pair])

        def body(i, carry):
            for tt in range(2):
                pair_both[pair, tt, i, cx] = low(wide(whole().at[tt, i, cx]) + wide(pair_x.at[pair, tt, i]))
            return carry

        lax.fori_loop(0, shards, body, 0)
        wait = link(lambda: whole().at[nt, :, cx], lambda: pair_y.at[pair], p.y)
        yield
        wait(pair_y.at[pair])

        def body_y(i, carry):
            pair_both[pair, t, i, cx] = low(wide(whole().at[t, i, cx]) + wide(pair_y.at[pair, i]))
            return carry

        lax.fori_loop(0, shards, body_y, 0)
        waits = link.around(lambda b: whole().at[t, b, cx], lambda r: pair_z.at[pair, r])
        yield
        total = wide(whole().at[t, s, cx])
        for r, wait in enumerate(waits):
            wait()
            total = total + wide(pair_z.at[pair, r])
        fin = pair_fin.at[pair]
        fin[h, cx] = low(total)
        wait = link(fin.at[h, cx], fin.at[h, cx], p.x)
        yield
        wait(fin.at[h, nx])
        wait = link(fin.at[h], fin.at[h], p.core)
        yield
        wait(fin.at[nh])
        local(fin, qkv_out.at[pair])
        yield

    def reduce_vector(first, got, steps, around, result):
        wait = link(lambda: first, lambda: got.at[0], p.core)
        yield
        wait(got.at[0])
        steps[0] = first[...] + got[0]
        wait = link(lambda: steps.at[0], lambda: got.at[1], p.x)
        yield
        wait(got.at[1])
        steps[1] = steps[0] + got[1]
        wait = link(lambda: steps.at[1], lambda: got.at[2], p.y)
        yield
        wait(got.at[2])
        around[s] = steps[1] + got[2]
        waits = []
        for there, source in p.steps:
            waits.append((link(around.at[s], around.at[s], (there, p.c, t)), source))
        yield
        for wait, source in waits:
            wait(around.at[source])
        total = around[0]
        for at in range(1, shards):
            total = total + around[at]
        result[...] = total
        yield

    act = deliver(final_ref, act_out)
    down, up, out = reduce_down(), reduce_up(), reduce_out()
    early = reduce_vector(early_ref, early_got, early_sums, early_z, early_out)

    def step(*names):
        for chain in names:
            next(chain)

    step(down, up, out, early, act)

    x_here.wait()

    for i in range(length // block):
        rows = slice(i * block, (i + 1) * block)
        x_t[:, rows] = jnp.transpose(x_all[rows, :])
    step(down, up, out, early)
    for copy in others:
        copy.wait()
    for wait in grad_waits:
        wait()

    def pair_grads(pair):
        values = jnp.concatenate([dqkv[j * pairs + pair] for j in range(3)], axis=1)
        for i in range(shards):
            terms = low(matmul(x_t[i * 4 * quarter : (i + 1) * 4 * quarter, :], values))
            for hh in range(2):
                for xx in range(2):
                    first = (2 * hh + xx) * quarter
                    pair_sent[pair, hh, i, xx] = terms[first : first + quarter]

    def pair_inputs(pair):
        weights = jnp.concatenate(
            [
                wqkv[:, j * half + pair * PAIR : j * half + (pair + 1) * PAIR]
                for j in range(3)
            ],
            axis=1,
        )

        def body(i, carry):
            rows = pl.ds(pl.multiple_of(i * block, block), block)
            terms = over_cols(
                jnp.concatenate([dqkv[j * pairs + pair, rows, :] for j in range(3)], axis=1),
                weights,
            )
            if pair == 0:
                input_acc[i] = terms
            else:
                input_acc[i] += terms
            return carry

        lax.fori_loop(0, length // block, body, 0)

    chain_of = [None] * pairs

    def attend(pair, carry):
        attend_back_pair(
            starts_ref,
            near,
            qkv.at[pair],
            qkv.at[pairs + pair],
            qkv.at[2 * pairs + pair],
            heads.at[pair],
            grad_heads.at[pair],
            total_ref.at[pair],
            dqkv.at[pair],
            dqkv.at[pairs + pair],
            dqkv.at[2 * pairs + pair],
            sums.at[pair],
            dk_acc,
            dv_acc,
        )
        for at in range(pairs):

            @pl.when(pair == at)
            def _():
                pair_inputs(at)
                if at == pairs - 1:
                    exchange_inputs()
                pair_grads(at)
                between(at)

        return carry

    part_waits = []

    def exchange_inputs():
        for late in range(2):
            part_sent[late] = low(input_acc[2 * late + 1 - h])
        part_waits.append(link(part_sent, part_got, p.core))

    def between(at):
        chain_of[at] = reduce_pair(at)
        next(chain_of[at])
        if at == 0:
            step(early, out)
        if at == 1:
            step(chain_of[0], down, early, act)

    lax.fori_loop(0, pairs, attend, 0)
    first, second, third = chain_of
    sum_here.wait()
    part_waits[0](part_got)
    for late in range(2):
        input_rows[late] = low(
            sum_one[late] + input_acc[2 * late + h] + wide(part_got.at[late])
        )
    inputs = deliver(input_rows, input_out)
    step(inputs)
    head_first = head_sums.at[2]
    head_first[...] = jnp.zeros(head_first.shape, jnp.float32)
    for row in range(2 * pairs):
        kind = row // pairs
        head_first[pl.ds(h * 2 * pairs + row, 1), :] = sums[row % pairs, kind : kind + 1, :]
    vector = reduce_vector(head_first, head_got, head_sums, head_z, head_out)
    step(vector, third, second, out, vector)
    step(down, first, early, second, third, vector)
    step(inputs, first, out, second, vector)
    step(down, first, third, second, out, up)
    step(down, first, second, third, up)
    step(down, first, second, third, up)
    step(third, vector, act, inputs, up)
    copies.finish()
    for copy in locals_:
        if all(copy is not done for done in [x_here, sum_here] + mine + others):
            copy.wait()


def backward(
    shards, starts, down, up, out, qkv, wqkv, x, heads, totals, mixed_grad, sum_one, final, early
):
    seq_dev, block, width = x.shape
    length = seq_dev * block
    pairs = heads.shape[0]
    half = pairs * PAIR
    units = down.shape[1] // 2
    quarter = width // shards // 4
    low_type, full_type = jnp.bfloat16, jnp.float32
    shape = jax.ShapeDtypeStruct
    vmem = pl.BlockSpec(memory_space=pltpu.VMEM)
    anywhere = pl.BlockSpec(memory_space=pl.ANY)
    scratch = lambda *dims, kind=low_type: pltpu.VMEM(dims, kind)
    around = shards - 1
    early = early.reshape(-1, PAIR)
    copies = 6 + 2 * 6 + 3 + 24 + 8 * around + pairs * (5 + around)
    return pl.pallas_call(
        lambda *refs: backward_kernel(shards, *refs),
        in_specs=[pl.BlockSpec(memory_space=pltpu.SMEM)]
        + [anywhere] * 7
        + [vmem]
        + [anywhere] * 2
        + [vmem] * 2,
        out_specs=[anywhere] * 6 + [vmem] * 2,
        out_shape=[
            shape((seq_dev, block, width), low_type),
            shape((seq_dev, block, width), low_type),
            shape((2, 2, quarter, units), low_type),
            shape((2, 2 * quarter, units), low_type),
            shape((2, 2 * quarter, half), low_type),
            shape((pairs, 2, 2, quarter, 3 * PAIR), low_type),
            shape(early.shape, full_type),
            shape((4 * pairs, PAIR), full_type),
        ],
        scratch_shapes=[
            scratch(3 * pairs, length, PAIR),
            scratch(width, 3 * half),
            scratch(width, length),
            scratch(length, width),
            scratch(pairs, length, PAIR),
            scratch(pairs, length, PAIR),
            scratch(2, block, width, kind=full_type),
            scratch(3 * pairs, length, PAIR),
            scratch(length, PAIR, kind=full_type),
            scratch(length, PAIR, kind=full_type),
            scratch(pairs, 2, PAIR, kind=full_type),
            scratch(seq_dev, block, width, kind=full_type),
            scratch(2, block, width),
            scratch(2, block, width),
            scratch(2, block, width),
            scratch(2, shards, 2, quarter, units),
            scratch(2, shards, 2, quarter, units),
            scratch(2, shards, quarter, units),
            scratch(shards, quarter, units),
            scratch(around, quarter, units),
            scratch(2, 2, quarter, units),
            scratch(2, shards, 2 * quarter, units),
            scratch(2, shards, 2 * quarter, units),
            scratch(around, 2, 2 * quarter, units),
            scratch(2 * quarter, units),
            scratch(2 * quarter, units),
            scratch(2, 2 * quarter, units),
            scratch(2, shards, 2 * quarter, half),
            scratch(2, shards, 2 * quarter, half),
            scratch(shards, 2 * quarter, half),
            scratch(around, 2 * quarter, half),
            scratch(2 * quarter, half),
            scratch(2, 2 * quarter, half),
            scratch(pairs, 2, shards, 2, quarter, 3 * PAIR),
            scratch(pairs, 2, shards, 2, quarter, 3 * PAIR),
            scratch(pairs, 2, shards, quarter, 3 * PAIR),
            scratch(pairs, shards, quarter, 3 * PAIR),
            scratch(pairs, around, quarter, 3 * PAIR),
            scratch(pairs, 2, 2, quarter, 3 * PAIR),
            scratch(2, *early.shape, kind=full_type),
            scratch(3, *early.shape, kind=full_type),
            scratch(shards, *early.shape, kind=full_type),
            scratch(3, 4 * pairs, PAIR, kind=full_type),
            scratch(3, 4 * pairs, PAIR, kind=full_type),
            scratch(shards, 4 * pairs, PAIR, kind=full_type),
            pltpu.SemaphoreType.DMA((copies,)),
            pltpu.SemaphoreType.DMA((copies,)),
            pltpu.SemaphoreType.DMA((24 + 4 * pairs,)),
        ],
        compiler_params=pltpu.CompilerParams(
            collective_id=2, has_side_effects=True, vmem_limit_bytes=62 * 1024 * 1024
        ),
    )(
        starts,
        down.reshape(shards, 2, 2, quarter, 2 * units),
        up.reshape(shards, 2, 2 * quarter, 2 * units),
        out.reshape(shards, 2, 2 * quarter, 2 * half),
        qkv,
        wqkv.reshape(width, 3 * half),
        x.reshape(length, width),
        heads,
        totals,
        mixed_grad.reshape(2, block, width),
        sum_one.reshape(2, block, width),
        final.reshape(2, block, width),
        early,
    )


def make_local(shards, ctxs, tps):
    def pick(flag, former, latter):
        return jnp.where(flag, former, latter)

    def local(
        tokens,
        starts,
        w_query,
        w_key,
        w_value,
        w_out,
        w_up,
        w_down,
        head_bias,
        up_bias,
        out_biases,
        norm_gains,
        norm_shifts,
        cotangent,
    ):
        seq_dev, block, width = tokens.shape
        assert ctxs == 4 and tps == 2 and seq_dev == 4 and block == BLOCK
        rows_own = w_query.shape[0]
        half_width = w_query.shape[1]
        ctx = lax.axis_index("ctx")
        t = lax.axis_index("tp")
        core = lax.rem(ctx, 2)
        cx = lax.div(ctx, 2)
        seq_of = lambda cx_, t_: 2 * cx_ + t_
        seq = seq_of(cx, t)
        other_x = 1 - cx

        def take(array, index):
            return lax.dynamic_index_in_dim(array, index, 0, False)

        (
            x_blocks,
            cot_rows,
            wqkv,
            qkv,
            mixed_heads,
            mixed_rows,
            totals,
            out_full,
            up_full,
            down_full,
            up_bias_full,
        ) = forward(
            shards,
            starts,
            (w_query, w_key, w_value, w_out, w_up, w_down),
            head_bias,
            up_bias.reshape(1, -1),
            tokens,
            cotangent,
        )
        x_pairs_ = x_blocks.reshape(2, 2, block, width)
        rows_here = pick(core == 0, x_pairs_[:, 0], x_pairs_[:, 1]).reshape(2 * block, width)
        cot_here = cot_rows.reshape(2 * block, width)
        out_full = out_full.reshape(width, -1)
        up_full = up_full.reshape(width, -1)
        down_full = down_full.reshape(width, -1)
        up_bias_full = up_bias_full.reshape(-1)
        mixed = mixed_rows.reshape(2 * block, width)

        attn_out = over_cols(mixed, out_full) + out_biases[0]
        first_scaled, first_rstd = normalize(rows_here.astype(jnp.float32) + attn_out)
        first_norm = first_scaled * norm_gains[0] + norm_shifts[0]
        first_low = low(first_norm)
        hidden = matmul(first_low, up_full) + up_bias_full
        gauss = 0.5 * (1.0 + lax.erf(hidden * (1.0 / math.sqrt(2.0))))
        active = low(hidden * gauss)
        slope = low(
            gauss + hidden * jnp.exp(-0.5 * hidden * hidden) * (1.0 / math.sqrt(2.0 * math.pi))
        )
        ffn_out = over_cols(active, down_full) + out_biases[1]
        second_scaled, second_rstd = normalize(first_norm + ffn_out)
        final_low = low(second_scaled * norm_gains[1] + norm_shifts[1])

        grad_final = cot_here.astype(jnp.float32)
        gain_two = jnp.sum(grad_final * second_scaled, axis=0)
        shift_two = jnp.sum(grad_final, axis=0)
        grad_second = norm_back(grad_final, second_scaled, second_rstd, norm_gains[1])
        bias_two = jnp.sum(grad_second, axis=0)
        grad_ffn = low(grad_second)
        grad_active = matmul(grad_ffn, down_full)
        grad_hidden = grad_active * slope.astype(jnp.float32)
        up_bias_grad = jnp.sum(grad_hidden, axis=0)
        grad_hidden_low = low(grad_hidden)
        grad_first = grad_second + over_cols(grad_hidden_low, up_full)
        gain_one = jnp.sum(grad_first * first_scaled, axis=0)
        shift_one = jnp.sum(grad_first, axis=0)
        grad_sum_one = norm_back(grad_first, first_scaled, first_rstd, norm_gains[0])
        bias_one = jnp.sum(grad_sum_one, axis=0)
        grad_attn = low(grad_sum_one)
        grad_mixed = low(matmul(grad_attn, out_full))
        grad_down_local = low(over_rows(grad_ffn, active))
        grad_up_local = low(over_rows(first_low, grad_hidden_low))
        grad_out_local = low(over_rows(grad_attn, mixed))

        early = jnp.concatenate(
            [up_bias_grad, bias_one, bias_two, gain_one, gain_two, shift_one, shift_two]
        )
        (
            activations,
            input_grad,
            grad_down,
            grad_up,
            grad_out,
            grad_pairs,
            early,
            head_sums,
        ) = backward(
            shards,
            starts,
            grad_down_local,
            grad_up_local,
            grad_out_local,
            qkv,
            wqkv,
            x_blocks,
            mixed_heads,
            totals,
            grad_mixed,
            grad_sum_one,
            final_low,
            early,
        )
        whole = lambda grad: grad.reshape(rows_own, -1).astype(jnp.float32)
        pairs = half_width // PAIR
        grad_pairs = grad_pairs.reshape(pairs, rows_own, 3, PAIR).transpose(2, 1, 0, 3)
        grad_pairs = grad_pairs.reshape(3, rows_own, half_width).astype(jnp.float32)
        units = up_bias_grad.shape[0]
        early = early.reshape(-1)
        up_sum = lax.dynamic_index_in_dim(early[:units].reshape(2, units // 2), t, 0, False)
        vectors = early[units:].reshape(3, 2, width)
        head_sums = lax.dynamic_index_in_dim(
            head_sums.reshape(2, 2, half_width), t, 0, False
        )
        return (
            activations,
            input_grad.astype(jnp.float32),
            grad_pairs[0],
            grad_pairs[1],
            grad_pairs[2],
            whole(grad_out),
            whole(grad_up),
            whole(grad_down),
            head_sums,
            up_sum,
            vectors[0],
            vectors[1],
            vectors[2],
        )

    return local


def solution(mesh):
    sizes = [mesh.shape[name] for name in AXES]
    return jax.shard_map(
        make_local(*sizes),
        mesh=mesh,
        in_specs=(
            P("shard", "ctx", None),
            P("shard", None),
            P("shard", "tp"),
            P("shard", "tp"),
            P("shard", "tp"),
            P("shard", "tp"),
            P("shard", "tp"),
            P("shard", "tp"),
            P(None, "tp"),
            P("tp"),
            P(),
            P(),
            P(),
            P("shard", "ctx", None),
        ),
        out_specs=(
            P("shard", "ctx", None),
            P("shard", "ctx", None),
            P("shard", "tp"),
            P("shard", "tp"),
            P("shard", "tp"),
            P("shard", "tp"),
            P("shard", "tp"),
            P("shard", "tp"),
            P(None, "tp"),
            P("tp"),
            P(),
            P(),
            P(),
        ),
        check_vma=False,
    )
```

```python
import math

import jax
import jax.numpy as jnp
from jax import lax
from jax.experimental import pallas as pl
from jax.experimental.pallas import tpu as pltpu
from jax.sharding import PartitionSpec as P

HEAD = 64
PIECE = 256
BLOCK = 256
PAIR = 128

norm_eps = 1e-05
masked_score = -1e30
AXES = ("shard", "ctx", "tp")


def matmul(former, latter):
    return jnp.dot(former, latter, preferred_element_type=jnp.float32)


def over_rows(former, latter):
    return lax.dot_general(
        former, latter, (((0,), (0,)), ((), ())), preferred_element_type=jnp.float32
    )


def over_cols(former, latter):
    return lax.dot_general(
        former, latter, (((1,), (1,)), ((), ())), preferred_element_type=jnp.float32
    )


def low(values):
    return values.astype(jnp.bfloat16)


def normalize(values):
    centre = jnp.mean(values, axis=-1, keepdims=True)
    centred = values - centre
    spread = jnp.mean(centred * centred, axis=-1, keepdims=True)
    scaling = lax.rsqrt(spread + norm_eps)
    return (centred * scaling, scaling)


def norm_back(grad_out, scaled, scaling, gain_row):
    grad_scaled = grad_out * gain_row
    mean_grad = jnp.mean(grad_scaled, axis=-1, keepdims=True)
    mean_along = jnp.mean(grad_scaled * scaled, axis=-1, keepdims=True)
    return scaling * (grad_scaled - mean_grad - scaled * mean_along)


def edge_mask(starts_ref, seq, key_first, query_first, keys_first):
    key_shape = (BLOCK, 1) if keys_first else (1, BLOCK)
    query_shape = (1, BLOCK) if keys_first else (BLOCK, 1)
    key_at = key_first + lax.broadcasted_iota(jnp.int32, key_shape, 0 if keys_first else 1)
    query_at = query_first + lax.broadcasted_iota(jnp.int32, query_shape, 1 if keys_first else 0)
    seen = key_at <= query_at
    for piece in range(2):
        start = starts_ref[seq, piece]
        key_in = (key_at >= start) & (key_at < start + PIECE)
        query_in = (query_at >= start) & (query_at < start + PIECE)
        seen = seen | (key_in & query_in)
    return seen


def two_heads(rows):
    lane = lax.broadcasted_iota(jnp.int32, rows.shape, 1)
    zero = jnp.zeros_like(rows)
    return jnp.concatenate(
        [jnp.where(lane < HEAD, rows, zero), jnp.where(lane >= HEAD, rows, zero)], axis=0
    )


def join_heads(rows):
    half = rows.shape[0] // 2
    lane = lax.broadcasted_iota(jnp.int32, (half, rows.shape[1]), 1)
    return jnp.where(lane < HEAD, rows[:half], rows[half:])


def attend_pair(starts_ref, seq, q_ref, k_ref, v_ref, mixed_ref, total_ref):
    length = q_ref.shape[0]
    blocks = length // BLOCK
    for at in range(blocks):
        rows = slice(at * BLOCK, (at + 1) * BLOCK)
        reach = min(blocks, at + 2)
        queries = two_heads(q_ref[rows, :])
        scores = []
        for key_at in range(reach):
            part = over_cols(queries, k_ref[key_at * BLOCK : (key_at + 1) * BLOCK, :])
            if key_at >= at:
                seen = edge_mask(starts_ref, seq, key_at * BLOCK, at * BLOCK, False)
                seen = jnp.concatenate([seen, seen], axis=0)
                part = jnp.where(seen, part, masked_score)
            scores.append(part)
        scores = jnp.concatenate(scores, axis=1)
        top = jnp.max(scores, axis=1, keepdims=True)
        raised = jnp.exp(scores - top)
        total = jnp.sum(raised, axis=1, keepdims=True)
        mixed = matmul(low(raised), v_ref[: reach * BLOCK, :]) / total
        mixed_ref[rows, :] = low(join_heads(mixed))
        wide = jnp.broadcast_to(top + jnp.log(total), (2 * BLOCK, PAIR))
        row = jnp.transpose(wide)[0:1, :]
        total_ref[0:1, rows] = row[:, :BLOCK]
        total_ref[1:2, rows] = row[:, BLOCK:]


class Copies:
    def __init__(self):
        self.sent = []

    def start(self, when, make):
        self.sent.append((when, make))
        if when is None:
            make().start()
        else:
            pl.when(when)(lambda: make().start())

    def finish(self):
        for when, make in self.sent:
            if when is None:
                make().wait_send()
            else:
                pl.when(when)(lambda make=make: make().wait_send())


def both(former, latter):
    if former is None:
        return latter
    return former if latter is None else former & latter


def arrive(when, region, sem, device):
    def wait():
        pltpu.make_async_remote_copy(
            src_ref=region,
            dst_ref=region,
            send_sem=sem,
            recv_sem=sem,
            device_id=device,
            device_id_type=pl.DeviceIdType.MESH,
        ).wait_recv()

    if when is None:
        wait()
    else:
        pl.when(when)(wait)


class Place:
    def __init__(self, shards):
        self.shards = shards
        self.s = lax.axis_index("shard")
        self.c = lax.axis_index("ctx")
        self.t = lax.axis_index("tp")
        self.h = lax.rem(self.c, 2)
        self.cx = lax.div(self.c, 2)
        self.core = (self.s, self.c + 1 - 2 * self.h, self.t)
        self.x = (self.s, self.c + 2 - 4 * self.cx, self.t)
        self.y = (self.s, self.c, 1 - self.t)
        self.up = (self.s + 1, self.c, self.t)
        self.down = (self.s - 1, self.c, self.t)
        self.nh, self.nx, self.nt = 1 - self.h, 1 - self.cx, 1 - self.t
        self.steps = [
            (lax.rem(self.s + r, shards), lax.rem(self.s + shards - r, shards))
            for r in range(1, shards)
        ]
        self.has_up = self.s < shards - 1
        self.has_down = self.s > 0

    def enter(self, whole_line):
        barrier = pltpu.get_barrier_semaphore()

        def greet(device):
            pl.semaphore_signal(
                barrier, inc=1, device_id=device, device_id_type=pl.DeviceIdType.MESH
            )

        for device in (self.core, self.x, self.y):
            greet(device)
        if whole_line:
            for there, _ in self.steps:
                greet((there, self.c, self.t))
            pl.semaphore_wait(barrier, 3 + len(self.steps))
            return
        pl.when(self.has_up)(lambda: greet(self.up))
        pl.when(self.has_down)(lambda: greet(self.down))
        vertical = jnp.where(self.has_up, 1, 0) + jnp.where(self.has_down, 1, 0)
        pl.semaphore_wait(barrier, 3 + vertical)

    def ring(self, k):
        if k == 0:
            return [(None, self.s)]
        return [(self.s - k >= 0, self.s - k), (self.s + k < self.shards, self.s + k)]


class Gather:
    def __init__(self, place, copies, sems, row, here, first, relayed, wanted):
        self.place, self.copies, self.row = place, copies, row
        self.sems, self.here, self.first = sems, here, first
        self.relayed, self.wanted = relayed, wanted

    def copy(self, kind, index, source, target, device):
        send, recv = self.sems
        return pltpu.make_async_remote_copy(
            src_ref=source,
            dst_ref=target,
            send_sem=send.at[self.row, kind, index],
            recv_sem=recv.at[self.row, 0 if kind < 2 else kind - 1, index],
            device_id=device,
            device_id_type=pl.DeviceIdType.MESH,
        )

    def source(self, k, block):
        return self.first if k == 0 else self.here(block, self.place.t)

    def z_send(self, k):
        p = self.place
        (under, below), *rest = p.ring(k - 1)
        over, above = rest[0] if rest else (under, below)
        self.copies.start(
            both(under, p.has_up),
            lambda: self.copy(0, below, self.source(k - 1, below), self.here(below, p.t), p.up),
        )
        self.copies.start(
            both(over, p.has_down),
            lambda: self.copy(1, above, self.source(k - 1, above), self.here(above, p.t), p.down),
        )

    def send(self, kind, k, region, device):
        for when, block in self.place.ring(k):
            self.copies.start(
                when,
                lambda block=block: self.copy(
                    kind, block, region(block, k), region(block, None), device
                ),
            )

    def wait(self, stage, k, region, device):
        for when, block in self.place.ring(k):
            arrive(when, region(block), self.sems[1].at[self.row, stage, block], device)

    def z(self, k):
        p = self.place
        if k > 0:
            self.wait(0, k, lambda b: self.here(b, p.t), p.y)
        if k + 1 < p.shards:
            self.z_send(k + 1)
        self.send(
            2,
            k,
            lambda b, at: (self.source(0, b) if at == 0 else self.here(b, p.t)).at[p.cx],
            p.y,
        )

    def y(self, k):
        p = self.place
        self.wait(1, k, lambda b: self.here(b, p.nt).at[p.cx], p.y)
        self.send(3, k, lambda b, at: self.here(b, p.nt).at[p.cx], p.x)

    def x(self, k):
        p = self.place
        self.wait(2, k, lambda b: self.here(b, p.nt).at[p.nx], p.x)
        self.send(4, k, lambda b, at: self.relayed(b), p.core)

    def core(self, k):
        self.wait(3, k, self.wanted, self.place.core)


def forward_kernel(
    shards,
    starts_ref,
    wq_ref,
    wk_ref,
    wv_ref,
    wo_ref,
    wu_ref,
    wd_ref,
    head_bias_ref,
    up_bias_ref,
    tokens_ref,
    cot_ref,
    x_ref,
    cot_rows_ref,
    wqkv_ref,
    qkv_ref,
    heads_ref,
    rows_ref,
    total_ref,
    out_ref,
    up_ref,
    down_ref,
    up_bias_out,
    x_all,
    wg,
    qkv,
    mixed,
    wo_low,
    wu_low,
    wd_low,
    bias_all,
    send,
    recv,
    token_send,
    token_recv,
    local_sem,
):
    p = Place(shards)
    copies = Copies()
    half = wq_ref.shape[1]
    quarter = wg.shape[4]
    units = wu_ref.shape[1]
    seq_of = lambda cx, t: 2 * cx + t
    seq = seq_of(p.cx, p.t)
    seq_far = seq_of(1 - p.cx, p.t)
    far = 2 * (1 - p.cx) + p.h
    peer = p.c + 1 - 2 * p.h
    locals_ = []

    def local(source, target):
        copy = pltpu.make_async_copy(source, target, local_sem.at[len(locals_)])
        copy.start()
        locals_.append(copy)
        return copy

    def remote(index, source, target, device):
        return pltpu.make_async_remote_copy(
            src_ref=source,
            dst_ref=target,
            send_sem=token_send.at[index],
            recv_sem=token_recv.at[index],
            device_id=device,
            device_id_type=pl.DeviceIdType.MESH,
        )

    own_tokens = local(tokens_ref.at[seq], x_all.at[p.c])
    cot_own = local(cot_ref.at[seq], cot_rows_ref.at[p.cx])
    for third, ref in enumerate((wq_ref, wk_ref, wv_ref)):
        for hh in range(2):
            for xx in range(2):
                first = (2 * hh + xx) * quarter
                wg[p.t, p.s, hh, xx, :, third * half : (third + 1) * half] = low(
                    ref[first : first + quarter, :]
                )
    p.enter(False)
    copies.start(None, lambda: remote(0, tokens_ref.at[seq_far], x_all.at[p.c], p.x))
    copies.start(None, lambda: remote(1, tokens_ref.at[seq], x_all.at[p.c], p.core))
    sems = (send, recv)
    attn = Gather(
        p,
        copies,
        sems,
        0,
        lambda b, t: wg.at[t, b, p.h],
        wg.at[p.t, p.s, p.h],
        lambda b: wg.at[p.nh, b, p.h],
        lambda b: wg.at[p.h, b, p.nh],
    )
    attn.z(0)
    copies.start(None, lambda: remote(2, head_bias_ref, bias_all.at[p.t], p.y))
    copies.start(None, lambda: remote(3, up_bias_ref, up_bias_out.at[p.t], p.y))
    bias_all[p.t] = head_bias_ref[...]
    up_bias_out[p.t] = up_bias_ref[...]

    for hh in range(2):
        for xx in range(2):
            first = (2 * hh + xx) * quarter
            rows = slice(first, first + quarter)
            wo_low[hh, xx] = low(wo_ref[rows, :])
            wu_low[hh, xx] = low(wu_ref[rows, :])
            wd_low[hh, xx] = low(wd_ref[rows, :])
    cols = lambda t, n: pl.ds(pl.multiple_of(t * n, 128), n)
    own_weights = []
    gathers = []
    for row, (ref, source, n) in enumerate(
        ((out_ref, wo_low, half), (up_ref, wu_low, units), (down_ref, wd_low, units))
    ):
        own_weights.append(local(source.at[p.h], ref.at[p.s, p.h, :, :, cols(p.t, n)]))
        gathers.append(
            Gather(
                p,
                copies,
                sems,
                row + 1,
                lambda b, t, ref=ref, n=n: ref.at[b, p.h, :, :, cols(t, n)],
                source.at[p.h],
                lambda b, ref=ref: ref.at[b, p.h],
                lambda b, ref=ref: ref.at[b, p.nh],
            )
        )
    out, up, down = gathers

    far_block = x_all.at[far]
    arrive(None, far_block, token_recv.at[0], p.x)
    copies.start(None, lambda: remote(4, far_block, far_block, p.core))

    attn.z(1)
    attn.y(0)
    attn.z(2)
    attn.y(1)
    attn.x(0)
    for k in range(3, shards):
        attn.z(k)
        attn.y(k - 1)
        attn.x(k - 2)
    out.z(0)
    up.z(0)
    attn.y(shards - 1)
    attn.x(shards - 2)
    for copy in own_weights:
        copy.wait()
    out.z(1)
    attn.x(shards - 1)
    copies.start(None, lambda: remote(5, cot_ref.at[seq_far], cot_rows_ref.at[p.cx], p.x))
    out.y(0)
    for k in range(2, shards):
        out.z(k)
        out.y(k - 1)
    up.z(1)
    for k in range(shards):
        attn.core(k)
    own_tokens.wait()
    peer_far = 2 * (1 - p.cx) + 1 - p.h
    arrive(None, x_all.at[peer], token_recv.at[1], p.core)
    arrive(None, x_all.at[peer_far], token_recv.at[4], p.core)
    arrive(None, bias_all.at[1 - p.t], token_recv.at[2], p.y)
    local(x_all, x_ref)
    local(wg.at[p.h], wqkv_ref)

    weights = wg[p.h].reshape(shards * 4 * quarter, 3 * half)
    bias = bias_all[p.h]
    scale = 1.0 / math.sqrt(HEAD)
    pairs = half // PAIR

    def project(at, carry):
        result = matmul(x_all[at], weights)
        rows = pl.ds(pl.multiple_of(at * BLOCK, BLOCK), BLOCK)
        for j in range(3 * pairs):
            part = result[:, j * PAIR : (j + 1) * PAIR]
            if j < pairs:
                part = low(part + bias[0:1, j * PAIR : (j + 1) * PAIR])
                part = low(part.astype(jnp.float32) * scale)
            elif j < 2 * pairs:
                part = low(part)
            else:
                column = (j - 2 * pairs) * PAIR
                part = low(part + bias[1:2, column : column + PAIR])
            qkv[j, rows, :] = part
        return carry

    lax.fori_loop(0, x_all.shape[0], project, 0)
    local(qkv, qkv_ref)

    def on_the_way(stage):
        if stage == 0:
            out.y(shards - 1)
            for k in range(shards):
                out.x(k)
            up.y(0)
            up.z(2)
            up.y(1)
            up.x(0)
            down.z(0)
        if stage == 1:
            for k in range(3, shards):
                up.z(k)
                up.y(k - 1)
                up.x(k - 2)
            down.z(1)
            down.y(0)

    def attend(pair, carry):
        attend_pair(
            starts_ref,
            seq,
            qkv.at[pair],
            qkv.at[pairs + pair],
            qkv.at[2 * pairs + pair],
            mixed.at[pair],
            total_ref.at[pair],
        )
        return carry

    lax.fori_loop(0, 1, attend, 0)
    on_the_way(0)
    lax.fori_loop(1, 2, attend, 0)
    on_the_way(1)
    lax.fori_loop(2, pairs, attend, 0)

    def heads_of(late, hh, pair):
        column = pl.multiple_of(hh * half + pair * PAIR, PAIR)
        return rows_ref.at[late, :, pl.ds(column, PAIR)]

    for pair in range(pairs):
        for late in range(2):
            block = 2 * late + 1 - p.h
            index = 6 + 2 * pair + late
            rows = pl.ds(pl.multiple_of(block * BLOCK, BLOCK), BLOCK)
            copies.start(
                None,
                lambda index=index, pair=pair, rows=rows, late=late: remote(
                    index, mixed.at[pair, rows, :], heads_of(late, p.h, pair), p.core
                ),
            )
    for pair in range(pairs):
        local(mixed.at[pair], heads_ref.at[pair])
        for late in range(2):
            rows = pl.ds(pl.multiple_of((2 * late + p.h) * BLOCK, BLOCK), BLOCK)
            local(mixed.at[pair, rows, :], heads_of(late, p.h, pair))

    up.y(shards - 1)
    up.x(shards - 2)
    down.z(2)
    down.y(1)
    down.x(0)
    up.x(shards - 1)
    for k in range(3, shards):
        down.z(k)
        down.y(k - 1)
        down.x(k - 2)
    down.y(shards - 1)
    down.x(shards - 2)
    down.x(shards - 1)
    for array in gathers:
        for k in range(shards):
            array.core(k)
    for pair in range(pairs):
        for late in range(2):
            index = 6 + 2 * pair + late
            arrive(None, heads_of(late, 1 - p.h, pair), token_recv.at[index], p.core)
    arrive(None, up_bias_out.at[1 - p.t], token_recv.at[3], p.y)
    arrive(None, cot_rows_ref.at[1 - p.cx], token_recv.at[5], p.x)
    copies.finish()
    for copy in locals_:
        if all(copy is not done for done in [own_tokens] + own_weights):
            copy.wait()


def forward(shards, starts, weights, head_bias, up_bias, tokens, cotangent):
    w_query, w_out, w_up = weights[0], weights[3], weights[4]
    seq_dev, block, width = tokens.shape
    rows_own, half = w_query.shape
    units = w_up.shape[1]
    quarter = rows_own // 4
    pairs = half // PAIR
    length = seq_dev * block
    low_type, full_type = jnp.bfloat16, jnp.float32
    shape = jax.ShapeDtypeStruct
    vmem = pl.BlockSpec(memory_space=pltpu.VMEM)
    anywhere = pl.BlockSpec(memory_space=pl.ANY)
    return pl.pallas_call(
        lambda *refs: forward_kernel(shards, *refs),
        in_specs=[pl.BlockSpec(memory_space=pltpu.SMEM)] + [vmem] * 8 + [anywhere] * 2,
        out_specs=[anywhere] * 6 + [vmem] + [anywhere] * 3 + [vmem],
        out_shape=[
            shape((seq_dev, block, width), low_type),
            shape((2, block, width), low_type),
            shape((shards, 2, 2, quarter, 3 * half), low_type),
            shape((3 * pairs, length, PAIR), low_type),
            shape((pairs, length, PAIR), low_type),
            shape((2, block, 2 * half), low_type),
            shape((pairs, 2, length), full_type),
            shape((shards, 2, 2, quarter, 2 * half), low_type),
            shape((shards, 2, 2, quarter, 2 * units), low_type),
            shape((shards, 2, 2, quarter, 2 * units), low_type),
            shape((2, 1, units), full_type),
        ],
        scratch_shapes=[
            pltpu.VMEM((seq_dev, block, width), low_type),
            pltpu.VMEM((2, shards, 2, 2, quarter, 3 * half), low_type),
            pltpu.VMEM((3 * pairs, length, PAIR), low_type),
            pltpu.VMEM((pairs, length, PAIR), low_type),
            pltpu.VMEM((2, 2, quarter, half), low_type),
            pltpu.VMEM((2, 2, quarter, units), low_type),
            pltpu.VMEM((2, 2, quarter, units), low_type),
            pltpu.VMEM((2, 2, half), full_type),
            pltpu.SemaphoreType.DMA((4, 5, shards)),
            pltpu.SemaphoreType.DMA((4, 4, shards)),
            pltpu.SemaphoreType.DMA((6 + 2 * pairs,)),
            pltpu.SemaphoreType.DMA((6 + 2 * pairs,)),
            pltpu.SemaphoreType.DMA((8 + 3 * pairs,)),
        ],
        compiler_params=pltpu.CompilerParams(
            collective_id=1, has_side_effects=True, vmem_limit_bytes=60 * 1024 * 1024
        ),
    )(starts, *weights, head_bias, up_bias, tokens, cotangent)


def attend_back_pair(
    starts_ref, seq, q_ref, k_ref, v_ref, mixed_ref, grad_ref, total_ref, dq_ref, dk_ref, dv_ref,
    sums_ref, dk_acc, dv_acc
):
    length = q_ref.shape[0]
    blocks = length // BLOCK
    query_sum = jnp.zeros((1, PAIR), jnp.float32)
    for at in range(blocks):
        rows = slice(at * BLOCK, (at + 1) * BLOCK)
        reach = min(blocks, at + 2)
        span = slice(0, reach * BLOCK)
        queries = two_heads(q_ref[rows, :])
        grads = two_heads(grad_ref[rows, :])
        along = grad_ref[rows, :].astype(jnp.float32) * mixed_ref[rows, :].astype(jnp.float32)
        along = jnp.transpose(along)
        inner = jnp.concatenate(
            [
                jnp.sum(along[:HEAD], axis=0, keepdims=True),
                jnp.sum(along[HEAD:], axis=0, keepdims=True),
            ],
            axis=1,
        )
        total = jnp.concatenate([total_ref[0:1, rows], total_ref[1:2, rows]], axis=1)
        scores = []
        for key_at in range(reach):
            part = over_cols(k_ref[key_at * BLOCK : (key_at + 1) * BLOCK, :], queries)
            if key_at >= at:
                seen = edge_mask(starts_ref, seq, key_at * BLOCK, at * BLOCK, True)
                seen = jnp.concatenate([seen, seen], axis=1)
                part = jnp.where(seen, part, masked_score)
            scores.append(part)
        probs = jnp.exp(jnp.concatenate(scores, axis=0) - total)
        grad_probs = over_cols(v_ref[span, :], grads)
        grad_scores = low(probs * (grad_probs - inner))
        dv = matmul(low(probs), grads)
        dk = matmul(grad_scores, queries)
        if at == 0:
            dv_acc[span, :] = dv
            dk_acc[span, :] = dk
        elif at + 1 == blocks:
            dv_acc[span, :] += dv
            dk_acc[span, :] += dk
        else:
            old = slice(0, (reach - 1) * BLOCK)
            fresh = slice((reach - 1) * BLOCK, reach * BLOCK)
            dv_acc[old, :] += dv[old, :]
            dk_acc[old, :] += dk[old, :]
            dv_acc[fresh, :] = dv[fresh, :]
            dk_acc[fresh, :] = dk[fresh, :]
        dq = join_heads(over_rows(grad_scores, k_ref[span, :])) * (1.0 / math.sqrt(HEAD))
        query_sum += jnp.sum(dq, axis=0, keepdims=True)
        dq_ref[rows, :] = low(dq)
    dk_ref[...] = low(dk_acc[...])
    dv_ref[...] = low(dv_acc[...])
    sums_ref[0:1, :] = query_sum
    sums_ref[1:2, :] = jnp.sum(dv_acc[...], axis=0, keepdims=True)


class Links:
    def __init__(self, place, send, recv, copies):
        self.place, self.send, self.recv, self.copies = place, send, recv, copies
        self.made = 0

    def __call__(self, source, target, device):
        index = self.made
        ref = lambda of: of() if callable(of) else of
        self.made += 1
        make = lambda: pltpu.make_async_remote_copy(
            src_ref=ref(source),
            dst_ref=ref(target),
            send_sem=self.send.at[index],
            recv_sem=self.recv.at[index],
            device_id=device,
            device_id_type=pl.DeviceIdType.MESH,
        )
        self.copies.start(None, make)
        return lambda region: arrive(None, region, self.recv.at[index], device)

    def around(self, source, target):
        p = self.place
        waits = []
        for r, (there, _) in enumerate(p.steps):
            wait = self(
                lambda there=there: source(there), lambda r=r: target(r), (there, p.c, p.t)
            )
            waits.append(lambda wait=wait, r=r: wait(target(r)))
        return waits


def wide(ref):
    return ref[...].astype(jnp.float32)


def add_blocks(target, other, count):
    def body(i, carry):
        target[i] = low(wide(target.at[i]) + wide(other.at[i]))
        return carry

    lax.fori_loop(0, count, body, 0)


def backward_kernel(
    shards,
    starts_ref,
    down_ref,
    up_ref,
    out_ref,
    qkv_ref,
    wqkv_ref,
    x_ref,
    heads_ref,
    total_ref,
    mixed_grad_ref,
    sum_one_ref,
    final_ref,
    early_ref,
    act_out,
    input_out,
    down_out,
    up_out,
    out_out,
    qkv_out,
    early_out,
    head_out,
    qkv,
    wqkv,
    x_t,
    x_all,
    heads,
    grad_heads,
    sum_one,
    dqkv,
    dk_acc,
    dv_acc,
    sums,
    input_acc,
    part_sent,
    part_got,
    input_rows,
    down_own,
    down_core,
    down_x,
    down_y,
    down_z,
    down_fin,
    up_own,
    up_core,
    up_z,
    up_y,
    up_x,
    up_fin,
    out_own,
    out_core,
    out_y,
    out_z,
    out_x,
    out_fin,
    pair_sent,
    pair_both,
    pair_x,
    pair_y,
    pair_z,
    pair_fin,
    early_sums,
    early_got,
    early_z,
    head_sums,
    head_got,
    head_z,
    send,
    recv,
    local_sem,
):
    p = Place(shards)
    copies = Copies()
    link = Links(p, send, recv, copies)
    h, cx, t, s = p.h, p.cx, p.t, p.s
    nh, nx, nt = p.nh, p.nx, p.nt
    pairs = heads.shape[0]
    half = pairs * PAIR
    block = input_rows.shape[1]
    quarter = down_own.shape[3]
    units = down_own.shape[4]
    length = x_all.shape[0]
    seq_of = lambda cx_, t_: 2 * cx_ + t_
    near, far = seq_of(cx, t), seq_of(1 - cx, t)
    locals_ = []

    def local(source, target):
        copy = pltpu.make_async_copy(source, target, local_sem.at[len(locals_)])
        copy.start()
        locals_.append(copy)
        return copy

    x_here = local(x_ref, x_all)
    others = [local(qkv_ref, qkv), local(wqkv_ref, wqkv), local(heads_ref, heads)]
    sum_here = local(sum_one_ref, sum_one)
    for tt in range(2):
        one = pl.ds(tt * units, units)
        local(down_ref.at[:, h, :, :, one], down_own.at[tt])
        local(up_ref.at[:, h, :, one], up_own.at[tt])
        local(out_ref.at[:, h, :, pl.ds(tt * half, half)], out_own.at[tt])
    mine = locals_[5:11]
    for pair in range(pairs):
        for late in range(2):
            rows = pl.ds(pl.multiple_of((2 * late + h) * block, block), block)
            column = pl.multiple_of(h * half + pair * PAIR, PAIR)
            others.append(
                local(
                    mixed_grad_ref.at[late, :, pl.ds(column, PAIR)], grad_heads.at[pair, rows, :]
                )
            )

    p.enter(True)

    grad_waits = []
    for pair in range(pairs):
        for late in range(2):
            there = pl.ds(pl.multiple_of((2 * late + h) * block, block), block)
            here = pl.ds(pl.multiple_of((2 * late + 1 - h) * block, block), block)
            column = pl.multiple_of((1 - h) * half + pair * PAIR, PAIR)
            wait = link(
                mixed_grad_ref.at[late, :, pl.ds(column, PAIR)],
                grad_heads.at[pair, there, :],
                p.core,
            )
            grad_waits.append(
                lambda wait=wait, pair=pair, here=here: wait(grad_heads.at[pair, here, :])
            )

    def deliver(source, target):
        local(source.at[cx], target.at[near])
        wait_y = link(source.at[cx], target.at[near], p.y)
        wait_x = link(source.at[nx], target.at[near], p.x)
        yield
        wait_x(target.at[far])
        wait_far = link(lambda: target.at[far], lambda: target.at[far], p.y)
        yield
        wait_y(target.at[seq_of(cx, nt)])
        wait_far(target.at[seq_of(nx, nt)])
        yield

    def reduce_down():
        waits = [
            link(
                down_ref.at[:, nh, :, :, pl.ds(tt * units, units)], down_core.at[tt], p.core
            )
            for tt in range(2)
        ]
        yield
        for tt in range(2):
            mine[3 * tt].wait()
            waits[tt](down_core.at[tt])
            add_blocks(down_own.at[tt], down_core.at[tt], shards)
        wait = link(down_own.at[:, :, nx], down_x, p.x)
        yield
        wait(down_x)

        def body(i, carry):
            for tt in range(2):
                down_own[tt, i, cx] = low(wide(down_own.at[tt, i, cx]) + wide(down_x.at[tt, i]))
            return carry

        lax.fori_loop(0, shards, body, 0)
        wait = link(lambda: down_own.at[nt, :, cx], down_y, p.y)
        yield
        wait(down_y)

        def body_y(i, carry):
            down_own[t, i, cx] = low(wide(down_own.at[t, i, cx]) + wide(down_y.at[i]))
            return carry

        lax.fori_loop(0, shards, body_y, 0)
        waits = link.around(lambda b: down_own.at[t, b, cx], lambda r: down_z.at[r])
        yield
        total = wide(down_own.at[t, s, cx])
        for r, wait in enumerate(waits):
            wait()
            total = total + wide(down_z.at[r])
        down_fin[h, cx] = low(total)
        wait = link(down_fin.at[h, cx], down_fin.at[h, cx], p.x)
        yield
        wait(down_fin.at[h, nx])
        wait = link(down_fin.at[h], down_fin.at[h], p.core)
        yield
        wait(down_fin.at[nh])
        local(down_fin, down_out)
        yield

    def reduce_up():
        waits = [
            link(up_ref.at[:, nh, :, pl.ds(tt * units, units)], up_core.at[tt], p.core)
            for tt in range(2)
        ]
        yield
        for tt in range(2):
            mine[3 * tt + 1].wait()
            waits[tt](up_core.at[tt])
            add_blocks(up_own.at[tt], up_core.at[tt], shards)
        waits = link.around(lambda b: up_own.at[:, b], lambda r: up_z.at[r])
        yield
        for wait in waits:
            wait()
        for tt in range(2):
            total = wide(up_own.at[tt, s])
            for r in range(shards - 1):
                total = total + wide(up_z.at[r, tt])
            up_own[tt, s] = low(total)
        wait = link(up_own.at[nt, s], up_y, p.y)
        yield
        wait(up_y)
        up_own[t, s] = low(wide(up_own.at[t, s]) + wide(up_y))
        wait = link(up_own.at[t, s], up_x, p.x)
        yield
        wait(up_x)
        up_fin[h] = low(wide(up_own.at[t, s]) + wide(up_x))
        wait = link(up_fin.at[h], up_fin.at[h], p.core)
        yield
        wait(up_fin.at[nh])
        local(up_fin, up_out)
        yield

    def reduce_out():
        waits = [
            link(out_ref.at[:, nh, :, pl.ds(tt * half, half)], out_core.at[tt], p.core)
            for tt in range(2)
        ]
        yield
        for tt in range(2):
            mine[3 * tt + 2].wait()
            waits[tt](out_core.at[tt])
            add_blocks(out_own.at[tt], out_core.at[tt], shards)
        wait = link(out_own.at[nt], out_y, p.y)
        yield
        wait(out_y)
        add_blocks(out_own.at[t], out_y, shards)
        waits = link.around(lambda b: out_own.at[t, b], lambda r: out_z.at[r])
        yield
        total = wide(out_own.at[t, s])
        for r, wait in enumerate(waits):
            wait()
            total = total + wide(out_z.at[r])
        out_own[t, s] = low(total)
        wait = link(out_own.at[t, s], out_x, p.x)
        yield
        wait(out_x)
        out_fin[h] = low(wide(out_own.at[t, s]) + wide(out_x))
        wait = link(out_fin.at[h], out_fin.at[h], p.core)
        yield
        wait(out_fin.at[nh])
        local(out_fin, out_out)
        yield

    def reduce_pair(pair):
        sent, whole = lambda: pair_sent.at[pair], lambda: pair_both.at[pair]
        wait = link(lambda: sent().at[nh], lambda: whole().at[h], p.core)
        pair_both[pair, h] = pair_sent[pair, h]
        yield
        wait(whole().at[nh])
        wait = link(lambda: whole().at[:, :, nx], lambda: pair_x.at[pair], p.x)
        yield
        wait(pair_x.at[pair])

        def body(i, carry):
            for tt in range(2):
                pair_both[pair, tt, i, cx] = low(wide(whole().at[tt, i, cx]) + wide(pair_x.at[pair, tt, i]))
            return carry

        lax.fori_loop(0, shards, body, 0)
        wait = link(lambda: whole().at[nt, :, cx], lambda: pair_y.at[pair], p.y)
        yield
        wait(pair_y.at[pair])

        def body_y(i, carry):
            pair_both[pair, t, i, cx] = low(wide(whole().at[t, i, cx]) + wide(pair_y.at[pair, i]))
            return carry

        lax.fori_loop(0, shards, body_y, 0)
        waits = link.around(lambda b: whole().at[t, b, cx], lambda r: pair_z.at[pair, r])
        yield
        total = wide(whole().at[t, s, cx])
        for r, wait in enumerate(waits):
            wait()
            total = total + wide(pair_z.at[pair, r])
        fin = pair_fin.at[pair]
        fin[h, cx] = low(total)
        wait = link(fin.at[h, cx], fin.at[h, cx], p.x)
        yield
        wait(fin.at[h, nx])
        wait = link(fin.at[h], fin.at[h], p.core)
        yield
        wait(fin.at[nh])
        local(fin, qkv_out.at[pair])
        yield

    def reduce_vector(first, got, steps, around, result):
        wait = link(lambda: first, lambda: got.at[0], p.core)
        yield
        wait(got.at[0])
        steps[0] = first[...] + got[0]
        wait = link(lambda: steps.at[0], lambda: got.at[1], p.x)
        yield
        wait(got.at[1])
        steps[1] = steps[0] + got[1]
        wait = link(lambda: steps.at[1], lambda: got.at[2], p.y)
        yield
        wait(got.at[2])
        around[s] = steps[1] + got[2]
        waits = []
        for there, source in p.steps:
            waits.append((link(around.at[s], around.at[s], (there, p.c, t)), source))
        yield
        for wait, source in waits:
            wait(around.at[source])
        total = around[0]
        for at in range(1, shards):
            total = total + around[at]
        result[...] = total
        yield

    act = deliver(final_ref, act_out)
    down, up, out = reduce_down(), reduce_up(), reduce_out()
    early = reduce_vector(early_ref, early_got, early_sums, early_z, early_out)

    def step(*names):
        for chain in names:
            next(chain)

    step(down, up, out, early, act)

    x_here.wait()

    for i in range(length // block):
        rows = slice(i * block, (i + 1) * block)
        x_t[:, rows] = jnp.transpose(x_all[rows, :])
    step(down, up, out, early)
    for copy in others:
        copy.wait()
    for wait in grad_waits:
        wait()

    def pair_grads(pair):
        values = jnp.concatenate([dqkv[j * pairs + pair] for j in range(3)], axis=1)
        for i in range(shards):
            terms = low(matmul(x_t[i * 4 * quarter : (i + 1) * 4 * quarter, :], values))
            for hh in range(2):
                for xx in range(2):
                    first = (2 * hh + xx) * quarter
                    pair_sent[pair, hh, i, xx] = terms[first : first + quarter]

    def pair_inputs(pair):
        weights = jnp.concatenate(
            [
                wqkv[:, j * half + pair * PAIR : j * half + (pair + 1) * PAIR]
                for j in range(3)
            ],
            axis=1,
        )

        def body(i, carry):
            rows = pl.ds(pl.multiple_of(i * block, block), block)
            terms = over_cols(
                jnp.concatenate([dqkv[j * pairs + pair, rows, :] for j in range(3)], axis=1),
                weights,
            )
            if pair == 0:
                input_acc[i] = terms
            else:
                input_acc[i] += terms
            return carry

        lax.fori_loop(0, length // block, body, 0)

    chain_of = [None] * pairs

    def attend(pair, carry):
        attend_back_pair(
            starts_ref,
            near,
            qkv.at[pair],
            qkv.at[pairs + pair],
            qkv.at[2 * pairs + pair],
            heads.at[pair],
            grad_heads.at[pair],
            total_ref.at[pair],
            dqkv.at[pair],
            dqkv.at[pairs + pair],
            dqkv.at[2 * pairs + pair],
            sums.at[pair],
            dk_acc,
            dv_acc,
        )
        for at in range(pairs):

            @pl.when(pair == at)
            def _():
                pair_inputs(at)
                if at == pairs - 1:
                    exchange_inputs()
                pair_grads(at)
                between(at)

        return carry

    part_waits = []

    def exchange_inputs():
        for late in range(2):
            part_sent[late] = low(input_acc[2 * late + 1 - h])
        part_waits.append(link(part_sent, part_got, p.core))

    def between(at):
        chain_of[at] = reduce_pair(at)
        next(chain_of[at])
        if at == 0:
            step(early, out)
        if at == 1:
            step(chain_of[0], down, early, act)

    lax.fori_loop(0, pairs, attend, 0)
    first, second, third = chain_of
    sum_here.wait()
    part_waits[0](part_got)
    for late in range(2):
        input_rows[late] = low(
            sum_one[late] + input_acc[2 * late + h] + wide(part_got.at[late])
        )
    inputs = deliver(input_rows, input_out)
    step(inputs)
    head_first = head_sums.at[2]
    head_first[...] = jnp.zeros(head_first.shape, jnp.float32)
    for row in range(2 * pairs):
        kind = row // pairs
        head_first[pl.ds(h * 2 * pairs + row, 1), :] = sums[row % pairs, kind : kind + 1, :]
    vector = reduce_vector(head_first, head_got, head_sums, head_z, head_out)
    step(vector, third, second, out, vector)
    step(down, first, early, second, third, vector)
    step(inputs, first, out, second, vector)
    step(down, first, third, second, out, up)
    step(down, first, second, third, up)
    step(down, first, second, third, up)
    step(third, vector, act, inputs, up)
    copies.finish()
    for copy in locals_:
        if all(copy is not done for done in [x_here, sum_here] + mine + others):
            copy.wait()


def backward(
    shards, starts, down, up, out, qkv, wqkv, x, heads, totals, mixed_grad, sum_one, final, early
):
    seq_dev, block, width = x.shape
    length = seq_dev * block
    pairs = heads.shape[0]
    half = pairs * PAIR
    units = down.shape[1] // 2
    quarter = width // shards // 4
    low_type, full_type = jnp.bfloat16, jnp.float32
    shape = jax.ShapeDtypeStruct
    vmem = pl.BlockSpec(memory_space=pltpu.VMEM)
    anywhere = pl.BlockSpec(memory_space=pl.ANY)
    scratch = lambda *dims, kind=low_type: pltpu.VMEM(dims, kind)
    around = shards - 1
    early = early.reshape(-1, PAIR)
    copies = 6 + 2 * 6 + 3 + 24 + 8 * around + pairs * (5 + around)
    return pl.pallas_call(
        lambda *refs: backward_kernel(shards, *refs),
        in_specs=[pl.BlockSpec(memory_space=pltpu.SMEM)]
        + [anywhere] * 7
        + [vmem]
        + [anywhere] * 2
        + [vmem] * 2,
        out_specs=[anywhere] * 6 + [vmem] * 2,
        out_shape=[
            shape((seq_dev, block, width), low_type),
            shape((seq_dev, block, width), low_type),
            shape((2, 2, quarter, units), low_type),
            shape((2, 2 * quarter, units), low_type),
            shape((2, 2 * quarter, half), low_type),
            shape((pairs, 2, 2, quarter, 3 * PAIR), low_type),
            shape(early.shape, full_type),
            shape((4 * pairs, PAIR), full_type),
        ],
        scratch_shapes=[
            scratch(3 * pairs, length, PAIR),
            scratch(width, 3 * half),
            scratch(width, length),
            scratch(length, width),
            scratch(pairs, length, PAIR),
            scratch(pairs, length, PAIR),
            scratch(2, block, width, kind=full_type),
            scratch(3 * pairs, length, PAIR),
            scratch(length, PAIR, kind=full_type),
            scratch(length, PAIR, kind=full_type),
            scratch(pairs, 2, PAIR, kind=full_type),
            scratch(seq_dev, block, width, kind=full_type),
            scratch(2, block, width),
            scratch(2, block, width),
            scratch(2, block, width),
            scratch(2, shards, 2, quarter, units),
            scratch(2, shards, 2, quarter, units),
            scratch(2, shards, quarter, units),
            scratch(shards, quarter, units),
            scratch(around, quarter, units),
            scratch(2, 2, quarter, units),
            scratch(2, shards, 2 * quarter, units),
            scratch(2, shards, 2 * quarter, units),
            scratch(around, 2, 2 * quarter, units),
            scratch(2 * quarter, units),
            scratch(2 * quarter, units),
            scratch(2, 2 * quarter, units),
            scratch(2, shards, 2 * quarter, half),
            scratch(2, shards, 2 * quarter, half),
            scratch(shards, 2 * quarter, half),
            scratch(around, 2 * quarter, half),
            scratch(2 * quarter, half),
            scratch(2, 2 * quarter, half),
            scratch(pairs, 2, shards, 2, quarter, 3 * PAIR),
            scratch(pairs, 2, shards, 2, quarter, 3 * PAIR),
            scratch(pairs, 2, shards, quarter, 3 * PAIR),
            scratch(pairs, shards, quarter, 3 * PAIR),
            scratch(pairs, around, quarter, 3 * PAIR),
            scratch(pairs, 2, 2, quarter, 3 * PAIR),
            scratch(2, *early.shape, kind=full_type),
            scratch(3, *early.shape, kind=full_type),
            scratch(shards, *early.shape, kind=full_type),
            scratch(3, 4 * pairs, PAIR, kind=full_type),
            scratch(3, 4 * pairs, PAIR, kind=full_type),
            scratch(shards, 4 * pairs, PAIR, kind=full_type),
            pltpu.SemaphoreType.DMA((copies,)),
            pltpu.SemaphoreType.DMA((copies,)),
            pltpu.SemaphoreType.DMA((24 + 4 * pairs,)),
        ],
        compiler_params=pltpu.CompilerParams(
            collective_id=2, has_side_effects=True, vmem_limit_bytes=62 * 1024 * 1024
        ),
    )(
        starts,
        down.reshape(shards, 2, 2, quarter, 2 * units),
        up.reshape(shards, 2, 2 * quarter, 2 * units),
        out.reshape(shards, 2, 2 * quarter, 2 * half),
        qkv,
        wqkv.reshape(width, 3 * half),
        x.reshape(length, width),
        heads,
        totals,
        mixed_grad.reshape(2, block, width),
        sum_one.reshape(2, block, width),
        final.reshape(2, block, width),
        early,
    )


def make_local(shards, ctxs, tps):
    def pick(flag, former, latter):
        return jnp.where(flag, former, latter)

    def local(
        tokens,
        starts,
        w_query,
        w_key,
        w_value,
        w_out,
        w_up,
        w_down,
        head_bias,
        up_bias,
        out_biases,
        norm_gains,
        norm_shifts,
        cotangent,
    ):
        seq_dev, block, width = tokens.shape
        assert ctxs == 4 and tps == 2 and seq_dev == 4 and block == BLOCK
        rows_own = w_query.shape[0]
        half_width = w_query.shape[1]
        ctx = lax.axis_index("ctx")
        t = lax.axis_index("tp")
        core = lax.rem(ctx, 2)
        cx = lax.div(ctx, 2)
        seq_of = lambda cx_, t_: 2 * cx_ + t_
        seq = seq_of(cx, t)
        other_x = 1 - cx

        def take(array, index):
            return lax.dynamic_index_in_dim(array, index, 0, False)

        (
            x_blocks,
            cot_rows,
            wqkv,
            qkv,
            mixed_heads,
            mixed_rows,
            totals,
            out_full,
            up_full,
            down_full,
            up_bias_full,
        ) = forward(
            shards,
            starts,
            (w_query, w_key, w_value, w_out, w_up, w_down),
            head_bias,
            up_bias.reshape(1, -1),
            tokens,
            cotangent,
        )
        x_pairs_ = x_blocks.reshape(2, 2, block, width)
        rows_here = pick(core == 0, x_pairs_[:, 0], x_pairs_[:, 1]).reshape(2 * block, width)
        cot_here = cot_rows.reshape(2 * block, width)
        out_full = out_full.reshape(width, -1)
        up_full = up_full.reshape(width, -1)
        down_full = down_full.reshape(width, -1)
        up_bias_full = up_bias_full.reshape(-1)
        mixed = mixed_rows.reshape(2 * block, width)

        attn_out = over_cols(mixed, out_full) + out_biases[0]
        first_scaled, first_rstd = normalize(rows_here.astype(jnp.float32) + attn_out)
        first_norm = first_scaled * norm_gains[0] + norm_shifts[0]
        first_low = low(first_norm)
        hidden = matmul(first_low, up_full) + up_bias_full
        gauss = 0.5 * (1.0 + lax.erf(hidden * (1.0 / math.sqrt(2.0))))
        active = low(hidden * gauss)
        slope = low(
            gauss + hidden * jnp.exp(-0.5 * hidden * hidden) * (1.0 / math.sqrt(2.0 * math.pi))
        )
        ffn_out = over_cols(active, down_full) + out_biases[1]
        second_scaled, second_rstd = normalize(first_norm + ffn_out)
        final_low = low(second_scaled * norm_gains[1] + norm_shifts[1])

        grad_final = cot_here.astype(jnp.float32)
        gain_two = jnp.sum(grad_final * second_scaled, axis=0)
        shift_two = jnp.sum(grad_final, axis=0)
        grad_second = norm_back(grad_final, second_scaled, second_rstd, norm_gains[1])
        bias_two = jnp.sum(grad_second, axis=0)
        grad_ffn = low(grad_second)
        grad_active = matmul(grad_ffn, down_full)
        grad_hidden = grad_active * slope.astype(jnp.float32)
        up_bias_grad = jnp.sum(grad_hidden, axis=0)
        grad_hidden_low = low(grad_hidden)
        grad_first = grad_second + over_cols(grad_hidden_low, up_full)
        gain_one = jnp.sum(grad_first * first_scaled, axis=0)
        shift_one = jnp.sum(grad_first, axis=0)
        grad_sum_one = norm_back(grad_first, first_scaled, first_rstd, norm_gains[0])
        bias_one = jnp.sum(grad_sum_one, axis=0)
        grad_attn = low(grad_sum_one)
        grad_mixed = low(matmul(grad_attn, out_full))
        grad_down_local = low(over_rows(grad_ffn, active))
        grad_up_local = low(over_rows(first_low, grad_hidden_low))
        grad_out_local = low(over_rows(grad_attn, mixed))

        early = jnp.concatenate(
            [up_bias_grad, bias_one, bias_two, gain_one, gain_two, shift_one, shift_two]
        )
        (
            activations,
            input_grad,
            grad_down,
            grad_up,
            grad_out,
            grad_pairs,
            early,
            head_sums,
        ) = backward(
            shards,
            starts,
            grad_down_local,
            grad_up_local,
            grad_out_local,
            qkv,
            wqkv,
            x_blocks,
            mixed_heads,
            totals,
            grad_mixed,
            grad_sum_one,
            final_low,
            early,
        )
        whole = lambda grad: grad.reshape(rows_own, -1).astype(jnp.float32)
        pairs = half_width // PAIR
        grad_pairs = grad_pairs.reshape(pairs, rows_own, 3, PAIR).transpose(2, 1, 0, 3)
        grad_pairs = grad_pairs.reshape(3, rows_own, half_width).astype(jnp.float32)
        units = up_bias_grad.shape[0]
        early = early.reshape(-1)
        up_sum = lax.dynamic_index_in_dim(early[:units].reshape(2, units // 2), t, 0, False)
        vectors = early[units:].reshape(3, 2, width)
        head_sums = lax.dynamic_index_in_dim(
            head_sums.reshape(2, 2, half_width), t, 0, False
        )
        return (
            activations,
            input_grad.astype(jnp.float32),
            grad_pairs[0],
            grad_pairs[1],
            grad_pairs[2],
            whole(grad_out),
            whole(grad_up),
            whole(grad_down),
            head_sums,
            up_sum,
            vectors[0],
            vectors[1],
            vectors[2],
        )

    return local


def solution(mesh):
    sizes = [mesh.shape[name] for name in AXES]
    return jax.shard_map(
        make_local(*sizes),
        mesh=mesh,
        in_specs=(
            P("shard", "ctx", None),
            P("shard", None),
            P("shard", "tp"),
            P("shard", "tp"),
            P("shard", "tp"),
            P("shard", "tp"),
            P("shard", "tp"),
            P("shard", "tp"),
            P(None, "tp"),
            P("tp"),
            P(),
            P(),
            P(),
            P("shard", "ctx", None),
        ),
        out_specs=(
            P("shard", "ctx", None),
            P("shard", "ctx", None),
            P("shard", "tp"),
            P("shard", "tp"),
            P("shard", "tp"),
            P("shard", "tp"),
            P("shard", "tp"),
            P("shard", "tp"),
            P(None, "tp"),
            P("tp"),
            P(),
            P(),
            P(),
        ),
        check_vma=False,
    )
```

```python
import math

import jax
import jax.numpy as jnp
from jax import lax
from jax.experimental import pallas as pl
from jax.experimental.pallas import tpu as pltpu
from jax.sharding import PartitionSpec as P

HEAD = 64
PIECE = 256
BLOCK = 256
PAIR = 128

norm_eps = 1e-05
masked_score = -1e30
AXES = ("shard", "ctx", "tp")


def matmul(former, latter):
    return jnp.dot(former, latter, preferred_element_type=jnp.float32)


def over_rows(former, latter):
    return lax.dot_general(
        former, latter, (((0,), (0,)), ((), ())), preferred_element_type=jnp.float32
    )


def over_cols(former, latter):
    return lax.dot_general(
        former, latter, (((1,), (1,)), ((), ())), preferred_element_type=jnp.float32
    )


def low(values):
    return values.astype(jnp.bfloat16)


def normalize(values):
    centre = jnp.mean(values, axis=-1, keepdims=True)
    centred = values - centre
    spread = jnp.mean(centred * centred, axis=-1, keepdims=True)
    scaling = lax.rsqrt(spread + norm_eps)
    return (centred * scaling, scaling)


def norm_back(grad_out, scaled, scaling, gain_row):
    grad_scaled = grad_out * gain_row
    mean_grad = jnp.mean(grad_scaled, axis=-1, keepdims=True)
    mean_along = jnp.mean(grad_scaled * scaled, axis=-1, keepdims=True)
    return scaling * (grad_scaled - mean_grad - scaled * mean_along)


def edge_mask(starts_ref, seq, key_first, query_first, keys_first):
    key_shape = (BLOCK, 1) if keys_first else (1, BLOCK)
    query_shape = (1, BLOCK) if keys_first else (BLOCK, 1)
    key_at = key_first + lax.broadcasted_iota(jnp.int32, key_shape, 0 if keys_first else 1)
    query_at = query_first + lax.broadcasted_iota(jnp.int32, query_shape, 1 if keys_first else 0)
    seen = key_at <= query_at
    for piece in range(2):
        start = starts_ref[seq, piece]
        key_in = (key_at >= start) & (key_at < start + PIECE)
        query_in = (query_at >= start) & (query_at < start + PIECE)
        seen = seen | (key_in & query_in)
    return seen


def two_heads(rows):
    lane = lax.broadcasted_iota(jnp.int32, rows.shape, 1)
    zero = jnp.zeros_like(rows)
    return jnp.concatenate(
        [jnp.where(lane < HEAD, rows, zero), jnp.where(lane >= HEAD, rows, zero)], axis=0
    )


def join_heads(rows):
    half = rows.shape[0] // 2
    lane = lax.broadcasted_iota(jnp.int32, (half, rows.shape[1]), 1)
    return jnp.where(lane < HEAD, rows[:half], rows[half:])


def attend_pair(starts_ref, seq, q_ref, k_ref, v_ref, mixed_ref, total_ref):
    length = q_ref.shape[0]
    blocks = length // BLOCK
    for at in range(blocks):
        rows = slice(at * BLOCK, (at + 1) * BLOCK)
        reach = min(blocks, at + 2)
        queries = two_heads(q_ref[rows, :])
        scores = []
        for key_at in range(reach):
            part = over_cols(queries, k_ref[key_at * BLOCK : (key_at + 1) * BLOCK, :])
            if key_at >= at:
                seen = edge_mask(starts_ref, seq, key_at * BLOCK, at * BLOCK, False)
                seen = jnp.concatenate([seen, seen], axis=0)
                part = jnp.where(seen, part, masked_score)
            scores.append(part)
        scores = jnp.concatenate(scores, axis=1)
        top = jnp.max(scores, axis=1, keepdims=True)
        raised = jnp.exp(scores - top)
        total = jnp.sum(raised, axis=1, keepdims=True)
        mixed = matmul(low(raised), v_ref[: reach * BLOCK, :]) / total
        mixed_ref[rows, :] = low(join_heads(mixed))
        wide = jnp.broadcast_to(top + jnp.log(total), (2 * BLOCK, PAIR))
        row = jnp.transpose(wide)[0:1, :]
        total_ref[0:1, rows] = row[:, :BLOCK]
        total_ref[1:2, rows] = row[:, BLOCK:]


class Copies:
    def __init__(self):
        self.sent = []

    def start(self, when, make):
        self.sent.append((when, make))
        if when is None:
            make().start()
        else:
            pl.when(when)(lambda: make().start())

    def finish(self):
        for when, make in self.sent:
            if when is None:
                make().wait_send()
            else:
                pl.when(when)(lambda make=make: make().wait_send())


def both(former, latter):
    if former is None:
        return latter
    return former if latter is None else former & latter


def arrive(when, region, sem, device):
    def wait():
        pltpu.make_async_remote_copy(
            src_ref=region,
            dst_ref=region,
            send_sem=sem,
            recv_sem=sem,
            device_id=device,
            device_id_type=pl.DeviceIdType.MESH,
        ).wait_recv()

    if when is None:
        wait()
    else:
        pl.when(when)(wait)


class Place:
    def __init__(self, shards):
        self.shards = shards
        self.s = lax.axis_index("shard")
        self.c = lax.axis_index("ctx")
        self.t = lax.axis_index("tp")
        self.h = lax.rem(self.c, 2)
        self.cx = lax.div(self.c, 2)
        self.core = (self.s, self.c + 1 - 2 * self.h, self.t)
        self.x = (self.s, self.c + 2 - 4 * self.cx, self.t)
        self.y = (self.s, self.c, 1 - self.t)
        self.up = (self.s + 1, self.c, self.t)
        self.down = (self.s - 1, self.c, self.t)
        self.nh, self.nx, self.nt = 1 - self.h, 1 - self.cx, 1 - self.t
        self.steps = [
            (lax.rem(self.s + r, shards), lax.rem(self.s + shards - r, shards))
            for r in range(1, shards)
        ]
        self.has_up = self.s < shards - 1
        self.has_down = self.s > 0

    def enter(self, whole_line):
        barrier = pltpu.get_barrier_semaphore()

        def greet(device):
            pl.semaphore_signal(
                barrier, inc=1, device_id=device, device_id_type=pl.DeviceIdType.MESH
            )

        for device in (self.core, self.x, self.y):
            greet(device)
        if whole_line:
            for there, _ in self.steps:
                greet((there, self.c, self.t))
            pl.semaphore_wait(barrier, 3 + len(self.steps))
            return
        pl.when(self.has_up)(lambda: greet(self.up))
        pl.when(self.has_down)(lambda: greet(self.down))
        vertical = jnp.where(self.has_up, 1, 0) + jnp.where(self.has_down, 1, 0)
        pl.semaphore_wait(barrier, 3 + vertical)

    def ring(self, k):
        if k == 0:
            return [(None, self.s)]
        return [(self.s - k >= 0, self.s - k), (self.s + k < self.shards, self.s + k)]


class Gather:
    def __init__(self, place, copies, sems, row, here, first, relayed, wanted):
        self.place, self.copies, self.row = place, copies, row
        self.sems, self.here, self.first = sems, here, first
        self.relayed, self.wanted = relayed, wanted

    def copy(self, kind, index, source, target, device):
        send, recv = self.sems
        return pltpu.make_async_remote_copy(
            src_ref=source,
            dst_ref=target,
            send_sem=send.at[self.row, kind, index],
            recv_sem=recv.at[self.row, 0 if kind < 2 else kind - 1, index],
            device_id=device,
            device_id_type=pl.DeviceIdType.MESH,
        )

    def source(self, k, block):
        return self.first if k == 0 else self.here(block, self.place.t)

    def z_send(self, k):
        p = self.place
        (under, below), *rest = p.ring(k - 1)
        over, above = rest[0] if rest else (under, below)
        self.copies.start(
            both(under, p.has_up),
            lambda: self.copy(0, below, self.source(k - 1, below), self.here(below, p.t), p.up),
        )
        self.copies.start(
            both(over, p.has_down),
            lambda: self.copy(1, above, self.source(k - 1, above), self.here(above, p.t), p.down),
        )

    def send(self, kind, k, region, device):
        for when, block in self.place.ring(k):
            self.copies.start(
                when,
                lambda block=block: self.copy(
                    kind, block, region(block, k), region(block, None), device
                ),
            )

    def wait(self, stage, k, region, device):
        for when, block in self.place.ring(k):
            arrive(when, region(block), self.sems[1].at[self.row, stage, block], device)

    def z(self, k):
        p = self.place
        if k > 0:
            self.wait(0, k, lambda b: self.here(b, p.t), p.y)
        if k + 1 < p.shards:
            self.z_send(k + 1)
        self.send(
            2,
            k,
            lambda b, at: (self.source(0, b) if at == 0 else self.here(b, p.t)).at[p.cx],
            p.y,
        )

    def y(self, k):
        p = self.place
        self.wait(1, k, lambda b: self.here(b, p.nt).at[p.cx], p.y)
        self.send(3, k, lambda b, at: self.here(b, p.nt).at[p.cx], p.x)

    def x(self, k):
        p = self.place
        self.wait(2, k, lambda b: self.here(b, p.nt).at[p.nx], p.x)
        self.send(4, k, lambda b, at: self.relayed(b), p.core)

    def core(self, k):
        self.wait(3, k, self.wanted, self.place.core)


def forward_kernel(
    shards,
    starts_ref,
    wq_ref,
    wk_ref,
    wv_ref,
    wo_ref,
    wu_ref,
    wd_ref,
    head_bias_ref,
    up_bias_ref,
    tokens_ref,
    cot_ref,
    x_ref,
    cot_rows_ref,
    wqkv_ref,
    qkv_ref,
    heads_ref,
    rows_ref,
    total_ref,
    out_ref,
    up_ref,
    down_ref,
    up_bias_out,
    x_all,
    wg,
    qkv,
    mixed,
    wo_low,
    wu_low,
    wd_low,
    bias_all,
    send,
    recv,
    token_send,
    token_recv,
    local_sem,
):
    p = Place(shards)
    copies = Copies()
    half = wq_ref.shape[1]
    quarter = wg.shape[4]
    units = wu_ref.shape[1]
    seq_of = lambda cx, t: 2 * cx + t
    seq = seq_of(p.cx, p.t)
    seq_far = seq_of(1 - p.cx, p.t)
    far = 2 * (1 - p.cx) + p.h
    peer = p.c + 1 - 2 * p.h
    locals_ = []

    def local(source, target):
        copy = pltpu.make_async_copy(source, target, local_sem.at[len(locals_)])
        copy.start()
        locals_.append(copy)
        return copy

    def remote(index, source, target, device):
        return pltpu.make_async_remote_copy(
            src_ref=source,
            dst_ref=target,
            send_sem=token_send.at[index],
            recv_sem=token_recv.at[index],
            device_id=device,
            device_id_type=pl.DeviceIdType.MESH,
        )

    own_tokens = local(tokens_ref.at[seq], x_all.at[p.c])
    cot_own = local(cot_ref.at[seq], cot_rows_ref.at[p.cx])
    for third, ref in enumerate((wq_ref, wk_ref, wv_ref)):
        for hh in range(2):
            for xx in range(2):
                first = (2 * hh + xx) * quarter
                wg[p.t, p.s, hh, xx, :, third * half : (third + 1) * half] = low(
                    ref[first : first + quarter, :]
                )
    p.enter(False)
    copies.start(None, lambda: remote(0, tokens_ref.at[seq_far], x_all.at[p.c], p.x))
    copies.start(None, lambda: remote(1, tokens_ref.at[seq], x_all.at[p.c], p.core))
    sems = (send, recv)
    attn = Gather(
        p,
        copies,
        sems,
        0,
        lambda b, t: wg.at[t, b, p.h],
        wg.at[p.t, p.s, p.h],
        lambda b: wg.at[p.nh, b, p.h],
        lambda b: wg.at[p.h, b, p.nh],
    )
    attn.z(0)
    copies.start(None, lambda: remote(2, head_bias_ref, bias_all.at[p.t], p.y))
    copies.start(None, lambda: remote(3, up_bias_ref, up_bias_out.at[p.t], p.y))
    bias_all[p.t] = head_bias_ref[...]
    up_bias_out[p.t] = up_bias_ref[...]

    for hh in range(2):
        for xx in range(2):
            first = (2 * hh + xx) * quarter
            rows = slice(first, first + quarter)
            wo_low[hh, xx] = low(wo_ref[rows, :])
            wu_low[hh, xx] = low(wu_ref[rows, :])
            wd_low[hh, xx] = low(wd_ref[rows, :])
    cols = lambda t, n: pl.ds(pl.multiple_of(t * n, 128), n)
    own_weights = []
    gathers = []
    for row, (ref, source, n) in enumerate(
        ((out_ref, wo_low, half), (up_ref, wu_low, units), (down_ref, wd_low, units))
    ):
        own_weights.append(local(source.at[p.h], ref.at[p.s, p.h, :, :, cols(p.t, n)]))
        gathers.append(
            Gather(
                p,
                copies,
                sems,
                row + 1,
                lambda b, t, ref=ref, n=n: ref.at[b, p.h, :, :, cols(t, n)],
                source.at[p.h],
                lambda b, ref=ref: ref.at[b, p.h],
                lambda b, ref=ref: ref.at[b, p.nh],
            )
        )
    out, up, down = gathers

    far_block = x_all.at[far]
    arrive(None, far_block, token_recv.at[0], p.x)
    copies.start(None, lambda: remote(4, far_block, far_block, p.core))

    attn.z(1)
    attn.y(0)
    attn.z(2)
    attn.y(1)
    attn.x(0)
    for k in range(3, shards):
        attn.z(k)
        attn.y(k - 1)
        attn.x(k - 2)
    out.z(0)
    up.z(0)
    attn.y(shards - 1)
    attn.x(shards - 2)
    for copy in own_weights:
        copy.wait()
    out.z(1)
    attn.x(shards - 1)
    copies.start(None, lambda: remote(5, cot_ref.at[seq_far], cot_rows_ref.at[p.cx], p.x))
    out.y(0)
    for k in range(2, shards):
        out.z(k)
        out.y(k - 1)
    up.z(1)
    for k in range(shards):
        attn.core(k)
    own_tokens.wait()
    peer_far = 2 * (1 - p.cx) + 1 - p.h
    arrive(None, x_all.at[peer], token_recv.at[1], p.core)
    arrive(None, x_all.at[peer_far], token_recv.at[4], p.core)
    arrive(None, bias_all.at[1 - p.t], token_recv.at[2], p.y)
    local(x_all, x_ref)
    local(wg.at[p.h], wqkv_ref)

    weights = wg[p.h].reshape(shards * 4 * quarter, 3 * half)
    bias = bias_all[p.h]
    scale = 1.0 / math.sqrt(HEAD)
    pairs = half // PAIR

    def project(at, carry):
        result = matmul(x_all[at], weights)
        rows = pl.ds(pl.multiple_of(at * BLOCK, BLOCK), BLOCK)
        for j in range(3 * pairs):
            part = result[:, j * PAIR : (j + 1) * PAIR]
            if j < pairs:
                part = low(part + bias[0:1, j * PAIR : (j + 1) * PAIR])
                part = low(part.astype(jnp.float32) * scale)
            elif j < 2 * pairs:
                part = low(part)
            else:
                column = (j - 2 * pairs) * PAIR
                part = low(part + bias[1:2, column : column + PAIR])
            qkv[j, rows, :] = part
        return carry

    lax.fori_loop(0, x_all.shape[0], project, 0)
    local(qkv, qkv_ref)

    def on_the_way(stage):
        if stage == 0:
            out.y(shards - 1)
            for k in range(shards):
                out.x(k)
            up.y(0)
            up.z(2)
            up.y(1)
            up.x(0)
            down.z(0)
        if stage == 1:
            for k in range(3, shards):
                up.z(k)
                up.y(k - 1)
                up.x(k - 2)
            down.z(1)
            down.y(0)

    def attend(pair, carry):
        attend_pair(
            starts_ref,
            seq,
            qkv.at[pair],
            qkv.at[pairs + pair],
            qkv.at[2 * pairs + pair],
            mixed.at[pair],
            total_ref.at[pair],
        )
        return carry

    lax.fori_loop(0, 1, attend, 0)
    on_the_way(0)
    lax.fori_loop(1, 2, attend, 0)
    on_the_way(1)
    lax.fori_loop(2, pairs, attend, 0)

    def heads_of(late, hh, pair):
        column = pl.multiple_of(hh * half + pair * PAIR, PAIR)
        return rows_ref.at[late, :, pl.ds(column, PAIR)]

    for pair in range(pairs):
        for late in range(2):
            block = 2 * late + 1 - p.h
            index = 6 + 2 * pair + late
            rows = pl.ds(pl.multiple_of(block * BLOCK, BLOCK), BLOCK)
            copies.start(
                None,
                lambda index=index, pair=pair, rows=rows, late=late: remote(
                    index, mixed.at[pair, rows, :], heads_of(late, p.h, pair), p.core
                ),
            )
    for pair in range(pairs):
        local(mixed.at[pair], heads_ref.at[pair])
        for late in range(2):
            rows = pl.ds(pl.multiple_of((2 * late + p.h) * BLOCK, BLOCK), BLOCK)
            local(mixed.at[pair, rows, :], heads_of(late, p.h, pair))

    up.y(shards - 1)
    up.x(shards - 2)
    down.z(2)
    down.y(1)
    down.x(0)
    up.x(shards - 1)
    for k in range(3, shards):
        down.z(k)
        down.y(k - 1)
        down.x(k - 2)
    down.y(shards - 1)
    down.x(shards - 2)
    down.x(shards - 1)
    for array in gathers:
        for k in range(shards):
            array.core(k)
    for pair in range(pairs):
        for late in range(2):
            index = 6 + 2 * pair + late
            arrive(None, heads_of(late, 1 - p.h, pair), token_recv.at[index], p.core)
    arrive(None, up_bias_out.at[1 - p.t], token_recv.at[3], p.y)
    arrive(None, cot_rows_ref.at[1 - p.cx], token_recv.at[5], p.x)
    copies.finish()
    for copy in locals_:
        if all(copy is not done for done in [own_tokens] + own_weights):
            copy.wait()


def forward(shards, starts, weights, head_bias, up_bias, tokens, cotangent):
    w_query, w_out, w_up = weights[0], weights[3], weights[4]
    seq_dev, block, width = tokens.shape
    rows_own, half = w_query.shape
    units = w_up.shape[1]
    quarter = rows_own // 4
    pairs = half // PAIR
    length = seq_dev * block
    low_type, full_type = jnp.bfloat16, jnp.float32
    shape = jax.ShapeDtypeStruct
    vmem = pl.BlockSpec(memory_space=pltpu.VMEM)
    anywhere = pl.BlockSpec(memory_space=pl.ANY)
    return pl.pallas_call(
        lambda *refs: forward_kernel(shards, *refs),
        in_specs=[pl.BlockSpec(memory_space=pltpu.SMEM)] + [vmem] * 8 + [anywhere] * 2,
        out_specs=[anywhere] * 6 + [vmem] + [anywhere] * 3 + [vmem],
        out_shape=[
            shape((seq_dev, block, width), low_type),
            shape((2, block, width), low_type),
            shape((shards, 2, 2, quarter, 3 * half), low_type),
            shape((3 * pairs, length, PAIR), low_type),
            shape((pairs, length, PAIR), low_type),
            shape((2, block, 2 * half), low_type),
            shape((pairs, 2, length), full_type),
            shape((shards, 2, 2, quarter, 2 * half), low_type),
            shape((shards, 2, 2, quarter, 2 * units), low_type),
            shape((shards, 2, 2, quarter, 2 * units), low_type),
            shape((2, 1, units), full_type),
        ],
        scratch_shapes=[
            pltpu.VMEM((seq_dev, block, width), low_type),
            pltpu.VMEM((2, shards, 2, 2, quarter, 3 * half), low_type),
            pltpu.VMEM((3 * pairs, length, PAIR), low_type),
            pltpu.VMEM((pairs, length, PAIR), low_type),
            pltpu.VMEM((2, 2, quarter, half), low_type),
            pltpu.VMEM((2, 2, quarter, units), low_type),
            pltpu.VMEM((2, 2, quarter, units), low_type),
            pltpu.VMEM((2, 2, half), full_type),
            pltpu.SemaphoreType.DMA((4, 5, shards)),
            pltpu.SemaphoreType.DMA((4, 4, shards)),
            pltpu.SemaphoreType.DMA((6 + 2 * pairs,)),
            pltpu.SemaphoreType.DMA((6 + 2 * pairs,)),
            pltpu.SemaphoreType.DMA((8 + 3 * pairs,)),
        ],
        compiler_params=pltpu.CompilerParams(
            collective_id=1, has_side_effects=True, vmem_limit_bytes=60 * 1024 * 1024
        ),
    )(starts, *weights, head_bias, up_bias, tokens, cotangent)


def attend_back_pair(
    starts_ref, seq, q_ref, k_ref, v_ref, mixed_ref, grad_ref, total_ref, dq_ref, dk_ref, dv_ref,
    sums_ref, dk_acc, dv_acc
):
    length = q_ref.shape[0]
    blocks = length // BLOCK
    query_sum = jnp.zeros((1, PAIR), jnp.float32)
    for at in range(blocks):
        rows = slice(at * BLOCK, (at + 1) * BLOCK)
        reach = min(blocks, at + 2)
        span = slice(0, reach * BLOCK)
        queries = two_heads(q_ref[rows, :])
        grads = two_heads(grad_ref[rows, :])
        along = grad_ref[rows, :].astype(jnp.float32) * mixed_ref[rows, :].astype(jnp.float32)
        along = jnp.transpose(along)
        inner = jnp.concatenate(
            [
                jnp.sum(along[:HEAD], axis=0, keepdims=True),
                jnp.sum(along[HEAD:], axis=0, keepdims=True),
            ],
            axis=1,
        )
        total = jnp.concatenate([total_ref[0:1, rows], total_ref[1:2, rows]], axis=1)
        scores = []
        for key_at in range(reach):
            part = over_cols(k_ref[key_at * BLOCK : (key_at + 1) * BLOCK, :], queries)
            if key_at >= at:
                seen = edge_mask(starts_ref, seq, key_at * BLOCK, at * BLOCK, True)
                seen = jnp.concatenate([seen, seen], axis=1)
                part = jnp.where(seen, part, masked_score)
            scores.append(part)
        probs = jnp.exp(jnp.concatenate(scores, axis=0) - total)
        grad_probs = over_cols(v_ref[span, :], grads)
        grad_scores = low(probs * (grad_probs - inner))
        dv = matmul(low(probs), grads)
        dk = matmul(grad_scores, queries)
        if at == 0:
            dv_acc[span, :] = dv
            dk_acc[span, :] = dk
        elif at + 1 == blocks:
            dv_acc[span, :] += dv
            dk_acc[span, :] += dk
        else:
            old = slice(0, (reach - 1) * BLOCK)
            fresh = slice((reach - 1) * BLOCK, reach * BLOCK)
            dv_acc[old, :] += dv[old, :]
            dk_acc[old, :] += dk[old, :]
            dv_acc[fresh, :] = dv[fresh, :]
            dk_acc[fresh, :] = dk[fresh, :]
        dq = join_heads(over_rows(grad_scores, k_ref[span, :])) * (1.0 / math.sqrt(HEAD))
        query_sum += jnp.sum(dq, axis=0, keepdims=True)
        dq_ref[rows, :] = low(dq)
    dk_ref[...] = low(dk_acc[...])
    dv_ref[...] = low(dv_acc[...])
    sums_ref[0:1, :] = query_sum
    sums_ref[1:2, :] = jnp.sum(dv_acc[...], axis=0, keepdims=True)


class Links:
    def __init__(self, place, send, recv):
        self.place, self.send, self.recv = place, send, recv
        self.made, self.open = 0, {}

    def __call__(self, source, target, device):
        index = self.made
        self.made += 1
        self.open[index] = lambda: pltpu.make_async_remote_copy(
            src_ref=source(),
            dst_ref=target(),
            send_sem=self.send.at[index],
            recv_sem=self.recv.at[index],
            device_id=device,
            device_id_type=pl.DeviceIdType.MESH,
        )
        self.open[index]().start()
        return lambda region: arrive(None, region, self.recv.at[index], device)

    def around(self, source, target):
        p = self.place
        waits = []
        for r, (there, _) in enumerate(p.steps):
            wait = self(
                lambda there=there: source(there), lambda r=r: target(r), (there, p.c, p.t)
            )
            waits.append(lambda wait=wait, r=r: wait(target(r)))
        return waits

    def sent(self, since=0):
        for index in sorted(self.open):
            if index >= since:
                self.open.pop(index)().wait_send()


class Locals:
    def __init__(self, sems):
        self.sems, self.made, self.open = sems, 0, {}

    def __call__(self, source, target):
        index = self.made
        self.made += 1
        self.open[index] = lambda: pltpu.make_async_copy(source(), target(), self.sems.at[index])
        self.open[index]().start()
        return lambda: self.open.pop(index)().wait()

    def finish(self):
        for index in sorted(self.open):
            self.open.pop(index)().wait()


def wide(ref):
    return ref[...].astype(jnp.float32)


def each(count, body):
    def turn(i, carry):
        body(i)
        return carry

    lax.fori_loop(0, count, turn, 0)


def add_blocks(target, other, count):
    def body(i):
        target[i] = low(wide(target.at[i]) + wide(other.at[i]))

    each(count, body)


def summed(rows):
    return jnp.sum(rows, axis=0, keepdims=True)


def backward_kernel(
    shards,
    starts_ref,
    total_ref,
    up_bias_ref,
    out_bias_ref,
    gain_ref,
    shift_ref,
    mixed_ref,
    x_ref,
    cot_ref,
    w_out_ref,
    w_up_ref,
    w_down_ref,
    qkv_ref,
    wqkv_ref,
    heads_ref,
    act_out,
    input_out,
    down_out,
    up_a_out,
    up_c_out,
    out_out,
    query_out,
    key_out,
    value_out,
    up_bias_out,
    out_bias_out,
    gain_out,
    shift_out,
    head_bias_out,
    grad_heads,
    grad_mixed,
    sum_one,
    final_rows,
    input_rows,
    part_sent,
    part_got,
    grad_sent,
    down_own,
    down_core,
    down_x,
    down_y,
    down_z,
    down_fin,
    up_a_own,
    up_a_core,
    up_a_y,
    up_a_z,
    up_a_x,
    up_a_fin,
    up_c_own,
    up_c_core,
    up_c_z,
    up_c_y,
    up_c_x,
    up_c_fin,
    out_sent,
    out_own,
    out_core,
    out_y,
    out_z,
    out_x,
    out_fin,
    pair_both,
    pair_x,
    pair_y,
    pair_z,
    pair_fin,
    early_first,
    early_steps,
    early_got,
    early_z,
    head_first,
    head_steps,
    head_got,
    head_z,
    send,
    recv,
    local_sem,
):
    p = Place(shards)
    link = Links(p, send, recv)
    local = Locals(local_sem)
    h, cx, t, s = p.h, p.cx, p.t, p.s
    nh, nx, nt = p.nh, p.nx, p.nt
    pairs, length = grad_heads.shape[0], grad_heads.shape[1]
    half = pairs * PAIR
    block, width = input_rows.shape[1], input_rows.shape[2]
    quarter, units = down_own.shape[3], down_own.shape[4]
    rows_two = 2 * block
    seq_of = lambda cx_, t_: 2 * cx_ + t_
    near, far = seq_of(cx, t), seq_of(nx, t)
    near_y, far_y = seq_of(cx, nt), seq_of(nx, nt)
    p.enter(True)

    def deliver(source, target):
        local(lambda: source.at[cx], lambda: target.at[near])
        wait_y = link(lambda: source.at[cx], lambda: target.at[near], p.y)
        wait_x = link(lambda: source.at[nx], lambda: target.at[near], p.x)
        yield
        wait_x(target.at[far])
        wait_far = link(lambda: target.at[far], lambda: target.at[far], p.y)
        yield
        wait_y(target.at[near_y])
        wait_far(target.at[far_y])
        yield

    def own_sum(first, later, waits):
        total = wide(first())
        for r, wait in enumerate(waits):
            wait()
            total = total + wide(later(r))
        return low(total)

    def reduce_down():
        waits = [
            link(lambda tt=tt: grad_sent.at[tt], lambda tt=tt: down_core.at[tt], p.core)
            for tt in range(2)
        ]
        yield
        for tt in range(2):
            waits[tt](down_core.at[tt])
            add_blocks(down_own.at[tt], down_core.at[tt], shards)
        wait = link(lambda: down_own.at[:, :, nx], lambda: down_x, p.x)
        yield
        wait(down_x)

        def body(i):
            for tt in range(2):
                down_own[tt, i, cx] = low(wide(down_own.at[tt, i, cx]) + wide(down_x.at[tt, i]))

        each(shards, body)
        wait = link(lambda: down_own.at[nt, :, cx], lambda: down_y, p.y)
        yield
        wait(down_y)

        def body_y(i):
            down_own[t, i, cx] = low(wide(down_own.at[t, i, cx]) + wide(down_y.at[i]))

        each(shards, body_y)
        waits = link.around(lambda b: down_own.at[t, b, cx], lambda r: down_z.at[r])
        yield
        down_fin[h, cx] = own_sum(
            lambda: down_own.at[t, s, cx], lambda r: down_z.at[r], waits
        )
        wait = link(lambda: down_fin.at[h, cx], lambda: down_fin.at[h, cx], p.x)
        yield
        wait(down_fin.at[h, nx])
        wait = link(lambda: down_fin.at[h], lambda: down_fin.at[h], p.core)
        yield
        wait(down_fin.at[nh])
        local(lambda: down_fin, lambda: down_out)
        yield

    def reduce_zyx(sent, own, core, z, y, x, fin, result):
        waits = [
            link(lambda tt=tt: sent(tt), lambda tt=tt: core.at[tt], p.core) for tt in range(2)
        ]
        yield
        for tt in range(2):
            waits[tt](core.at[tt])
            add_blocks(own.at[tt], core.at[tt], shards)
        waits = link.around(lambda b: own.at[:, b], lambda r: z.at[r])
        yield
        for wait in waits:
            wait()
        for tt in range(2):
            own[tt, s] = own_sum(lambda: own.at[tt, s], lambda r: z.at[r, tt], [lambda: None] * len(waits))
        wait = link(lambda: own.at[nt, s], lambda: y, p.y)
        yield
        wait(y)
        own[t, s] = low(wide(own.at[t, s]) + wide(y))
        yield from finish_x(own, x, fin, result)

    def reduce_yzx(sent, own, core, y, z, x, fin, result):
        waits = [
            link(lambda tt=tt: sent(tt), lambda tt=tt: core.at[tt], p.core) for tt in range(2)
        ]
        yield
        for tt in range(2):
            waits[tt](core.at[tt])
            add_blocks(own.at[tt], core.at[tt], shards)
        wait = link(lambda: own.at[nt], lambda: y, p.y)
        yield
        wait(y)
        add_blocks(own.at[t], y, shards)
        waits = link.around(lambda b: own.at[t, b], lambda r: z.at[r])
        yield
        own[t, s] = own_sum(lambda: own.at[t, s], lambda r: z.at[r], waits)
        yield from finish_x(own, x, fin, result)

    def finish_x(own, x, fin, result):
        wait = link(lambda: own.at[t, s], lambda: x, p.x)
        yield
        wait(x)
        fin[h] = low(wide(own.at[t, s]) + wide(x))
        wait = link(lambda: fin.at[h], lambda: fin.at[h], p.core)
        yield
        wait(fin.at[nh])
        local(lambda: fin, lambda: result)
        yield

    def reduce_pair(pair, pair_sent):
        sent, whole = lambda: pair_sent.at[pair], lambda: pair_both.at[pair]
        wait = link(lambda: sent().at[nh], lambda: whole().at[h], p.core)
        pair_both[pair, h] = pair_sent[pair, h]
        yield
        wait(whole().at[nh])
        wait = link(lambda: whole().at[:, :, nx], lambda: pair_x.at[pair], p.x)
        yield
        wait(pair_x.at[pair])

        def body(i):
            for tt in range(2):
                pair_both[pair, tt, i, cx] = low(
                    wide(whole().at[tt, i, cx]) + wide(pair_x.at[pair, tt, i])
                )

        each(shards, body)
        wait = link(lambda: whole().at[nt, :, cx], lambda: pair_y.at[pair], p.y)
        yield
        wait(pair_y.at[pair])

        def body_y(i):
            pair_both[pair, t, i, cx] = low(
                wide(whole().at[t, i, cx]) + wide(pair_y.at[pair, i])
            )

        each(shards, body_y)
        waits = link.around(lambda b: whole().at[t, b, cx], lambda r: pair_z.at[pair, r])
        yield
        fin = lambda: pair_fin.at[pair]
        pair_fin[pair, h, cx] = own_sum(
            lambda: whole().at[t, s, cx], lambda r: pair_z.at[pair, r], waits
        )
        wait = link(lambda: fin().at[h, cx], lambda: fin().at[h, cx], p.x)
        yield
        wait(fin().at[h, nx])
        wait = link(lambda: fin().at[h], lambda: fin().at[h], p.core)
        yield
        wait(fin().at[nh])
        for j, result in enumerate((query_out, key_out, value_out)):
            local(
                lambda j=j: fin().at[:, :, :, j * PAIR : (j + 1) * PAIR],
                lambda result=result: result.at[:, :, :, pair * PAIR : (pair + 1) * PAIR],
            )
        yield

    def reduce_vector(first, got, steps, around, finish):
        index = link.made
        wait = link(lambda: first, lambda: got.at[0], p.core)
        yield
        wait(got.at[0])
        steps[0] = first[...] + got[0]
        wait = link(lambda: steps.at[0], lambda: got.at[1], p.x)
        yield
        wait(got.at[1])
        steps[1] = steps[0] + got[1]
        wait = link(lambda: steps.at[1], lambda: got.at[2], p.y)
        yield
        wait(got.at[2])
        around[s] = steps[1] + got[2]
        waits = []
        for there, source in p.steps:
            waits.append(
                (link(lambda: around.at[s], lambda: around.at[s], (there, p.c, t)), source)
            )
        yield
        for wait, source in waits:
            wait(around.at[source])
        total = around[0]
        for at in range(1, shards):
            total = total + around[at]
        link.open.pop(index)().wait_send()
        finish(total)
        yield

    rows_of_units = 2 * units // width

    def early_done(total):
        got = early_first
        got[...] = total
        for part in range(rows_of_units // 2):
            up_bias_out[:, part * width : (part + 1) * width] = got[
                pl.ds(t * (rows_of_units // 2) + part, 1), :
            ]
        at = rows_of_units
        for result in (out_bias_out, gain_out, shift_out):
            result[...] = got[at : at + 2, :]
            at += 2

    def head_done(total):
        got = head_first
        got[...] = total
        for j in range(2):
            for pair in range(pairs):
                head_bias_out[j : j + 1, pair * PAIR : (pair + 1) * PAIR] = got[
                    pl.ds(t * 2 * pairs + j * pairs + pair, 1), :
                ]

    act = deliver(final_rows, act_out)
    inputs = deliver(input_rows, input_out)
    down = reduce_down()
    up_a = reduce_yzx(
        lambda tt: grad_sent.at[tt, :, 0], up_a_own, up_a_core, up_a_y, up_a_z, up_a_x, up_a_fin,
        up_a_out,
    )
    up_c = reduce_zyx(
        lambda tt: grad_sent.at[tt, :, 1], up_c_own, up_c_core, up_c_z, up_c_y, up_c_x, up_c_fin,
        up_c_out,
    )
    out = reduce_yzx(
        lambda tt: out_sent.at[tt], out_own, out_core, out_y, out_z, out_x, out_fin, out_out
    )
    early = reduce_vector(early_first, early_got, early_steps, early_z, early_done)
    vector = reduce_vector(head_first, head_got, head_steps, head_z, head_done)
    chain_of = [None] * pairs
    grad_waits = []

    def step(*names):
        for chain in names:
            next(chain)

    def store_parts(terms, own, sent):
        parts = terms.shape[0] // 2
        for hh in range(2):
            value = terms[hh * parts : (hh + 1) * parts]
            pl.when(h == hh)(lambda value=value: own(value))
            pl.when(h != hh)(lambda value=value: sent(value))

    x_rows, cot = part_sent, input_rows

    def rows_phase(
        w_out, w_up, w_down, mixed, active, slope, first_low, scaled, rstd, acc, turned
    ):
        loads = [
            local(lambda: mixed_ref, lambda: mixed),
            local(lambda: w_out_ref, lambda: w_out),
            local(lambda: x_ref.at[h], lambda: x_rows.at[0]),
            local(lambda: x_ref.at[2 + h], lambda: x_rows.at[1]),
            local(lambda: w_up_ref, lambda: w_up),
            local(lambda: w_down_ref, lambda: w_down),
            local(lambda: cot_ref, lambda: cot),
        ]
        for load in loads[:4]:
            load()
        blocks = [(late, slice(late * block, (late + 1) * block)) for late in range(2)]
        for late, rows in blocks:
            attn_out = over_cols(mixed[late], w_out[...]) + out_bias_ref[0:1, :]
            values, root = normalize(wide(x_rows.at[late]) + attn_out)
            scaled[late] = values
            rstd[late] = root
            first_low[rows, :] = low(values * gain_ref[0:1, :] + shift_ref[0:1, :])
        loads[4]()
        loads[5]()
        acc[...] = jnp.zeros(acc.shape, jnp.float32)
        inv_root, inv_tau = math.sqrt(0.5), 1.0 / math.sqrt(2.0 * math.pi)

        def ffn(j):
            cols = pl.ds(pl.multiple_of(j * width, width), width)
            hidden = matmul(first_low[...], w_up[:, cols]) + up_bias_ref[:, cols]
            gauss = 0.5 * (1.0 + lax.erf(hidden * inv_root))
            value = low(hidden * gauss)
            active[:, cols] = value
            slope[:, cols] = low(gauss + hidden * jnp.exp(-0.5 * hidden * hidden) * inv_tau)
            acc[...] += over_cols(value, w_down[:, cols])

        each(rows_of_units, ffn)
        loads[6]()
        gain_two = shift_two = bias_two = 0.0
        for late, rows in blocks:
            first_norm = scaled[late] * gain_ref[0:1, :] + shift_ref[0:1, :]
            values, root = normalize(first_norm + acc[rows, :] + out_bias_ref[1:2, :])
            final_rows[late] = low(values * gain_ref[1:2, :] + shift_ref[1:2, :])
            grad_final = wide(cot.at[late])
            gain_two += summed(grad_final * values)
            shift_two += summed(grad_final)
            grad_second = norm_back(grad_final, values, root, gain_ref[1:2, :])
            bias_two += summed(grad_second)
            sum_one[late] = grad_second
            grad = low(grad_second)
            flipped = jnp.transpose(grad)
            for i in range(shards):
                turned[i, :, rows] = flipped[i * 4 * quarter : (i + 1) * 4 * quarter]
        step(act)

        def store_down(tt, i, terms):
            def own(value):
                for xx in range(2):
                    down_own[tt, i, xx] = value[xx * quarter : (xx + 1) * quarter]

            def sent(value):
                for xx in range(2):
                    grad_sent[tt, i, xx] = value[xx * quarter : (xx + 1) * quarter]

            store_parts(terms, own, sent)

        def store_up(tt, i, terms):
            def own(value):
                up_a_own[tt, i] = value[:quarter]
                up_c_own[tt, i] = value[quarter:]

            def sent(value):
                for xx in range(2):
                    grad_sent[tt, i, xx] = value[xx * quarter : (xx + 1) * quarter]

            store_parts(terms, own, sent)

        def store_out(tt, i, terms):
            def own(value):
                out_own[tt, i] = value

            def sent(value):
                out_sent[tt, i] = value

            store_parts(terms, own, sent)

        def products(right, cols, store):
            for tt in range(2):
                one = slice(tt * cols, (tt + 1) * cols)
                each(
                    shards, lambda i: store(tt, i, low(matmul(turned[i], right(one))))
                )

        before = link.made
        products(lambda one: active[:, one], units, store_down)
        step(down)
        acc[...] = jnp.zeros(acc.shape, jnp.float32)

        def ffn_back(j):
            cols = pl.ds(pl.multiple_of(j * width, width), width)
            grads = low(sum_one[...]).reshape(rows_two, width)
            grad_hidden = matmul(grads, w_down[:, cols]) * wide(slope.at[:, cols])
            early_first[pl.ds(j, 1), :] = summed(grad_hidden)
            value = low(grad_hidden)
            slope[:, cols] = value
            acc[...] += over_cols(value, w_up[:, cols])

        each(rows_of_units, ffn_back)
        step(down)
        for late, rows in blocks:
            flipped = jnp.transpose(first_low[rows, :])
            for i in range(shards):
                turned[i, :, rows] = flipped[i * 4 * quarter : (i + 1) * 4 * quarter]
        for index in (before, before + 1):
            link.open.pop(index)().wait_send()
        products(lambda one: slope[:, one], units, store_up)
        step(up_c, up_a)
        gain_one = shift_one = bias_one = 0.0
        for late, rows in blocks:
            grad_first = sum_one[late] + acc[rows, :]
            gain_one += summed(grad_first * scaled[late])
            shift_one += summed(grad_first)
            grad_sum = norm_back(grad_first, scaled[late], rstd[late], gain_ref[0:1, :])
            bias_one += summed(grad_sum)
            sum_one[late] = grad_sum
            grad = low(grad_sum)
            grad_mixed[late] = low(matmul(grad, w_out[...]))
            flipped = jnp.transpose(grad)
            for i in range(shards):
                turned[i, :, rows] = flipped[i * 4 * quarter : (i + 1) * 4 * quarter]
        for pair in range(pairs):
            for late in range(2):
                there = lambda late=late, hh=h: pl.ds(
                    pl.multiple_of((2 * late + hh) * block, block), block
                )
                column = lambda hh, pair=pair: pl.ds(
                    pl.multiple_of(hh * half + pair * PAIR, PAIR), PAIR
                )
                wait = link(
                    lambda late=late, column=column: grad_mixed.at[late, :, column(nh)],
                    lambda pair=pair, there=there: grad_heads.at[pair, there(), :],
                    p.core,
                )
                grad_waits.append(
                    lambda wait=wait, pair=pair, there=there: wait(
                        grad_heads.at[pair, there(hh=nh), :]
                    )
                )
                grad_heads[pair, there(), :] = grad_mixed[late, :, column(h)]
        rows = rows_of_units
        for value in (bias_one, bias_two, gain_one, gain_two, shift_one, shift_two):
            early_first[rows : rows + 1, :] = value
            rows += 1
        if early_first.shape[0] > rows:
            early_first[rows:, :] = jnp.zeros((early_first.shape[0] - rows, width), jnp.float32)
        step(early)
        step(up_c, up_a)
        products(lambda one: jnp.concatenate([mixed[0, :, one], mixed[1, :, one]], axis=0), half, store_out)
        step(out)

    low_vmem = lambda *dims: pltpu.VMEM(dims, jnp.bfloat16)
    full_vmem = lambda *dims: pltpu.VMEM(dims, jnp.float32)
    pl.run_scoped(
        rows_phase,
        low_vmem(width, width),
        low_vmem(width, 2 * units),
        low_vmem(width, 2 * units),
        low_vmem(2, block, width),
        low_vmem(rows_two, 2 * units),
        low_vmem(rows_two, 2 * units),
        low_vmem(rows_two, width),
        full_vmem(2, block, width),
        full_vmem(2, block, 1),
        full_vmem(rows_two, width),
        low_vmem(shards, 4 * quarter, rows_two),
    )

    def heads_phase(
        qkv, wqkv, x_t, x_all, heads, dqkv, dk_acc, dv_acc, sums, input_acc, pair_sent
    ):
        loads = [
            local(lambda: x_ref, lambda: x_all),
            local(lambda: qkv_ref, lambda: qkv),
            local(lambda: heads_ref, lambda: heads),
            local(lambda: wqkv_ref, lambda: wqkv),
        ]
        loads[0]()
        for i in range(length // block):
            x_t[:, i * block : (i + 1) * block] = jnp.transpose(x_all[i])
        step(out)
        for load in loads[1:]:
            load()
        for wait in grad_waits:
            wait()

        def pair_grads(pair):
            values = jnp.concatenate([dqkv[j * pairs + pair] for j in range(3)], axis=1)
            for i in range(shards):
                terms = low(matmul(x_t[i * 4 * quarter : (i + 1) * 4 * quarter, :], values))
                for hh in range(2):
                    for xx in range(2):
                        first = (2 * hh + xx) * quarter
                        pair_sent[pair, hh, i, xx] = terms[first : first + quarter]

        def pair_inputs(pair):
            weights = jnp.concatenate(
                [
                    wqkv[:, j * half + pair * PAIR : j * half + (pair + 1) * PAIR]
                    for j in range(3)
                ],
                axis=1,
            )

            def body(i):
                rows = pl.ds(pl.multiple_of(i * block, block), block)
                terms = over_cols(
                    jnp.concatenate([dqkv[j * pairs + pair, rows, :] for j in range(3)], axis=1),
                    weights,
                )
                if pair == 0:
                    input_acc[i] = terms
                else:
                    input_acc[i] += terms

            each(length // block, body)

        part_wait, swaps = [], []

        def after(pair):
            pair_inputs(pair)
            if pair == pairs - 1:
                for late in range(2):
                    part_sent[late] = low(input_acc[2 * late + nh])
                part_wait.append(link(lambda: part_sent, lambda: part_got, p.core))
            pair_grads(pair)
            chain_of[pair] = reduce_pair(pair, pair_sent)
            swaps.append(link.made)
            step(chain_of[pair])
            if pair == 0:
                step(early, act)
            if pair == 1:
                step(chain_of[0], down, early, up_a, out)

        def attend(pair):
            attend_back_pair(
                starts_ref,
                near,
                qkv.at[pair],
                qkv.at[pairs + pair],
                qkv.at[2 * pairs + pair],
                heads.at[pair],
                grad_heads.at[pair],
                total_ref.at[pair],
                dqkv.at[pair],
                dqkv.at[pairs + pair],
                dqkv.at[2 * pairs + pair],
                sums.at[pair],
                dk_acc,
                dv_acc,
            )
            for at in range(pairs):
                pl.when(pair == at)(lambda at=at: after(at))

        each(pairs, attend)
        head_first[...] = jnp.zeros(head_first.shape, jnp.float32)
        for row in range(2 * pairs):
            kind = row // pairs
            head_first[pl.ds(h * 2 * pairs + row, 1), :] = sums[row % pairs, kind : kind + 1, :]
        part_wait[0](part_got)
        for late in range(2):
            input_rows[late] = low(
                sum_one[late] + input_acc[2 * late + h] + wide(part_got.at[late])
            )
        for index in swaps:
            link.open.pop(index)().wait_send()

    pl.run_scoped(
        heads_phase,
        low_vmem(3 * pairs, length, PAIR),
        low_vmem(width, 3 * half),
        low_vmem(width, length),
        low_vmem(length // block, block, width),
        low_vmem(pairs, length, PAIR),
        low_vmem(3 * pairs, length, PAIR),
        full_vmem(length, PAIR),
        full_vmem(length, PAIR),
        full_vmem(pairs, 2, PAIR),
        full_vmem(length // block, block, width),
        low_vmem(pairs, 2, shards, 2, quarter, 3 * PAIR),
    )

    first, second, third = chain_of
    step(inputs, vector, third, second, down)
    step(first, vector, early, up_c, up_a, out)
    step(third, second, inputs, vector)
    step(first, down, up_c, up_a, out)
    step(third, second, vector)
    step(first, down, up_c, out, up_a)
    step(third, second, first, down)
    step(third, second, first, up_c)
    step(third, second)
    step(vector, early, act, inputs)
    for chain in chain_of + [down, up_a, up_c, out, early, vector, act, inputs]:
        for _ in chain:
            pass
    link.sent()
    local.finish()


def backward(
    shards,
    starts,
    totals,
    up_bias,
    out_biases,
    norm_gains,
    norm_shifts,
    mixed,
    x,
    cot,
    w_out,
    w_up,
    w_down,
    qkv,
    wqkv,
    heads,
):
    seq_dev, block, width = x.shape
    length = seq_dev * block
    pairs = heads.shape[0]
    half = pairs * PAIR
    quarter = width // shards // 4
    w_out = w_out.reshape(width, -1)
    w_up = w_up.reshape(width, -1)
    w_down = w_down.reshape(width, -1)
    units = w_up.shape[1] // 2
    low_type, full_type = jnp.bfloat16, jnp.float32
    shape = jax.ShapeDtypeStruct
    vmem = pl.BlockSpec(memory_space=pltpu.VMEM)
    anywhere = pl.BlockSpec(memory_space=pl.ANY)
    scratch = lambda *dims: pltpu.VMEM(dims, low_type)
    full = lambda *dims: pltpu.VMEM(dims, full_type)
    around = shards - 1
    early_rows = -(-(2 * units // width + 6) // 8) * 8
    copies = 64 + 10 * around
    head_grad = shape((2, 2, quarter, half), low_type)
    return pl.pallas_call(
        lambda *refs: backward_kernel(shards, *refs),
        in_specs=[pl.BlockSpec(memory_space=pltpu.SMEM)] + [vmem] * 5 + [anywhere] * 9,
        out_specs=[anywhere] * 9 + [vmem] * 5,
        out_shape=[
            shape((seq_dev, block, width), low_type),
            shape((seq_dev, block, width), low_type),
            shape((2, 2, quarter, units), low_type),
            shape((2, quarter, units), low_type),
            shape((2, quarter, units), low_type),
            shape((2, 2 * quarter, half), low_type),
            head_grad,
            head_grad,
            head_grad,
            shape((1, units), full_type),
            shape((2, width), full_type),
            shape((2, width), full_type),
            shape((2, width), full_type),
            shape((2, half), full_type),
        ],
        scratch_shapes=[
            scratch(pairs, length, PAIR),
            scratch(2, block, width),
            full(2, block, width),
            scratch(2, block, width),
            scratch(2, block, width),
            scratch(2, block, width),
            scratch(2, block, width),
            scratch(2, shards, 2, quarter, units),
            scratch(2, shards, 2, quarter, units),
            scratch(2, shards, 2, quarter, units),
            scratch(2, shards, quarter, units),
            scratch(shards, quarter, units),
            scratch(around, quarter, units),
            scratch(2, 2, quarter, units),
            scratch(2, shards, quarter, units),
            scratch(2, shards, quarter, units),
            scratch(shards, quarter, units),
            scratch(around, quarter, units),
            scratch(quarter, units),
            scratch(2, quarter, units),
            scratch(2, shards, quarter, units),
            scratch(2, shards, quarter, units),
            scratch(around, 2, quarter, units),
            scratch(quarter, units),
            scratch(quarter, units),
            scratch(2, quarter, units),
            scratch(2, shards, 2 * quarter, half),
            scratch(2, shards, 2 * quarter, half),
            scratch(2, shards, 2 * quarter, half),
            scratch(shards, 2 * quarter, half),
            scratch(around, 2 * quarter, half),
            scratch(2 * quarter, half),
            scratch(2, 2 * quarter, half),
            scratch(pairs, 2, shards, 2, quarter, 3 * PAIR),
            scratch(pairs, 2, shards, quarter, 3 * PAIR),
            scratch(pairs, shards, quarter, 3 * PAIR),
            scratch(pairs, around, quarter, 3 * PAIR),
            scratch(pairs, 2, 2, quarter, 3 * PAIR),
            full(early_rows, width),
            full(2, early_rows, width),
            full(3, early_rows, width),
            full(shards, early_rows, width),
            full(4 * pairs, PAIR),
            full(2, 4 * pairs, PAIR),
            full(3, 4 * pairs, PAIR),
            full(shards, 4 * pairs, PAIR),
            pltpu.SemaphoreType.DMA((copies,)),
            pltpu.SemaphoreType.DMA((copies,)),
            pltpu.SemaphoreType.DMA((20 + 3 * pairs,)),
        ],
        compiler_params=pltpu.CompilerParams(
            collective_id=2, has_side_effects=True, vmem_limit_bytes=67_043_328
        ),
    )(
        starts,
        totals,
        up_bias.reshape(1, -1),
        out_biases,
        norm_gains,
        norm_shifts,
        mixed,
        x,
        cot,
        w_out,
        w_up,
        w_down,
        qkv,
        wqkv.reshape(width, 3 * half),
        heads,
    )


def make_local(shards, ctxs, tps):
    def local(
        tokens,
        starts,
        w_query,
        w_key,
        w_value,
        w_out,
        w_up,
        w_down,
        head_bias,
        up_bias,
        out_biases,
        norm_gains,
        norm_shifts,
        cotangent,
    ):
        seq_dev, block, width = tokens.shape
        assert ctxs == 4 and tps == 2 and seq_dev == 4 and block == BLOCK
        rows_own = w_query.shape[0]
        (
            x_blocks,
            cot_rows,
            wqkv,
            qkv,
            mixed_heads,
            mixed_rows,
            totals,
            out_full,
            up_full,
            down_full,
            up_bias_full,
        ) = forward(
            shards,
            starts,
            (w_query, w_key, w_value, w_out, w_up, w_down),
            head_bias,
            up_bias.reshape(1, -1),
            tokens,
            cotangent,
        )
        (
            activations,
            input_grad,
            grad_down,
            grad_up_a,
            grad_up_c,
            grad_out,
            grad_query,
            grad_key,
            grad_value,
            grad_up_bias,
            grad_out_biases,
            grad_gains,
            grad_shifts,
            grad_head_bias,
        ) = backward(
            shards,
            starts,
            totals,
            up_bias_full,
            out_biases,
            norm_gains,
            norm_shifts,
            mixed_rows,
            x_blocks,
            cot_rows,
            out_full,
            up_full,
            down_full,
            qkv,
            wqkv,
            mixed_heads,
        )
        whole = lambda grad: grad.reshape(rows_own, -1).astype(jnp.float32)
        return (
            activations,
            input_grad.astype(jnp.float32),
            whole(grad_query),
            whole(grad_key),
            whole(grad_value),
            whole(grad_out),
            whole(jnp.stack([grad_up_a, grad_up_c], axis=1)),
            whole(grad_down),
            grad_head_bias,
            grad_up_bias.reshape(-1),
            grad_out_biases,
            grad_gains,
            grad_shifts,
        )

    return local


def solution(mesh):
    sizes = [mesh.shape[name] for name in AXES]
    return jax.shard_map(
        make_local(*sizes),
        mesh=mesh,
        in_specs=(
            P("shard", "ctx", None),
            P("shard", None),
            P("shard", "tp"),
            P("shard", "tp"),
            P("shard", "tp"),
            P("shard", "tp"),
            P("shard", "tp"),
            P("shard", "tp"),
            P(None, "tp"),
            P("tp"),
            P(),
            P(),
            P(),
            P("shard", "ctx", None),
        ),
        out_specs=(
            P("shard", "ctx", None),
            P("shard", "ctx", None),
            P("shard", "tp"),
            P("shard", "tp"),
            P("shard", "tp"),
            P("shard", "tp"),
            P("shard", "tp"),
            P("shard", "tp"),
            P(None, "tp"),
            P("tp"),
            P(),
            P(),
            P(),
        ),
        check_vma=False,
    )
```

```python
import math

import jax
import jax.numpy as jnp
from jax import lax
from jax.experimental import pallas as pl
from jax.experimental.pallas import tpu as pltpu
from jax.sharding import PartitionSpec as P

HEAD = 64
PIECE = 256
BLOCK = 256
PAIR = 128

norm_eps = 1e-05
masked_score = -1e30
AXES = ("shard", "ctx", "tp")


def matmul(former, latter):
    return jnp.dot(former, latter, preferred_element_type=jnp.float32)


def over_rows(former, latter):
    return lax.dot_general(
        former, latter, (((0,), (0,)), ((), ())), preferred_element_type=jnp.float32
    )


def over_cols(former, latter):
    return lax.dot_general(
        former, latter, (((1,), (1,)), ((), ())), preferred_element_type=jnp.float32
    )


def low(values):
    return values.astype(jnp.bfloat16)


def normalize(values):
    centre = jnp.mean(values, axis=-1, keepdims=True)
    centred = values - centre
    spread = jnp.mean(centred * centred, axis=-1, keepdims=True)
    scaling = lax.rsqrt(spread + norm_eps)
    return (centred * scaling, scaling)


def norm_back(grad_out, scaled, scaling, gain_row):
    grad_scaled = grad_out * gain_row
    mean_grad = jnp.mean(grad_scaled, axis=-1, keepdims=True)
    mean_along = jnp.mean(grad_scaled * scaled, axis=-1, keepdims=True)
    return scaling * (grad_scaled - mean_grad - scaled * mean_along)


def edge_mask(starts_ref, seq, key_first, query_first, keys_first):
    key_shape = (BLOCK, 1) if keys_first else (1, BLOCK)
    query_shape = (1, BLOCK) if keys_first else (BLOCK, 1)
    key_at = key_first + lax.broadcasted_iota(jnp.int32, key_shape, 0 if keys_first else 1)
    query_at = query_first + lax.broadcasted_iota(jnp.int32, query_shape, 1 if keys_first else 0)
    seen = key_at <= query_at
    for piece in range(2):
        start = starts_ref[seq, piece]
        key_in = (key_at >= start) & (key_at < start + PIECE)
        query_in = (query_at >= start) & (query_at < start + PIECE)
        seen = seen | (key_in & query_in)
    return seen


def two_heads(rows):
    lane = lax.broadcasted_iota(jnp.int32, rows.shape, 1)
    zero = jnp.zeros_like(rows)
    return jnp.concatenate(
        [jnp.where(lane < HEAD, rows, zero), jnp.where(lane >= HEAD, rows, zero)], axis=0
    )


def join_heads(rows):
    half = rows.shape[0] // 2
    lane = lax.broadcasted_iota(jnp.int32, (half, rows.shape[1]), 1)
    return jnp.where(lane < HEAD, rows[:half], rows[half:])


def attend_pair(starts_ref, seq, q_ref, k_ref, v_ref, mixed_ref, total_ref):
    length = q_ref.shape[0]
    blocks = length // BLOCK
    for at in range(blocks):
        rows = slice(at * BLOCK, (at + 1) * BLOCK)
        reach = min(blocks, at + 2)
        queries = two_heads(q_ref[rows, :])
        scores = []
        for key_at in range(reach):
            part = over_cols(queries, k_ref[key_at * BLOCK : (key_at + 1) * BLOCK, :])
            if key_at >= at:
                seen = edge_mask(starts_ref, seq, key_at * BLOCK, at * BLOCK, False)
                seen = jnp.concatenate([seen, seen], axis=0)
                part = jnp.where(seen, part, masked_score)
            scores.append(part)
        scores = jnp.concatenate(scores, axis=1)
        top = jnp.max(scores, axis=1, keepdims=True)
        raised = jnp.exp(scores - top)
        total = jnp.sum(raised, axis=1, keepdims=True)
        mixed = matmul(low(raised), v_ref[: reach * BLOCK, :]) / total
        mixed_ref[rows, :] = low(join_heads(mixed))
        wide = jnp.broadcast_to(top + jnp.log(total), (2 * BLOCK, PAIR))
        row = jnp.transpose(wide)[0:1, :]
        total_ref[0:1, rows] = row[:, :BLOCK]
        total_ref[1:2, rows] = row[:, BLOCK:]


class Copies:
    def __init__(self):
        self.sent = []

    def start(self, when, make):
        self.sent.append((when, make))
        if when is None:
            make().start()
        else:
            pl.when(when)(lambda: make().start())

    def finish(self):
        for when, make in self.sent:
            if when is None:
                make().wait_send()
            else:
                pl.when(when)(lambda make=make: make().wait_send())


def both(former, latter):
    if former is None:
        return latter
    return former if latter is None else former & latter


def arrive(when, region, sem, device):
    def wait():
        pltpu.make_async_remote_copy(
            src_ref=region,
            dst_ref=region,
            send_sem=sem,
            recv_sem=sem,
            device_id=device,
            device_id_type=pl.DeviceIdType.MESH,
        ).wait_recv()

    if when is None:
        wait()
    else:
        pl.when(when)(wait)


class Place:
    def __init__(self, shards):
        self.shards = shards
        self.s = lax.axis_index("shard")
        self.c = lax.axis_index("ctx")
        self.t = lax.axis_index("tp")
        self.h = lax.rem(self.c, 2)
        self.cx = lax.div(self.c, 2)
        self.core = (self.s, self.c + 1 - 2 * self.h, self.t)
        self.x = (self.s, self.c + 2 - 4 * self.cx, self.t)
        self.y = (self.s, self.c, 1 - self.t)
        self.up = (self.s + 1, self.c, self.t)
        self.down = (self.s - 1, self.c, self.t)
        self.nh, self.nx, self.nt = 1 - self.h, 1 - self.cx, 1 - self.t
        self.steps = [
            (lax.rem(self.s + r, shards), lax.rem(self.s + shards - r, shards))
            for r in range(1, shards)
        ]
        self.has_up = self.s < shards - 1
        self.has_down = self.s > 0

    def enter(self, whole_line):
        barrier = pltpu.get_barrier_semaphore()

        def greet(device):
            pl.semaphore_signal(
                barrier, inc=1, device_id=device, device_id_type=pl.DeviceIdType.MESH
            )

        for device in (self.core, self.x, self.y):
            greet(device)
        if whole_line:
            for there, _ in self.steps:
                greet((there, self.c, self.t))
            pl.semaphore_wait(barrier, 3 + len(self.steps))
            return
        pl.when(self.has_up)(lambda: greet(self.up))
        pl.when(self.has_down)(lambda: greet(self.down))
        vertical = jnp.where(self.has_up, 1, 0) + jnp.where(self.has_down, 1, 0)
        pl.semaphore_wait(barrier, 3 + vertical)

    def ring(self, k):
        if k == 0:
            return [(None, self.s)]
        return [(self.s - k >= 0, self.s - k), (self.s + k < self.shards, self.s + k)]


class Gather:
    def __init__(self, place, copies, sems, row, here, first, relayed, wanted):
        self.place, self.copies, self.row = place, copies, row
        self.sems, self.here, self.first = sems, here, first
        self.relayed, self.wanted = relayed, wanted

    def copy(self, kind, index, source, target, device):
        send, recv = self.sems
        return pltpu.make_async_remote_copy(
            src_ref=source,
            dst_ref=target,
            send_sem=send.at[self.row, kind, index],
            recv_sem=recv.at[self.row, 0 if kind < 2 else kind - 1, index],
            device_id=device,
            device_id_type=pl.DeviceIdType.MESH,
        )

    def source(self, k, block):
        return self.first if k == 0 else self.here(block, self.place.t)

    def z_send(self, k):
        p = self.place
        (under, below), *rest = p.ring(k - 1)
        over, above = rest[0] if rest else (under, below)
        self.copies.start(
            both(under, p.has_up),
            lambda: self.copy(0, below, self.source(k - 1, below), self.here(below, p.t), p.up),
        )
        self.copies.start(
            both(over, p.has_down),
            lambda: self.copy(1, above, self.source(k - 1, above), self.here(above, p.t), p.down),
        )

    def send(self, kind, k, region, device):
        for when, block in self.place.ring(k):
            self.copies.start(
                when,
                lambda block=block: self.copy(
                    kind, block, region(block, k), region(block, None), device
                ),
            )

    def wait(self, stage, k, region, device):
        for when, block in self.place.ring(k):
            arrive(when, region(block), self.sems[1].at[self.row, stage, block], device)

    def z(self, k):
        p = self.place
        if k > 0:
            self.wait(0, k, lambda b: self.here(b, p.t), p.y)
        if k + 1 < p.shards:
            self.z_send(k + 1)
        self.send(
            2,
            k,
            lambda b, at: (self.source(0, b) if at == 0 else self.here(b, p.t)).at[p.cx],
            p.y,
        )

    def y(self, k):
        p = self.place
        self.wait(1, k, lambda b: self.here(b, p.nt).at[p.cx], p.y)
        self.send(3, k, lambda b, at: self.here(b, p.nt).at[p.cx], p.x)

    def x(self, k):
        p = self.place
        self.wait(2, k, lambda b: self.here(b, p.nt).at[p.nx], p.x)
        self.send(4, k, lambda b, at: self.relayed(b), p.core)

    def core(self, k):
        self.wait(3, k, self.wanted, self.place.core)


def forward_kernel(
    shards,
    starts_ref,
    wq_ref,
    wk_ref,
    wv_ref,
    wo_ref,
    wu_ref,
    wd_ref,
    head_bias_ref,
    up_bias_ref,
    tokens_ref,
    cot_ref,
    x_ref,
    cot_rows_ref,
    wqkv_ref,
    qkv_ref,
    heads_ref,
    rows_ref,
    total_ref,
    out_ref,
    up_ref,
    down_ref,
    up_bias_out,
    x_all,
    wg,
    qkv,
    mixed,
    wo_low,
    wu_low,
    wd_low,
    bias_all,
    send,
    recv,
    token_send,
    token_recv,
    local_sem,
):
    p = Place(shards)
    copies = Copies()
    half = wq_ref.shape[1]
    quarter = wg.shape[4]
    units = wu_ref.shape[1]
    seq_of = lambda cx, t: 2 * cx + t
    seq = seq_of(p.cx, p.t)
    seq_far = seq_of(1 - p.cx, p.t)
    far = 2 * (1 - p.cx) + p.h
    peer = p.c + 1 - 2 * p.h
    locals_ = []

    def local(source, target):
        copy = pltpu.make_async_copy(source, target, local_sem.at[len(locals_)])
        copy.start()
        locals_.append(copy)
        return copy

    def remote(index, source, target, device):
        return pltpu.make_async_remote_copy(
            src_ref=source,
            dst_ref=target,
            send_sem=token_send.at[index],
            recv_sem=token_recv.at[index],
            device_id=device,
            device_id_type=pl.DeviceIdType.MESH,
        )

    own_tokens = local(tokens_ref.at[seq], x_all.at[p.c])
    cot_own = local(cot_ref.at[seq], cot_rows_ref.at[p.cx])
    for third, ref in enumerate((wq_ref, wk_ref, wv_ref)):
        for hh in range(2):
            for xx in range(2):
                first = (2 * hh + xx) * quarter
                wg[p.t, p.s, hh, xx, :, third * half : (third + 1) * half] = low(
                    ref[first : first + quarter, :]
                )
    p.enter(False)
    copies.start(None, lambda: remote(0, tokens_ref.at[seq_far], x_all.at[p.c], p.x))
    copies.start(None, lambda: remote(1, tokens_ref.at[seq], x_all.at[p.c], p.core))
    sems = (send, recv)
    attn = Gather(
        p,
        copies,
        sems,
        0,
        lambda b, t: wg.at[t, b, p.h],
        wg.at[p.t, p.s, p.h],
        lambda b: wg.at[p.nh, b, p.h],
        lambda b: wg.at[p.h, b, p.nh],
    )
    attn.z(0)
    copies.start(None, lambda: remote(2, head_bias_ref, bias_all.at[p.t], p.y))
    bias_all[p.t] = head_bias_ref[...]
    up_bias_out[p.t] = up_bias_ref[...].reshape(1, units)
    copies.start(None, lambda: remote(3, up_bias_out.at[p.t], up_bias_out.at[p.t], p.y))

    def cast(source, target):
        for hh in range(2):
            for xx in range(2):
                first = (2 * hh + xx) * quarter
                target[hh, xx] = low(source[first : first + quarter, :])

    cols = lambda t, n: pl.ds(pl.multiple_of(t * n, 128), n)
    own_weights = []
    gathers = []
    for row, (full_ref, ref, source, n) in enumerate(
        (
            (wo_ref, out_ref, wo_low, half),
            (wu_ref, up_ref, wu_low, units),
            (wd_ref, down_ref, wd_low, units),
        )
    ):
        cast(full_ref, source)
        own_weights.append(local(source.at[p.h], ref.at[p.s, p.h, :, :, cols(p.t, n)]))
        gathers.append(
            Gather(
                p,
                copies,
                sems,
                row + 1,
                lambda b, t, ref=ref, n=n: ref.at[b, p.h, :, :, cols(t, n)],
                source.at[p.h],
                lambda b, ref=ref: ref.at[b, p.h],
                lambda b, ref=ref: ref.at[b, p.nh],
            )
        )
        if row == 0:
            gathers[0].z(0)
    out, up, down = gathers

    far_block = x_all.at[far]
    arrive(None, far_block, token_recv.at[0], p.x)
    copies.start(None, lambda: remote(4, far_block, far_block, p.core))

    attn.z(1)
    out.z(1)
    attn.y(0)
    attn.z(2)
    out.z(2)
    attn.y(1)
    attn.x(0)
    up.z(0)
    for k in range(3, shards):
        attn.z(k)
        out.z(k)
        attn.y(k - 1)
        attn.x(k - 2)
    down.z(0)
    attn.y(shards - 1)
    attn.x(shards - 2)
    attn.x(shards - 1)
    copies.start(None, lambda: remote(5, cot_ref.at[seq_far], cot_rows_ref.at[p.cx], p.x))
    for copy in own_weights:
        copy.wait()
    up.z(1)
    for k in range(shards):
        out.y(k)
    for k in range(shards):
        attn.core(k)
    own_tokens.wait()
    peer_far = 2 * (1 - p.cx) + 1 - p.h
    arrive(None, x_all.at[peer], token_recv.at[1], p.core)
    arrive(None, x_all.at[peer_far], token_recv.at[4], p.core)
    arrive(None, bias_all.at[1 - p.t], token_recv.at[2], p.y)
    local(x_all, x_ref)
    local(wg.at[p.h], wqkv_ref)

    weights = wg[p.h].reshape(shards * 4 * quarter, 3 * half)
    bias = bias_all[p.h]
    scale = 1.0 / math.sqrt(HEAD)
    pairs = half // PAIR

    def project(at, carry):
        result = matmul(x_all[at], weights)
        rows = pl.ds(pl.multiple_of(at * BLOCK, BLOCK), BLOCK)
        for j in range(3 * pairs):
            part = result[:, j * PAIR : (j + 1) * PAIR]
            if j < pairs:
                part = low(part + bias[0:1, j * PAIR : (j + 1) * PAIR])
                part = low(part.astype(jnp.float32) * scale)
            elif j < 2 * pairs:
                part = low(part)
            else:
                column = (j - 2 * pairs) * PAIR
                part = low(part + bias[1:2, column : column + PAIR])
            qkv[j, rows, :] = part
        return carry

    lax.fori_loop(0, x_all.shape[0], project, 0)
    local(qkv, qkv_ref)

    def on_the_way(stage):
        if stage == 0:
            down.z(1)
            up.y(0)
            up.y(1)
            up.z(2)
            up.x(0)
        if stage == 1:
            down.y(0)
            down.y(1)
            down.z(2)
            up.y(2)
            up.x(1)
            down.x(0)
            for k in range(shards):
                out.x(k)

    def attend(pair, carry):
        attend_pair(
            starts_ref,
            seq,
            qkv.at[pair],
            qkv.at[pairs + pair],
            qkv.at[2 * pairs + pair],
            mixed.at[pair],
            total_ref.at[pair],
        )
        return carry

    lax.fori_loop(0, 1, attend, 0)
    on_the_way(0)
    lax.fori_loop(1, 2, attend, 0)
    on_the_way(1)
    lax.fori_loop(2, pairs, attend, 0)

    def heads_of(late, hh, pair):
        column = pl.multiple_of(hh * half + pair * PAIR, PAIR)
        return rows_ref.at[late, :, pl.ds(column, PAIR)]

    for pair in range(pairs):
        for late in range(2):
            block = 2 * late + 1 - p.h
            index = 6 + 2 * pair + late
            rows = pl.ds(pl.multiple_of(block * BLOCK, BLOCK), BLOCK)
            copies.start(
                None,
                lambda index=index, pair=pair, rows=rows, late=late: remote(
                    index, mixed.at[pair, rows, :], heads_of(late, p.h, pair), p.core
                ),
            )
    for pair in range(pairs):
        local(mixed.at[pair], heads_ref.at[pair])
        for late in range(2):
            rows = pl.ds(pl.multiple_of((2 * late + p.h) * BLOCK, BLOCK), BLOCK)
            local(mixed.at[pair, rows, :], heads_of(late, p.h, pair))

    for k in range(3, shards):
        up.z(k)
        up.x(k - 1)
        down.y(k - 1)
        up.y(k)
        down.x(k - 2)
        down.z(k)
    up.x(shards - 1)
    down.x(shards - 2)
    down.y(shards - 1)
    down.x(shards - 1)
    for array in gathers:
        for k in range(shards):
            array.core(k)
    for pair in range(pairs):
        for late in range(2):
            index = 6 + 2 * pair + late
            arrive(None, heads_of(late, 1 - p.h, pair), token_recv.at[index], p.core)
    arrive(None, up_bias_out.at[1 - p.t], token_recv.at[3], p.y)
    arrive(None, cot_rows_ref.at[1 - p.cx], token_recv.at[5], p.x)
    copies.finish()
    for copy in locals_:
        if all(copy is not done for done in [own_tokens] + own_weights):
            copy.wait()


def forward(shards, starts, weights, head_bias, up_bias, tokens, cotangent):
    w_query, w_out, w_up = weights[0], weights[3], weights[4]
    seq_dev, block, width = tokens.shape
    rows_own, half = w_query.shape
    units = w_up.shape[1]
    quarter = rows_own // 4
    pairs = half // PAIR
    length = seq_dev * block
    low_type, full_type = jnp.bfloat16, jnp.float32
    shape = jax.ShapeDtypeStruct
    vmem = pl.BlockSpec(memory_space=pltpu.VMEM)
    anywhere = pl.BlockSpec(memory_space=pl.ANY)
    return pl.pallas_call(
        lambda *refs: forward_kernel(shards, *refs),
        in_specs=[pl.BlockSpec(memory_space=pltpu.SMEM)] + [vmem] * 8 + [anywhere] * 2,
        out_specs=[anywhere] * 6 + [vmem] + [anywhere] * 3 + [vmem],
        out_shape=[
            shape((seq_dev, block, width), low_type),
            shape((2, block, width), low_type),
            shape((shards, 2, 2, quarter, 3 * half), low_type),
            shape((3 * pairs, length, PAIR), low_type),
            shape((pairs, length, PAIR), low_type),
            shape((2, block, 2 * half), low_type),
            shape((pairs, 2, length), full_type),
            shape((shards, 2, 2, quarter, 2 * half), low_type),
            shape((shards, 2, 2, quarter, 2 * units), low_type),
            shape((shards, 2, 2, quarter, 2 * units), low_type),
            shape((2, 1, units), full_type),
        ],
        scratch_shapes=[
            pltpu.VMEM((seq_dev, block, width), low_type),
            pltpu.VMEM((2, shards, 2, 2, quarter, 3 * half), low_type),
            pltpu.VMEM((3 * pairs, length, PAIR), low_type),
            pltpu.VMEM((pairs, length, PAIR), low_type),
            pltpu.VMEM((2, 2, quarter, half), low_type),
            pltpu.VMEM((2, 2, quarter, units), low_type),
            pltpu.VMEM((2, 2, quarter, units), low_type),
            pltpu.VMEM((2, 2, half), full_type),
            pltpu.SemaphoreType.DMA((4, 5, shards)),
            pltpu.SemaphoreType.DMA((4, 4, shards)),
            pltpu.SemaphoreType.DMA((6 + 2 * pairs,)),
            pltpu.SemaphoreType.DMA((6 + 2 * pairs,)),
            pltpu.SemaphoreType.DMA((8 + 3 * pairs,)),
        ],
        compiler_params=pltpu.CompilerParams(
            collective_id=1, has_side_effects=True, vmem_limit_bytes=60 * 1024 * 1024
        ),
    )(starts, *weights, head_bias, up_bias, tokens, cotangent)


def attend_back_pair(
    starts_ref, seq, q_ref, k_ref, v_ref, mixed_ref, grad_ref, total_ref, dq_ref, dk_ref, dv_ref,
    sums_ref, dk_acc, dv_acc
):
    length = q_ref.shape[0]
    blocks = length // BLOCK
    query_sum = jnp.zeros((1, PAIR), jnp.float32)
    for at in range(blocks):
        rows = slice(at * BLOCK, (at + 1) * BLOCK)
        reach = min(blocks, at + 2)
        span = slice(0, reach * BLOCK)
        queries = two_heads(q_ref[rows, :])
        grads = two_heads(grad_ref[rows, :])
        along = grad_ref[rows, :].astype(jnp.float32) * mixed_ref[rows, :].astype(jnp.float32)
        along = jnp.transpose(along)
        inner = jnp.concatenate(
            [
                jnp.sum(along[:HEAD], axis=0, keepdims=True),
                jnp.sum(along[HEAD:], axis=0, keepdims=True),
            ],
            axis=1,
        )
        total = jnp.concatenate([total_ref[0:1, rows], total_ref[1:2, rows]], axis=1)
        scores = []
        for key_at in range(reach):
            part = over_cols(k_ref[key_at * BLOCK : (key_at + 1) * BLOCK, :], queries)
            if key_at >= at:
                seen = edge_mask(starts_ref, seq, key_at * BLOCK, at * BLOCK, True)
                seen = jnp.concatenate([seen, seen], axis=1)
                part = jnp.where(seen, part, masked_score)
            scores.append(part)
        probs = jnp.exp(jnp.concatenate(scores, axis=0) - total)
        grad_probs = over_cols(v_ref[span, :], grads)
        grad_scores = low(probs * (grad_probs - inner))
        dv = matmul(low(probs), grads)
        dk = matmul(grad_scores, queries)
        if at == 0:
            dv_acc[span, :] = dv
            dk_acc[span, :] = dk
        elif at + 1 == blocks:
            dv_acc[span, :] += dv
            dk_acc[span, :] += dk
        else:
            old = slice(0, (reach - 1) * BLOCK)
            fresh = slice((reach - 1) * BLOCK, reach * BLOCK)
            dv_acc[old, :] += dv[old, :]
            dk_acc[old, :] += dk[old, :]
            dv_acc[fresh, :] = dv[fresh, :]
            dk_acc[fresh, :] = dk[fresh, :]
        dq = join_heads(over_rows(grad_scores, k_ref[span, :])) * (1.0 / math.sqrt(HEAD))
        query_sum += jnp.sum(dq, axis=0, keepdims=True)
        dq_ref[rows, :] = low(dq)
    dk_ref[...] = low(dk_acc[...])
    dv_ref[...] = low(dv_acc[...])
    sums_ref[0:1, :] = query_sum
    sums_ref[1:2, :] = jnp.sum(dv_acc[...], axis=0, keepdims=True)


class Links:
    def __init__(self, place, send, recv):
        self.place, self.send, self.recv = place, send, recv
        self.made, self.open = 0, {}

    def __call__(self, source, target, device):
        index = self.made
        self.made += 1
        self.open[index] = lambda: pltpu.make_async_remote_copy(
            src_ref=source(),
            dst_ref=target(),
            send_sem=self.send.at[index],
            recv_sem=self.recv.at[index],
            device_id=device,
            device_id_type=pl.DeviceIdType.MESH,
        )
        self.open[index]().start()
        return lambda region: arrive(None, region, self.recv.at[index], device)

    def around(self, source, target):
        p = self.place
        waits = []
        for r, (there, _) in enumerate(p.steps):
            wait = self(
                lambda there=there: source(there), lambda r=r: target(r), (there, p.c, p.t)
            )
            waits.append(lambda wait=wait, r=r: wait(target(r)))
        return waits

    def sent(self, since=0):
        for index in sorted(self.open):
            if index >= since:
                self.open.pop(index)().wait_send()


class Locals:
    def __init__(self, sems):
        self.sems, self.made, self.open = sems, 0, {}

    def __call__(self, source, target):
        index = self.made
        self.made += 1
        self.open[index] = lambda: pltpu.make_async_copy(source(), target(), self.sems.at[index])
        self.open[index]().start()
        return lambda: self.open.pop(index)().wait()

    def finish(self):
        for index in sorted(self.open):
            self.open.pop(index)().wait()


def wide(ref):
    return ref[...].astype(jnp.float32)


def each(count, body):
    def turn(i, carry):
        body(i)
        return carry

    lax.fori_loop(0, count, turn, 0)


def add_blocks(target, other, count):
    def body(i):
        target[i] = low(wide(target.at[i]) + wide(other.at[i]))

    each(count, body)


def summed(rows):
    return jnp.sum(rows, axis=0, keepdims=True)


def backward_kernel(
    shards,
    starts_ref,
    total_ref,
    up_bias_ref,
    out_bias_ref,
    gain_ref,
    shift_ref,
    mixed_ref,
    x_ref,
    cot_ref,
    w_out_ref,
    w_up_ref,
    w_down_ref,
    qkv_ref,
    wqkv_ref,
    heads_ref,
    act_out,
    input_out,
    down_out,
    up_a_out,
    up_c_out,
    out_out,
    query_out,
    key_out,
    value_out,
    up_bias_out,
    out_bias_out,
    gain_out,
    shift_out,
    head_bias_out,
    grad_heads,
    grad_mixed,
    sum_one,
    final_rows,
    input_rows,
    part_sent,
    part_got,
    grad_sent,
    down_own,
    down_core,
    down_x,
    down_y,
    down_z,
    down_fin,
    up_a_own,
    up_a_core,
    up_a_y,
    up_a_z,
    up_a_x,
    up_a_fin,
    up_c_own,
    up_c_core,
    up_c_z,
    up_c_y,
    up_c_x,
    up_c_fin,
    out_sent,
    out_own,
    out_core,
    out_y,
    out_z,
    out_x,
    out_fin,
    pair_both,
    pair_x,
    pair_y,
    pair_z,
    pair_fin,
    early_first,
    early_steps,
    early_got,
    early_z,
    head_first,
    head_steps,
    head_got,
    head_z,
    send,
    recv,
    local_sem,
):
    p = Place(shards)
    link = Links(p, send, recv)
    local = Locals(local_sem)
    h, cx, t, s = p.h, p.cx, p.t, p.s
    nh, nx, nt = p.nh, p.nx, p.nt
    pairs, length = grad_heads.shape[0], grad_heads.shape[1]
    half = pairs * PAIR
    block, width = input_rows.shape[1], input_rows.shape[2]
    quarter, units = down_own.shape[3], down_own.shape[4]
    rows_two = 2 * block
    seq_of = lambda cx_, t_: 2 * cx_ + t_
    near, far = seq_of(cx, t), seq_of(nx, t)
    near_y, far_y = seq_of(cx, nt), seq_of(nx, nt)
    p.enter(True)

    def deliver(source, target):
        local(lambda: source.at[cx], lambda: target.at[near])
        wait_y = link(lambda: source.at[cx], lambda: target.at[near], p.y)
        wait_x = link(lambda: source.at[nx], lambda: target.at[near], p.x)
        yield
        wait_x(target.at[far])
        wait_far = link(lambda: target.at[far], lambda: target.at[far], p.y)
        yield
        wait_y(target.at[near_y])
        wait_far(target.at[far_y])
        yield

    def own_sum(first, later, waits):
        total = wide(first())
        for r, wait in enumerate(waits):
            wait()
            total = total + wide(later(r))
        return low(total)

    def reduce_down():
        waits = [
            link(lambda tt=tt: grad_sent.at[tt], lambda tt=tt: down_core.at[tt], p.core)
            for tt in range(2)
        ]
        yield
        for tt in range(2):
            waits[tt](down_core.at[tt])
            add_blocks(down_own.at[tt], down_core.at[tt], shards)
        wait = link(lambda: down_own.at[:, :, nx], lambda: down_x, p.x)
        yield
        wait(down_x)

        def body(i):
            for tt in range(2):
                down_own[tt, i, cx] = low(wide(down_own.at[tt, i, cx]) + wide(down_x.at[tt, i]))

        each(shards, body)
        wait = link(lambda: down_own.at[nt, :, cx], lambda: down_y, p.y)
        yield
        wait(down_y)

        def body_y(i):
            down_own[t, i, cx] = low(wide(down_own.at[t, i, cx]) + wide(down_y.at[i]))

        each(shards, body_y)
        waits = link.around(lambda b: down_own.at[t, b, cx], lambda r: down_z.at[r])
        yield
        down_fin[h, cx] = own_sum(
            lambda: down_own.at[t, s, cx], lambda r: down_z.at[r], waits
        )
        wait = link(lambda: down_fin.at[h, cx], lambda: down_fin.at[h, cx], p.x)
        yield
        wait(down_fin.at[h, nx])
        wait = link(lambda: down_fin.at[h], lambda: down_fin.at[h], p.core)
        yield
        wait(down_fin.at[nh])
        local(lambda: down_fin, lambda: down_out)
        yield

    def reduce_zyx(sent, own, core, z, y, x, fin, result):
        waits = [
            link(lambda tt=tt: sent(tt), lambda tt=tt: core.at[tt], p.core) for tt in range(2)
        ]
        yield
        for tt in range(2):
            waits[tt](core.at[tt])
            add_blocks(own.at[tt], core.at[tt], shards)
        waits = link.around(lambda b: own.at[:, b], lambda r: z.at[r])
        yield
        for wait in waits:
            wait()
        for tt in range(2):
            own[tt, s] = own_sum(lambda: own.at[tt, s], lambda r: z.at[r, tt], [lambda: None] * len(waits))
        wait = link(lambda: own.at[nt, s], lambda: y, p.y)
        yield
        wait(y)
        own[t, s] = low(wide(own.at[t, s]) + wide(y))
        yield from finish_x(own, x, fin, result)

    def reduce_yzx(sent, own, core, y, z, x, fin, result):
        waits = [
            link(lambda tt=tt: sent(tt), lambda tt=tt: core.at[tt], p.core) for tt in range(2)
        ]
        yield
        for tt in range(2):
            waits[tt](core.at[tt])
            add_blocks(own.at[tt], core.at[tt], shards)
        wait = link(lambda: own.at[nt], lambda: y, p.y)
        yield
        wait(y)
        add_blocks(own.at[t], y, shards)
        waits = link.around(lambda b: own.at[t, b], lambda r: z.at[r])
        yield
        own[t, s] = own_sum(lambda: own.at[t, s], lambda r: z.at[r], waits)
        yield from finish_x(own, x, fin, result)

    def finish_x(own, x, fin, result):
        wait = link(lambda: own.at[t, s], lambda: x, p.x)
        yield
        wait(x)
        fin[h] = low(wide(own.at[t, s]) + wide(x))
        wait = link(lambda: fin.at[h], lambda: fin.at[h], p.core)
        yield
        wait(fin.at[nh])
        local(lambda: fin, lambda: result)
        yield

    def reduce_pair(pair, pair_sent):
        sent, whole = lambda: pair_sent.at[pair], lambda: pair_both.at[pair]
        wait = link(lambda: sent().at[nh], lambda: whole().at[h], p.core)
        pair_both[pair, h] = pair_sent[pair, h]
        yield
        wait(whole().at[nh])
        wait = link(lambda: whole().at[:, :, nx], lambda: pair_x.at[pair], p.x)
        yield
        wait(pair_x.at[pair])

        def body(i):
            for tt in range(2):
                pair_both[pair, tt, i, cx] = low(
                    wide(whole().at[tt, i, cx]) + wide(pair_x.at[pair, tt, i])
                )

        each(shards, body)
        wait = link(lambda: whole().at[nt, :, cx], lambda: pair_y.at[pair], p.y)
        yield
        wait(pair_y.at[pair])

        def body_y(i):
            pair_both[pair, t, i, cx] = low(
                wide(whole().at[t, i, cx]) + wide(pair_y.at[pair, i])
            )

        each(shards, body_y)
        waits = link.around(lambda b: whole().at[t, b, cx], lambda r: pair_z.at[pair, r])
        yield
        fin = lambda: pair_fin.at[pair]
        pair_fin[pair, h, cx] = own_sum(
            lambda: whole().at[t, s, cx], lambda r: pair_z.at[pair, r], waits
        )
        wait = link(lambda: fin().at[h, cx], lambda: fin().at[h, cx], p.x)
        yield
        wait(fin().at[h, nx])
        wait = link(lambda: fin().at[h], lambda: fin().at[h], p.core)
        yield
        wait(fin().at[nh])
        for j, result in enumerate((query_out, key_out, value_out)):
            local(
                lambda j=j: fin().at[:, :, :, j * PAIR : (j + 1) * PAIR],
                lambda result=result: result.at[:, :, :, pair * PAIR : (pair + 1) * PAIR],
            )
        yield

    def reduce_vector(first, got, steps, around, finish):
        index = link.made
        wait = link(lambda: first, lambda: got.at[0], p.core)
        yield
        wait(got.at[0])
        steps[0] = first[...] + got[0]
        wait = link(lambda: steps.at[0], lambda: got.at[1], p.x)
        yield
        wait(got.at[1])
        steps[1] = steps[0] + got[1]
        wait = link(lambda: steps.at[1], lambda: got.at[2], p.y)
        yield
        wait(got.at[2])
        around[s] = steps[1] + got[2]
        waits = []
        for there, source in p.steps:
            waits.append(
                (link(lambda: around.at[s], lambda: around.at[s], (there, p.c, t)), source)
            )
        yield
        for wait, source in waits:
            wait(around.at[source])
        total = around[0]
        for at in range(1, shards):
            total = total + around[at]
        link.open.pop(index)().wait_send()
        finish(total)
        yield

    rows_of_units = 2 * units // width

    def early_done(total):
        got = early_first
        got[...] = total
        for part in range(rows_of_units // 2):
            row = got[pl.ds(t * (rows_of_units // 2) + part, 1), :]
            up_bias_out[part * width : (part + 1) * width] = row[0]
        at = rows_of_units
        for result in (out_bias_out, gain_out, shift_out):
            result[...] = got[at : at + 2, :]
            at += 2

    def head_done(total):
        got = head_first
        got[...] = total
        for j in range(2):
            for pair in range(pairs):
                head_bias_out[j : j + 1, pair * PAIR : (pair + 1) * PAIR] = got[
                    pl.ds(t * 2 * pairs + j * pairs + pair, 1), :
                ]

    act = deliver(final_rows, act_out)
    inputs = deliver(input_rows, input_out)
    down = reduce_down()
    up_a = reduce_yzx(
        lambda tt: grad_sent.at[tt, :, 0], up_a_own, up_a_core, up_a_y, up_a_z, up_a_x, up_a_fin,
        up_a_out,
    )
    up_c = reduce_zyx(
        lambda tt: grad_sent.at[tt, :, 1], up_c_own, up_c_core, up_c_z, up_c_y, up_c_x, up_c_fin,
        up_c_out,
    )
    out = reduce_yzx(
        lambda tt: out_sent.at[tt], out_own, out_core, out_y, out_z, out_x, out_fin, out_out
    )
    early = reduce_vector(early_first, early_got, early_steps, early_z, early_done)
    vector = reduce_vector(head_first, head_got, head_steps, head_z, head_done)
    chain_of = [None] * pairs
    grad_waits = []

    def step(*names):
        for chain in names:
            next(chain)

    def store_parts(terms, own, sent):
        parts = terms.shape[0] // 2
        for hh in range(2):
            value = terms[hh * parts : (hh + 1) * parts]
            pl.when(h == hh)(lambda value=value: own(value))
            pl.when(h != hh)(lambda value=value: sent(value))

    x_rows, cot = part_sent, input_rows

    def rows_phase(
        w_out, w_up, w_down, mixed, active, slope, first_low, scaled, rstd, acc, turned
    ):
        loads = [
            local(lambda: mixed_ref, lambda: mixed),
            local(lambda: w_out_ref, lambda: w_out),
            local(lambda: x_ref.at[h], lambda: x_rows.at[0]),
            local(lambda: x_ref.at[2 + h], lambda: x_rows.at[1]),
            local(lambda: w_up_ref, lambda: w_up),
            local(lambda: w_down_ref, lambda: w_down),
            local(lambda: cot_ref, lambda: cot),
        ]
        for load in loads[:4]:
            load()
        blocks = [(late, slice(late * block, (late + 1) * block)) for late in range(2)]
        for late, rows in blocks:
            attn_out = over_cols(mixed[late], w_out[...]) + out_bias_ref[0:1, :]
            values, root = normalize(wide(x_rows.at[late]) + attn_out)
            scaled[late] = values
            rstd[late] = root
            first_low[rows, :] = low(values * gain_ref[0:1, :] + shift_ref[0:1, :])
        loads[4]()
        loads[5]()
        acc[...] = jnp.zeros(acc.shape, jnp.float32)
        inv_root, inv_tau = math.sqrt(0.5), 1.0 / math.sqrt(2.0 * math.pi)

        def ffn(j):
            cols = pl.ds(pl.multiple_of(j * width, width), width)
            hidden = matmul(first_low[...], w_up[:, cols]) + up_bias_ref[:, cols]
            gauss = 0.5 * (1.0 + lax.erf(hidden * inv_root))
            value = low(hidden * gauss)
            active[:, cols] = value
            slope[:, cols] = low(gauss + hidden * jnp.exp(-0.5 * hidden * hidden) * inv_tau)
            acc[...] += over_cols(value, w_down[:, cols])

        each(rows_of_units, ffn)
        loads[6]()
        gain_two = shift_two = bias_two = 0.0
        for late, rows in blocks:
            first_norm = scaled[late] * gain_ref[0:1, :] + shift_ref[0:1, :]
            values, root = normalize(first_norm + acc[rows, :] + out_bias_ref[1:2, :])
            final_rows[late] = low(values * gain_ref[1:2, :] + shift_ref[1:2, :])
            grad_final = wide(cot.at[late])
            gain_two += summed(grad_final * values)
            shift_two += summed(grad_final)
            grad_second = norm_back(grad_final, values, root, gain_ref[1:2, :])
            bias_two += summed(grad_second)
            sum_one[late] = grad_second
            grad = low(grad_second)
            flipped = jnp.transpose(grad)
            for i in range(shards):
                turned[i, :, rows] = flipped[i * 4 * quarter : (i + 1) * 4 * quarter]
        step(act)

        def store_down(tt, i, terms):
            def own(value):
                for xx in range(2):
                    down_own[tt, i, xx] = value[xx * quarter : (xx + 1) * quarter]

            def sent(value):
                for xx in range(2):
                    grad_sent[tt, i, xx] = value[xx * quarter : (xx + 1) * quarter]

            store_parts(terms, own, sent)

        def store_up(tt, i, terms):
            def own(value):
                up_a_own[tt, i] = value[:quarter]
                up_c_own[tt, i] = value[quarter:]

            def sent(value):
                for xx in range(2):
                    grad_sent[tt, i, xx] = value[xx * quarter : (xx + 1) * quarter]

            store_parts(terms, own, sent)

        def store_out(tt, i, terms):
            def own(value):
                out_own[tt, i] = value

            def sent(value):
                out_sent[tt, i] = value

            store_parts(terms, own, sent)

        def products(right, cols, store):
            for tt in range(2):
                one = slice(tt * cols, (tt + 1) * cols)
                each(
                    shards, lambda i: store(tt, i, low(matmul(turned[i], right(one))))
                )

        before = link.made
        products(lambda one: active[:, one], units, store_down)
        step(down)
        acc[...] = jnp.zeros(acc.shape, jnp.float32)

        def ffn_back(j):
            cols = pl.ds(pl.multiple_of(j * width, width), width)
            grads = low(sum_one[...]).reshape(rows_two, width)
            grad_hidden = matmul(grads, w_down[:, cols]) * wide(slope.at[:, cols])
            early_first[pl.ds(j, 1), :] = summed(grad_hidden)
            value = low(grad_hidden)
            slope[:, cols] = value
            acc[...] += over_cols(value, w_up[:, cols])

        each(rows_of_units, ffn_back)
        step(down)
        for late, rows in blocks:
            flipped = jnp.transpose(first_low[rows, :])
            for i in range(shards):
                turned[i, :, rows] = flipped[i * 4 * quarter : (i + 1) * 4 * quarter]
        for index in (before, before + 1):
            link.open.pop(index)().wait_send()
        products(lambda one: slope[:, one], units, store_up)
        step(up_c, up_a)
        gain_one = shift_one = bias_one = 0.0
        for late, rows in blocks:
            grad_first = sum_one[late] + acc[rows, :]
            gain_one += summed(grad_first * scaled[late])
            shift_one += summed(grad_first)
            grad_sum = norm_back(grad_first, scaled[late], rstd[late], gain_ref[0:1, :])
            bias_one += summed(grad_sum)
            sum_one[late] = grad_sum
            grad = low(grad_sum)
            grad_mixed[late] = low(matmul(grad, w_out[...]))
            flipped = jnp.transpose(grad)
            for i in range(shards):
                turned[i, :, rows] = flipped[i * 4 * quarter : (i + 1) * 4 * quarter]
        for pair in range(pairs):
            for late in range(2):
                there = lambda late=late, hh=h: pl.ds(
                    pl.multiple_of((2 * late + hh) * block, block), block
                )
                column = lambda hh, pair=pair: pl.ds(
                    pl.multiple_of(hh * half + pair * PAIR, PAIR), PAIR
                )
                wait = link(
                    lambda late=late, column=column: grad_mixed.at[late, :, column(nh)],
                    lambda pair=pair, there=there: grad_heads.at[pair, there(), :],
                    p.core,
                )
                grad_waits.append(
                    lambda wait=wait, pair=pair, there=there: wait(
                        grad_heads.at[pair, there(hh=nh), :]
                    )
                )
                grad_heads[pair, there(), :] = grad_mixed[late, :, column(h)]
        rows = rows_of_units
        for value in (bias_one, bias_two, gain_one, gain_two, shift_one, shift_two):
            early_first[rows : rows + 1, :] = value
            rows += 1
        if early_first.shape[0] > rows:
            early_first[rows:, :] = jnp.zeros((early_first.shape[0] - rows, width), jnp.float32)
        step(early)
        step(up_c, up_a)
        products(lambda one: jnp.concatenate([mixed[0, :, one], mixed[1, :, one]], axis=0), half, store_out)
        step(out)

    low_vmem = lambda *dims: pltpu.VMEM(dims, jnp.bfloat16)
    full_vmem = lambda *dims: pltpu.VMEM(dims, jnp.float32)
    pl.run_scoped(
        rows_phase,
        low_vmem(width, width),
        low_vmem(width, 2 * units),
        low_vmem(width, 2 * units),
        low_vmem(2, block, width),
        low_vmem(rows_two, 2 * units),
        low_vmem(rows_two, 2 * units),
        low_vmem(rows_two, width),
        full_vmem(2, block, width),
        full_vmem(2, block, 1),
        full_vmem(rows_two, width),
        low_vmem(shards, 4 * quarter, rows_two),
    )

    def heads_phase(
        qkv, wqkv, x_t, x_all, heads, dqkv, dk_acc, dv_acc, sums, input_acc, pair_sent
    ):
        loads = [
            local(lambda: x_ref, lambda: x_all),
            local(lambda: qkv_ref, lambda: qkv),
            local(lambda: heads_ref, lambda: heads),
            local(lambda: wqkv_ref, lambda: wqkv),
        ]
        loads[0]()
        for i in range(length // block):
            x_t[:, i * block : (i + 1) * block] = jnp.transpose(x_all[i])
        step(out)
        for load in loads[1:]:
            load()
        for wait in grad_waits:
            wait()

        def pair_grads(pair):
            values = jnp.concatenate([dqkv[j * pairs + pair] for j in range(3)], axis=1)
            for i in range(shards):
                terms = low(matmul(x_t[i * 4 * quarter : (i + 1) * 4 * quarter, :], values))
                for hh in range(2):
                    for xx in range(2):
                        first = (2 * hh + xx) * quarter
                        pair_sent[pair, hh, i, xx] = terms[first : first + quarter]

        def pair_inputs(pair):
            weights = jnp.concatenate(
                [
                    wqkv[:, j * half + pair * PAIR : j * half + (pair + 1) * PAIR]
                    for j in range(3)
                ],
                axis=1,
            )

            def body(i):
                rows = pl.ds(pl.multiple_of(i * block, block), block)
                terms = over_cols(
                    jnp.concatenate([dqkv[j * pairs + pair, rows, :] for j in range(3)], axis=1),
                    weights,
                )
                if pair == 0:
                    input_acc[i] = terms
                else:
                    input_acc[i] += terms

            each(length // block, body)

        part_wait, swaps = [], []

        def after(pair):
            pair_inputs(pair)
            if pair == pairs - 1:
                for late in range(2):
                    part_sent[late] = low(input_acc[2 * late + nh])
                part_wait.append(link(lambda: part_sent, lambda: part_got, p.core))
            pair_grads(pair)
            chain_of[pair] = reduce_pair(pair, pair_sent)
            swaps.append(link.made)
            step(chain_of[pair])
            if pair == 0:
                step(up_a, early, act)
            if pair == 1:
                step(chain_of[0], down, early, out)

        def attend(pair):
            attend_back_pair(
                starts_ref,
                near,
                qkv.at[pair],
                qkv.at[pairs + pair],
                qkv.at[2 * pairs + pair],
                heads.at[pair],
                grad_heads.at[pair],
                total_ref.at[pair],
                dqkv.at[pair],
                dqkv.at[pairs + pair],
                dqkv.at[2 * pairs + pair],
                sums.at[pair],
                dk_acc,
                dv_acc,
            )
            for at in range(pairs):
                pl.when(pair == at)(lambda at=at: after(at))

        each(pairs, attend)
        head_first[...] = jnp.zeros(head_first.shape, jnp.float32)
        for row in range(2 * pairs):
            kind = row // pairs
            head_first[pl.ds(h * 2 * pairs + row, 1), :] = sums[row % pairs, kind : kind + 1, :]
        part_wait[0](part_got)
        for late in range(2):
            input_rows[late] = low(
                sum_one[late] + input_acc[2 * late + h] + wide(part_got.at[late])
            )
        for index in swaps:
            link.open.pop(index)().wait_send()

    pl.run_scoped(
        heads_phase,
        low_vmem(3 * pairs, length, PAIR),
        low_vmem(width, 3 * half),
        low_vmem(width, length),
        low_vmem(length // block, block, width),
        low_vmem(pairs, length, PAIR),
        low_vmem(3 * pairs, length, PAIR),
        full_vmem(length, PAIR),
        full_vmem(length, PAIR),
        full_vmem(pairs, 2, PAIR),
        full_vmem(length // block, block, width),
        low_vmem(pairs, 2, shards, 2, quarter, 3 * PAIR),
    )

    first, second, third = chain_of
    step(inputs, vector, third, second, down)
    step(first, vector, early, up_c, up_a, out)
    step(third, second, inputs, vector)
    step(first, down, up_c, up_a, out)
    step(third, second, vector)
    step(first, down, up_c, out, up_a)
    step(third, second, first, down)
    step(third, second, first, up_c)
    step(third, second)
    step(vector, early, act, inputs)
    for chain in chain_of + [down, up_a, up_c, out, early, vector, act, inputs]:
        for _ in chain:
            pass
    link.sent()
    local.finish()


def backward(
    shards,
    starts,
    totals,
    up_bias,
    out_biases,
    norm_gains,
    norm_shifts,
    mixed,
    x,
    cot,
    w_out,
    w_up,
    w_down,
    qkv,
    wqkv,
    heads,
):
    seq_dev, block, width = x.shape
    length = seq_dev * block
    pairs = heads.shape[0]
    half = pairs * PAIR
    quarter = width // shards // 4
    w_out = w_out.reshape(width, -1)
    w_up = w_up.reshape(width, -1)
    w_down = w_down.reshape(width, -1)
    units = w_up.shape[1] // 2
    low_type, full_type = jnp.bfloat16, jnp.float32
    shape = jax.ShapeDtypeStruct
    vmem = pl.BlockSpec(memory_space=pltpu.VMEM)
    anywhere = pl.BlockSpec(memory_space=pl.ANY)
    scratch = lambda *dims: pltpu.VMEM(dims, low_type)
    full = lambda *dims: pltpu.VMEM(dims, full_type)
    around = shards - 1
    early_rows = -(-(2 * units // width + 6) // 8) * 8
    copies = 64 + 10 * around
    head_grad = shape((2, 2, quarter, half), low_type)
    return pl.pallas_call(
        lambda *refs: backward_kernel(shards, *refs),
        in_specs=[pl.BlockSpec(memory_space=pltpu.SMEM)] + [vmem] * 5 + [anywhere] * 9,
        out_specs=[anywhere] * 9 + [vmem] * 5,
        out_shape=[
            shape((seq_dev, block, width), low_type),
            shape((seq_dev, block, width), low_type),
            shape((2, 2, quarter, units), low_type),
            shape((2, quarter, units), low_type),
            shape((2, quarter, units), low_type),
            shape((2, 2 * quarter, half), low_type),
            head_grad,
            head_grad,
            head_grad,
            shape((units,), full_type),
            shape((2, width), full_type),
            shape((2, width), full_type),
            shape((2, width), full_type),
            shape((2, half), full_type),
        ],
        scratch_shapes=[
            scratch(pairs, length, PAIR),
            scratch(2, block, width),
            full(2, block, width),
            scratch(2, block, width),
            scratch(2, block, width),
            scratch(2, block, width),
            scratch(2, block, width),
            scratch(2, shards, 2, quarter, units),
            scratch(2, shards, 2, quarter, units),
            scratch(2, shards, 2, quarter, units),
            scratch(2, shards, quarter, units),
            scratch(shards, quarter, units),
            scratch(around, quarter, units),
            scratch(2, 2, quarter, units),
            scratch(2, shards, quarter, units),
            scratch(2, shards, quarter, units),
            scratch(shards, quarter, units),
            scratch(around, quarter, units),
            scratch(quarter, units),
            scratch(2, quarter, units),
            scratch(2, shards, quarter, units),
            scratch(2, shards, quarter, units),
            scratch(around, 2, quarter, units),
            scratch(quarter, units),
            scratch(quarter, units),
            scratch(2, quarter, units),
            scratch(2, shards, 2 * quarter, half),
            scratch(2, shards, 2 * quarter, half),
            scratch(2, shards, 2 * quarter, half),
            scratch(shards, 2 * quarter, half),
            scratch(around, 2 * quarter, half),
            scratch(2 * quarter, half),
            scratch(2, 2 * quarter, half),
            scratch(pairs, 2, shards, 2, quarter, 3 * PAIR),
            scratch(pairs, 2, shards, quarter, 3 * PAIR),
            scratch(pairs, shards, quarter, 3 * PAIR),
            scratch(pairs, around, quarter, 3 * PAIR),
            scratch(pairs, 2, 2, quarter, 3 * PAIR),
            full(early_rows, width),
            full(2, early_rows, width),
            full(3, early_rows, width),
            full(shards, early_rows, width),
            full(4 * pairs, PAIR),
            full(2, 4 * pairs, PAIR),
            full(3, 4 * pairs, PAIR),
            full(shards, 4 * pairs, PAIR),
            pltpu.SemaphoreType.DMA((copies,)),
            pltpu.SemaphoreType.DMA((copies,)),
            pltpu.SemaphoreType.DMA((20 + 3 * pairs,)),
        ],
        compiler_params=pltpu.CompilerParams(
            collective_id=2, has_side_effects=True, vmem_limit_bytes=67_043_328
        ),
    )(
        starts,
        totals,
        up_bias.reshape(1, -1),
        out_biases,
        norm_gains,
        norm_shifts,
        mixed,
        x,
        cot,
        w_out,
        w_up,
        w_down,
        qkv,
        wqkv.reshape(width, 3 * half),
        heads,
    )


def make_local(shards, ctxs, tps):
    def local(
        tokens,
        starts,
        w_query,
        w_key,
        w_value,
        w_out,
        w_up,
        w_down,
        head_bias,
        up_bias,
        out_biases,
        norm_gains,
        norm_shifts,
        cotangent,
    ):
        seq_dev, block, width = tokens.shape
        assert ctxs == 4 and tps == 2 and seq_dev == 4 and block == BLOCK
        rows_own = w_query.shape[0]
        (
            x_blocks,
            cot_rows,
            wqkv,
            qkv,
            mixed_heads,
            mixed_rows,
            totals,
            out_full,
            up_full,
            down_full,
            up_bias_full,
        ) = forward(
            shards,
            starts,
            (w_query, w_key, w_value, w_out, w_up, w_down),
            head_bias,
            up_bias,
            tokens,
            cotangent,
        )
        (
            activations,
            input_grad,
            grad_down,
            grad_up_a,
            grad_up_c,
            grad_out,
            grad_query,
            grad_key,
            grad_value,
            grad_up_bias,
            grad_out_biases,
            grad_gains,
            grad_shifts,
            grad_head_bias,
        ) = backward(
            shards,
            starts,
            totals,
            up_bias_full,
            out_biases,
            norm_gains,
            norm_shifts,
            mixed_rows,
            x_blocks,
            cot_rows,
            out_full,
            up_full,
            down_full,
            qkv,
            wqkv,
            mixed_heads,
        )
        whole = lambda grad: grad.reshape(rows_own, -1).astype(jnp.float32)
        return (
            activations,
            input_grad.astype(jnp.float32),
            whole(grad_query),
            whole(grad_key),
            whole(grad_value),
            whole(grad_out),
            whole(jnp.stack([grad_up_a, grad_up_c], axis=1)),
            whole(grad_down),
            grad_head_bias,
            grad_up_bias,
            grad_out_biases,
            grad_gains,
            grad_shifts,
        )

    return local


def solution(mesh):
    sizes = [mesh.shape[name] for name in AXES]
    return jax.shard_map(
        make_local(*sizes),
        mesh=mesh,
        in_specs=(
            P("shard", "ctx", None),
            P("shard", None),
            P("shard", "tp"),
            P("shard", "tp"),
            P("shard", "tp"),
            P("shard", "tp"),
            P("shard", "tp"),
            P("shard", "tp"),
            P(None, "tp"),
            P("tp"),
            P(),
            P(),
            P(),
            P("shard", "ctx", None),
        ),
        out_specs=(
            P("shard", "ctx", None),
            P("shard", "ctx", None),
            P("shard", "tp"),
            P("shard", "tp"),
            P("shard", "tp"),
            P("shard", "tp"),
            P("shard", "tp"),
            P("shard", "tp"),
            P(None, "tp"),
            P("tp"),
            P(),
            P(),
            P(),
        ),
        check_vma=False,
    )
```
